32 devices in a mesh: dp: 8 (over z, x), gate: 4 (over y, core).
Axes of the slice: x: 2, y: 2, z: 4, core: 2. Of those that a mesh axis runs over, the one named last changes fastest.
Arguments:
- inputs: bfloat16 [8, 2048, 2048], P('dp'), may hold values from -6 to 6
- weight: bfloat16 [2048, 6144], P(None, 'gate'), may hold values from -0.125 to 0.125
- ln_gain: float32 [2048], replicated, may hold values from 0.5 to 1.5
- ln_bias: float32 [2048], replicated, may hold values from -3 to 3
- forget_peep: float32 [2048], P('gate'), may hold values from -1 to 1
- reset_peep: float32 [2048], P('gate'), may hold values from -1 to 1
- forget_bias: float32 [2048], P('gate'), may hold values from 0 to 8
- reset_bias: float32 [2048], P('gate'), may hold values from -1 to 1
- resets: int32 [8, 2048], P('dp'), may hold values from 0 to 1, as said below
- padding: int32 [8, 2048], P('dp'), may hold values from 0 to 1, as said below
- grad_out: bfloat16 [8, 2048, 2048], P('dp', None, 'gate'), may hold values from -6 to 6
Outputs:
- hidden_out: bfloat16 [8, 2048, 2048], P('dp', None, 'gate')
- grad_inputs: bfloat16 [8, 2048, 2048], P('dp', None, 'gate')
- grad_weight: float32 [2048, 6144], P(None, 'gate')
- grad_ln_gain: float32 [2048], P('gate')
- grad_ln_bias: float32 [2048], P('gate')
- grad_forget_peep: float32 [2048], P('gate')
- grad_reset_peep: float32 [2048], P('gate')
- grad_forget_bias: float32 [2048], P('gate')
- grad_reset_bias: float32 [2048], P('gate')
The draws below stay inside these ranges and needn't reach their ends.
Inputs may be any that keep to these rules, and one draw needn't show every extreme that they name: `padding`: each row holds ones followed by zeros, with more than 1536 ones; row 0 is all ones. `resets`: position 0 of every row is 1; row 0 has no other ones.
All inputs are finite; a program needn't handle non-finite values.
Results may differ from the reference program's by a relative error of at most 0.0065.
Values may be sent and summed in bfloat16 or wider, within the bound.
No kernel may reach another device: no remote copies, remote signals or barrier semaphores. Data moves between devices by JAX's collectives and lax.ppermute only.
A program may use at most 192 MiB of HBM per device.

```python
import jax
import jax.numpy as jnp
from jax import lax

D = 2048
LEN = 2048
ROWS_DEV = 1
ROWS = 8
CH = 512
PIECE = 384
N_DP = 8
N_GATE = 4


def draw_padding(key, part):
    lengths = LEN - jax.random.randint(key, (ROWS,), 0, LEN // 4)
    lengths = jnp.where(jnp.arange(ROWS) == 0, LEN, lengths)
    return (jnp.arange(LEN)[None, :] < lengths[:, None]).astype(jnp.int32)


def draw_resets(key, part):
    top_level = LEN.bit_length() - 1
    doc_count = LEN // 4
    level_key, offset_key = jax.random.split(key)
    levels = jax.random.randint(level_key, (ROWS, doc_count), 2, top_level + 1)
    base_len = jnp.left_shift(jnp.ones_like(levels), levels)
    extra_len = jax.random.randint(offset_key, (ROWS, doc_count), 0, 1048576) % base_len
    starts = jnp.cumsum(base_len + extra_len, axis=1).astype(jnp.int32)
    row_ids = jnp.broadcast_to(jnp.arange(ROWS, dtype=jnp.int32)[:, None], (ROWS, doc_count))
    reset_marks = jnp.zeros((ROWS, LEN), jnp.int32).at[row_ids, starts].set(1, mode='drop')
    first_only = (jnp.arange(LEN) == 0).astype(jnp.int32)[None, :]
    reset_marks = jnp.maximum(reset_marks, first_only)
    return jnp.where(jnp.arange(ROWS)[:, None] == 0, first_only, reset_marks).astype(jnp.int32)


def block_levels(rng, shape, cuts, low, largest):
    def one(dim, blocks):
        steps = jax.random.uniform(jax.random.fold_in(jax.random.fold_in(rng, 6), dim), (blocks,), jnp.float32, low / len(cuts), largest / len(cuts))
        return jnp.repeat(jnp.exp(steps), shape[dim] // blocks).reshape((-1,) + (1,) * (len(shape) - dim - 1))

    factor_of = one(*cuts[0])
    for cut in cuts[1:]:
        factor_of = factor_of * one(*cut)
    return factor_of


def noise(rng, extent, deviation, limit, shards=(), held_as=jnp.bfloat16):
    gain = block_levels(rng, extent, shards, -0.22, 0.18) if shards else 1.0
    values = jax.random.normal(rng, extent, jnp.float32) * deviation * gain
    return jnp.minimum(jnp.maximum(values, -limit), limit).astype(held_as)


def setup_inputs(seed: int = 0) -> dict:
    keys = jax.random.split(jax.random.key(seed), 12)
    inputs = noise(keys[0], (ROWS, LEN, D), 1.0, 6.0, ((0, 8),))
    weight = noise(keys[1], (D, 3 * D), D ** -0.5, 0.125, ((1, 4),))
    ln_gain = jnp.clip(1.0 + 0.1 * jax.random.normal(keys[2], (D,), jnp.float32), 0.5, 1.5)
    ln_bias = noise(keys[3], (D,), 0.5, 3.0, (), jnp.float32)
    forget_peep = jnp.clip(jax.random.uniform(keys[4], (D,), jnp.float32, -1.0, 1.0) * block_levels(keys[4], (D,), ((0, 4),), -0.4, 0.0), -1.0, 1.0)
    reset_peep = jnp.clip(jax.random.uniform(keys[5], (D,), jnp.float32, -1.0, 1.0) * block_levels(keys[5], (D,), ((0, 4),), -0.4, 0.0), -1.0, 1.0)
    forget_bias = jnp.clip(8.0 * jax.random.uniform(keys[6], (D,), jnp.float32) ** block_levels(keys[6], (D,), ((0, 4),), -0.2, 0.2), 0.0, 8.0)
    reset_bias = jnp.clip(jax.random.uniform(keys[7], (D,), jnp.float32, -1.0, 1.0) * block_levels(keys[7], (D,), ((0, 4),), -0.4, 0.0), -1.0, 1.0)
    resets = draw_resets(jax.random.fold_in(keys[11], 71), 0)
    padding = draw_padding(jax.random.fold_in(keys[11], 71), 0)
    grad_out = noise(keys[10], (ROWS, LEN, D), 1.0, 6.0, ((0, 8), (2, 4)))
    return {"inputs": inputs, "weight": weight, "ln_gain": ln_gain, "ln_bias": ln_bias, "forget_peep": forget_peep, "reset_peep": reset_peep, "forget_bias": forget_bias, "reset_bias": reset_bias, "resets": resets, "padding": padding, "grad_out": grad_out}


epsilon = 1e-05

@jax.custom_vjp
def low(v):
    return lax.optimization_barrier(v.astype(jnp.bfloat16)).astype(jnp.float32)

@jax.custom_vjp
def low_back(v):
    return v

def low_keep(v):
    return (low(v), None)

def low_pass(kept, grad):
    return (grad,)

def back_keep(v):
    return (v, None)

def back_low(kept, grad):
    return (low(grad),)
low.defvjp(low_keep, low_pass)
low_back.defvjp(back_keep, back_low)

def combine(earlier, later):
    early_decay, early_drive = earlier
    late_decay, late_drive = later
    return (early_decay * late_decay, late_decay * early_drive + late_drive)

def forward(inputs, weight, ln_gain, ln_bias, forget_peep, reset_peep, forget_bias, reset_bias, carry_keep, live_mask):
    row_count = inputs.shape[0]
    flat_rows = inputs.reshape(-1, D)
    row_mean = lax.optimization_barrier(jnp.mean(flat_rows, axis=1, keepdims=True))
    centered = flat_rows - row_mean
    inv_std = lax.rsqrt(lax.optimization_barrier(jnp.mean(centered * centered, axis=1, keepdims=True)) + epsilon)
    normed = low(centered * inv_std * ln_gain + ln_bias)
    mixed = low_back(low(jnp.dot(normed, weight, precision=lax.Precision.HIGHEST)))
    mixed = mixed.reshape(-1, N_GATE, N_GATE, PIECE).transpose(0, 2, 1, 3)
    mixed = mixed.reshape(-1, N_GATE, 3, CH).transpose(0, 2, 1, 3).reshape(row_count, LEN, 3, D)
    forget = jax.nn.sigmoid(mixed[:, :, 1] + forget_peep * inputs + forget_bias)
    reset_gate = jax.nn.sigmoid(mixed[:, :, 2] + reset_peep * inputs + reset_bias)
    decays = forget * carry_keep
    drives = (1.0 - forget) * mixed[:, :, 0]
    memory = lax.associative_scan(combine, (decays, drives), axis=1)[1]
    return live_mask * (reset_gate * memory + (1.0 - reset_gate) * inputs)

def reference(inputs, weight, ln_gain, ln_bias, forget_peep, reset_peep, forget_bias, reset_bias, resets, padding, grad_out):
    params = (weight.astype(jnp.float32), ln_gain, ln_bias, forget_peep, reset_peep, forget_bias, reset_bias)
    groups = inputs.reshape(N_DP, ROWS_DEV, LEN, D)
    keeps = (1 - resets).astype(jnp.float32).reshape(N_DP, ROWS_DEV, LEN, 1)
    lives = padding.astype(jnp.float32).reshape(N_DP, ROWS_DEV, LEN, 1)
    cotangents = grad_out.reshape(N_DP, ROWS_DEV, LEN, D)

    def accumulate(running, slices):
        row_group, keep_rows, live_rows, cot_rows = slices

        def layer_call(inputs32, *weights):
            return forward(inputs32, *weights, keep_rows, live_rows)
        outputs, pullback = jax.vjp(layer_call, row_group.astype(jnp.float32), *params)
        gradients = pullback(cot_rows.astype(jnp.float32))
        running = tuple((previous + fresh for previous, fresh in zip(running, gradients[1:])))
        return (running, (outputs.astype(jnp.bfloat16), gradients[0].astype(jnp.bfloat16)))
    zero_grads = tuple((jnp.zeros_like(entry) for entry in params))
    running, (outputs, dinputs) = lax.scan(accumulate, zero_grads, (groups, keeps, lives, cotangents))
    return (outputs.reshape(ROWS, LEN, D), dinputs.reshape(ROWS, LEN, D), running[0], running[1], running[2], running[3], running[4], running[5], running[6])
```

```python
import functools

import jax
import jax.numpy as jnp
from jax import lax
from jax.experimental import pallas as pl
from jax.experimental.pallas import tpu as pltpu
from jax.sharding import PartitionSpec as P

epsilon = 1e-05
F32 = jnp.float32
BF16 = jnp.bfloat16
LANES = 128
VMEM_LIMIT = 60 * 1024 * 1024


def call(kernel, meta, args, grid, in_specs, out_specs, out_shape, scratch=(), aliases=None, cost=None):
    return pl.pallas_call(
        kernel,
        grid_spec=pltpu.PrefetchScalarGridSpec(
            num_scalar_prefetch=1,
            grid=grid,
            in_specs=in_specs,
            out_specs=out_specs,
            scratch_shapes=list(scratch),
        ),
        out_shape=out_shape,
        input_output_aliases=aliases or {},
        compiler_params=pltpu.CompilerParams(
            dimension_semantics=("arbitrary",) * len(grid), vmem_limit_bytes=VMEM_LIMIT
        ),
        cost_estimate=cost,
    )(meta, *args)


def cost(flops, nbytes, trans=0):
    return pl.CostEstimate(flops=int(flops), bytes_accessed=int(nbytes), transcendentals=int(trans))


def struct(shape, dtype):
    return jax.ShapeDtypeStruct(shape, dtype)


def norm_kernel(meta, x_ref, gain_ref, bias_ref, out_ref, mu_ref, inv_ref):
    x = x_ref[...].astype(F32)
    features = x.shape[1]
    mu = jnp.sum(x, axis=1, keepdims=True) * (1.0 / features)
    centered = x - mu
    inv = lax.rsqrt(jnp.sum(centered * centered, axis=1, keepdims=True) * (1.0 / features) + epsilon)
    out_ref[...] = (centered * inv * gain_ref[...] + bias_ref[...]).astype(BF16)
    mu_ref[...] = jnp.broadcast_to(mu, mu_ref.shape)
    inv_ref[...] = jnp.broadcast_to(inv, inv_ref.shape)


def norm(meta, x, gain, bias, tb=256):
    tokens, features = x.shape
    row = pl.BlockSpec((tb, features), lambda t, m: (t, 0))
    whole = pl.BlockSpec((1, features), lambda t, m: (0, 0))
    stat = pl.BlockSpec((tb, LANES), lambda t, m: (t, 0))
    return call(
        norm_kernel,
        meta,
        (x, gain[None], bias[None]),
        (tokens // tb,),
        [row, whole, whole],
        [row, stat, stat],
        [struct(x.shape, BF16), struct((tokens, LANES), F32), struct((tokens, LANES), F32)],
        cost=cost(8 * tokens * features, 4 * tokens * features),
    )


def swap_halves(value, flag):
    half = value.shape[1] // 2
    swapped = jnp.concatenate([value[:, half:], value[:, :half]], axis=1)
    return jnp.where(flag, swapped, value)


def project_kernel(planes, mixed, meta, normed_ref, *refs):
    weights = refs[: len(planes)]
    out_ref = refs[-1]
    which = pl.program_id(1)
    for number, w_ref in enumerate(weights):

        @pl.when(which == number)
        def _(w_ref=w_ref, number=number):
            value = jnp.dot(normed_ref[...], w_ref[...], preferred_element_type=F32).astype(BF16)
            if mixed[number]:
                value = swap_halves(value, meta[M_CORE] == 1)
            out_ref[0] = value


def project(meta, normed, weights, planes, mixed, earlier, tb=512):
    tokens, features = normed.shape
    width = weights[0].shape[1]
    first = planes[0]
    number = len(weights)

    def where_to(t, n, m):
        return (m[first + n], t, 0)

    in_specs = [pl.BlockSpec((tb, features), lambda t, n, m: (t, 0))]
    in_specs += [pl.BlockSpec((features, width), lambda t, n, m: (0, 0))] * number
    args = [normed, *weights]
    aliases = None
    if earlier is not None:
        in_specs.append(pl.BlockSpec(memory_space=pl.ANY))
        args.append(earlier)
        aliases = {len(args): 0}
    return call(
        functools.partial(project_kernel, planes, mixed),
        meta,
        args,
        (tokens // tb, number),
        in_specs,
        pl.BlockSpec((1, tb, width), where_to),
        struct((3, tokens, width), BF16),
        aliases=aliases,
        cost=cost(2 * tokens * features * width * number, 2 * tokens * (features + width * number)),
    )


def sigmoid(z):
    return 0.5 * jnp.tanh(0.5 * z) + 0.5


def scan_kernel(
    chains,
    meta,
    u_ref,
    x_ref,
    g_ref,
    keep_ref,
    live_ref,
    prm_ref,
    *refs,
):
    hid_ref, ds_ref, direct_ref, vec_ref, A, B, FG, R, PV, D, CE, PE, CI, EI = refs[-14:]
    length = x_ref.shape[0]
    seg = length // (8 * chains)
    tile = 64
    pf, pr, bf, br = (jnp.broadcast_to(prm_ref[i : i + 1, :], (tile, LANES)) for i in range(4))

    def gates(i, carry):
        rows = pl.ds(pl.multiple_of(i * tile, tile), tile)
        x = x_ref[rows, :].astype(F32)
        ut = u_ref[0, rows, :].astype(F32)
        forget = sigmoid(u_ref[1, rows, :].astype(F32) + pf * x + bf)
        reset = sigmoid(u_ref[2, rows, :].astype(F32) + pr * x + br)
        FG[rows, :] = forget
        R[rows, :] = reset
        A[rows, :] = forget * keep_ref[rows, :]
        B[rows, :] = (1.0 - forget) * ut
        D[rows, :] = g_ref[rows, :].astype(F32) * live_ref[rows, :] * reset
        return carry

    lax.fori_loop(0, length // tile, gates, 0)

    def strided(q, i):
        return pl.ds(q * 8 * seg + i, 8, stride=seg)

    zeros = jnp.zeros((8, LANES), F32)
    ones = jnp.ones((8, LANES), F32)

    def summary(i, carry):
        out = []
        for q in range(chains):
            c, p, e = carry[q]
            a = A[strided(q, i), :]
            c = a * c + B[strided(q, i), :]
            p = a * p
            back = seg - 1 - i
            e = A[strided(q, back), :] * (D[strided(q, back), :] + e)
            out.append((c, p, e))
        return tuple(out)

    ends = lax.fori_loop(0, seg, summary, ((zeros, ones, zeros),) * chains, unroll=4)
    for q in range(chains):
        CE[8 * q : 8 * q + 8, :] = ends[q][0]
        PE[8 * q : 8 * q + 8, :] = ends[q][1]
        EI[8 * q : 8 * q + 8, :] = ends[q][2]
    count = 8 * chains
    c = jnp.zeros((1, LANES), F32)
    for j in range(count):
        CI[j : j + 1, :] = c
        c = CE[j : j + 1, :] + PE[j : j + 1, :] * c
    e = jnp.zeros((1, LANES), F32)
    for j in reversed(range(count)):
        own = EI[j : j + 1, :]
        EI[j : j + 1, :] = e
        e = own + PE[j : j + 1, :] * e

    def final(i, carry):
        out = []
        for q in range(chains):
            c, e = carry[q]
            PV[strided(q, i), :] = c
            c = A[strided(q, i), :] * c + B[strided(q, i), :]
            back = seg - 1 - i
            dc = D[strided(q, back), :] + e
            D[strided(q, back), :] = dc
            e = A[strided(q, back), :] * dc
            out.append((c, e))
        return tuple(out)

    starts = tuple((CI[8 * q : 8 * q + 8, :], EI[8 * q : 8 * q + 8, :]) for q in range(chains))
    lax.fori_loop(0, seg, final, starts, unroll=4)

    def fold(v):
        return v.reshape(tile // 8, 8, LANES).sum(axis=0)

    def grads(i, carry):
        rows = pl.ds(pl.multiple_of(i * tile, tile), tile)
        x = x_ref[rows, :].astype(F32)
        ut = u_ref[0, rows, :].astype(F32)
        live = live_ref[rows, :]
        g = g_ref[rows, :].astype(F32) * live
        forget = FG[rows, :]
        reset = R[rows, :]
        prev = PV[rows, :]
        dc = D[rows, :]
        memory = A[rows, :] * prev + B[rows, :]
        gap = memory - x
        hid_ref[rows, :] = (live * (x + reset * gap)).astype(BF16)
        rest = 1.0 - reset
        dreset = g * gap * (reset * rest)
        lose = 1.0 - forget
        dtilde = dc * lose
        dforget = dtilde * forget * (prev * keep_ref[rows, :] - ut)
        ds_ref[0, rows, :] = dtilde.astype(BF16)
        ds_ref[1, rows, :] = dforget.astype(BF16)
        ds_ref[2, rows, :] = dreset.astype(BF16)
        direct_ref[rows, :] = (g * rest + dforget * pf + dreset * pr).astype(BF16)
        s0, s1, s2, s3 = carry
        return (
            s0 + fold(dforget * x),
            s1 + fold(dreset * x),
            s2 + fold(dforget),
            s3 + fold(dreset),
        )

    sums = lax.fori_loop(0, length // tile, grads, (zeros,) * 4)
    for n, s in enumerate(sums):
        vec_ref[n : n + 1, :] = jnp.sum(s, axis=0, keepdims=True)
    vec_ref[4:8, :] = jnp.zeros((4, LANES), F32)


def scan(meta, half, u, x, grad, keep, live, params, earlier):
    length = x.shape[0]
    width = u.shape[2]
    blocks = width // LANES
    channels = grad.shape[1]
    col = lambda k, m: (0, m[half] * blocks + k)
    xcol = lambda k, m: (0, m[M_GATE] * (channels // LANES) + m[half] * blocks + k)
    tall = (length, LANES)
    plane = pl.BlockSpec((3, length, LANES), lambda k, m: (0, 0, k))
    in_specs = [
        plane,
        pl.BlockSpec(tall, xcol),
        pl.BlockSpec(tall, col),
        pl.BlockSpec(tall, lambda k, m: (0, 0)),
        pl.BlockSpec(tall, lambda k, m: (0, 0)),
        pl.BlockSpec((8, LANES), col),
    ]
    args = [u, x, grad, keep, live, params]
    aliases = None
    if earlier is not None:
        aliases = {len(args) + 1: 0, len(args) + 2: 2, len(args) + 3: 3}
        args += list(earlier)
        in_specs += [pl.BlockSpec(memory_space=pl.ANY)] * 3
    chains = 4
    small = pltpu.VMEM((8 * chains, LANES), F32)
    return call(
        functools.partial(scan_kernel, chains),
        meta,
        args,
        (blocks,),
        in_specs,
        [
            pl.BlockSpec(tall, col),
            plane,
            pl.BlockSpec(tall, col),
            pl.BlockSpec((8, LANES), col),
        ],
        [
            struct((length, channels), BF16),
            struct(u.shape, BF16),
            struct((length, channels), BF16),
            struct((8, channels), F32),
        ],
        scratch=[pltpu.VMEM(tall, F32)] * 6 + [small] * 4,
        aliases=aliases,
        cost=cost(60 * length * width, 2 * 9 * length * width, 2 * length * width),
    )


def wgrad_kernel(meta, normed_ref, ds_ref, a_ref, b_ref):
    step = pl.program_id(0)
    half = pl.num_programs(0) // 2
    left = normed_ref[...]
    for s in range(3):
        value = lax.dot_general(
            left, ds_ref[s], (((0,), (0,)), ((), ())), preferred_element_type=F32
        ).astype(BF16)

        @pl.when(step < half)
        def _(value=value, s=s):
            a_ref[s] = value

        @pl.when(step >= half)
        def _(value=value, s=s):
            b_ref[s] = value


def wgrad(meta, normed, ds, first, mb=256):
    tokens, features = normed.shape
    width = ds.shape[2]
    rows = features // 4
    steps = rows // mb

    def lhs(i, m):
        stream = i // steps
        return (0, (stream * 2 + m[first + stream]) * steps + i % steps)

    return call(
        wgrad_kernel,
        meta,
        (normed, ds),
        (2 * steps,),
        [
            pl.BlockSpec((tokens, mb), lhs),
            pl.BlockSpec((3, tokens, width), lambda i, m: (0, 0, 0)),
        ],
        [
            pl.BlockSpec((3, mb, width), lambda i, m: (0, jnp.minimum(i, steps - 1), 0)),
            pl.BlockSpec((3, mb, width), lambda i, m: (0, jnp.maximum(i - steps, 0), 0)),
        ],
        [struct((3, rows, width), BF16)] * 2,
        cost=cost(12 * tokens * rows * width, 2 * tokens * (features // 2 + 3 * width)),
    )


def back_kernel(meta, ds1_ref, ds2_ref, p1, q1, m1, p2, q2, m2, out_ref):
    total = None
    for ds_ref, table, (p, q, m) in ((ds1_ref, M_S1, (p1, q1, m1)), (ds2_ref, M_S2, (p2, q2, m2))):
        for n, w_ref in enumerate((p, q, m)):
            left = ds_ref[meta[table + n]]
            if n == 2:
                left = swap_halves(left, meta[M_CORE] == 1)
            term = lax.dot_general(
                left, w_ref[...], (((1,), (1,)), ((), ())), preferred_element_type=F32
            )
            total = term if total is None else total + term
    out_ref[0] = total.astype(BF16)


def back(meta, ds1, ds2, w1, w2, first, tb=512):
    tokens, width = ds1.shape[1:]
    features = w1[0].shape[0]
    block = features // 4
    dspec = pl.BlockSpec((3, tb, width), lambda n, t, m: (0, t, 0))
    wspec = pl.BlockSpec((block, width), lambda n, t, m: (m[first + n], 0))
    return call(
        back_kernel,
        meta,
        (ds1, ds2, *w1, *w2),
        (2, tokens // tb),
        [dspec, dspec] + [wspec] * 6,
        pl.BlockSpec((1, tb, block), lambda n, t, m: (n, t, 0)),
        struct((2, tokens, block), BF16),
        cost=cost(24 * tokens * block * width, 12 * tokens * width * 2),
    )


def unit_of(x_ref, mu_ref, inv_ref):
    repeat = x_ref.shape[1] // LANES
    mu = jnp.concatenate([mu_ref[...]] * repeat, axis=1)
    inv = jnp.concatenate([inv_ref[...]] * repeat, axis=1)
    return (x_ref[...].astype(F32) - mu) * inv, inv


def tail_sums_kernel(meta, k_ref, rc_ref, ry_ref, x_ref, mu_ref, inv_ref, gain_ref, dn_ref, row_ref, col_ref):
    unit, _ = unit_of(x_ref, mu_ref, inv_ref)
    dn = k_ref[0].astype(F32) + rc_ref[0].astype(F32) + ry_ref[...].astype(F32)
    dn_ref[...] = dn
    gu = dn * gain_ref[...]
    ones = jnp.ones((8, gu.shape[1]), F32)
    dims = (((1,), (1,)), ((), ()))
    first = lax.dot_general(ones, gu, dims, precision=lax.Precision.HIGHEST, preferred_element_type=F32)
    second = lax.dot_general(ones, gu * unit, dims, precision=lax.Precision.HIGHEST, preferred_element_type=F32)
    pick = lax.broadcasted_iota(jnp.int32, first.shape, 0) == 0
    row_ref[...] = jnp.where(pick, first, second)

    @pl.when(pl.program_id(0) == 0)
    def _():
        col_ref[...] = jnp.zeros_like(col_ref)

    col_ref[0:1, :] += jnp.sum(dn * unit, axis=0, keepdims=True)
    col_ref[1:2, :] += jnp.sum(dn, axis=0, keepdims=True)


def tail_sums(meta, keep, got, far, x, mu, inv, gain, tb=512):
    tokens, channels = far.shape
    return call(
        tail_sums_kernel,
        meta,
        (keep, got, far, x, mu, inv, gain[None]),
        (tokens // tb,),
        [
            pl.BlockSpec((1, tb, channels), lambda t, m: (1, t, 0)),
            pl.BlockSpec((1, tb, channels), lambda t, m: (1, t, 0)),
            pl.BlockSpec((tb, channels), lambda t, m: (t, 0)),
            pl.BlockSpec((tb, channels), lambda t, m: (t, m[M_GATE])),
            pl.BlockSpec((tb, LANES), lambda t, m: (t, 0)),
            pl.BlockSpec((tb, LANES), lambda t, m: (t, 0)),
            pl.BlockSpec((1, channels), lambda t, m: (0, m[M_GATE])),
        ],
        [
            pl.BlockSpec((tb, channels), lambda t, m: (t, 0)),
            pl.BlockSpec((8, tb), lambda t, m: (0, t)),
            pl.BlockSpec((8, channels), lambda t, m: (0, 0)),
        ],
        [struct((tokens, channels), F32), struct((8, tokens), F32), struct((8, channels), F32)],
        cost=cost(20 * tokens * channels, 12 * tokens * channels),
    )


def tail_kernel(features, meta, dn_ref, row_ref, x_ref, mu_ref, inv_ref, gain_ref, direct_ref, out_ref):
    unit, inv = unit_of(x_ref, mu_ref, inv_ref)
    rows = row_ref[...] * (1.0 / features)
    shape = (8, 2 * LANES)
    at = lax.broadcasted_iota(jnp.int32, shape, 0)
    lane = lax.broadcasted_iota(jnp.int32, shape, 1)
    pick = jnp.where(at == jnp.where(lane < LANES, 0, 1), 1.0, 0.0).astype(F32)
    means = lax.dot_general(
        rows, pick, (((0,), (0,)), ((), ())), precision=lax.Precision.HIGHEST, preferred_element_type=F32
    )
    repeat = x_ref.shape[1] // LANES
    m1 = jnp.concatenate([means[:, :LANES]] * repeat, axis=1)
    m2 = jnp.concatenate([means[:, LANES:]] * repeat, axis=1)
    gu = dn_ref[...] * gain_ref[...]
    out_ref[...] = (inv * (gu - m1 - unit * m2) + direct_ref[...].astype(F32)).astype(BF16)


def tail(meta, dn, rows, x, mu, inv, gain, direct, features, tb=512):
    tokens, channels = dn.shape
    return call(
        functools.partial(tail_kernel, features),
        meta,
        (dn, rows, x, mu, inv, gain[None], direct),
        (tokens // tb,),
        [
            pl.BlockSpec((tb, channels), lambda t, m: (t, 0)),
            pl.BlockSpec((8, tb), lambda t, m: (0, t)),
            pl.BlockSpec((tb, channels), lambda t, m: (t, m[M_GATE])),
            pl.BlockSpec((tb, LANES), lambda t, m: (t, 0)),
            pl.BlockSpec((tb, LANES), lambda t, m: (t, 0)),
            pl.BlockSpec((1, channels), lambda t, m: (0, m[M_GATE])),
            pl.BlockSpec((tb, channels), lambda t, m: (t, 0)),
        ],
        pl.BlockSpec((tb, channels), lambda t, m: (t, 0)),
        struct((tokens, channels), BF16),
        cost=cost(10 * tokens * channels, 12 * tokens * channels),
    )


def place_kernel(n_dp, meta, *refs):
    out_ref = refs[-1]
    step = pl.program_id(0)
    for stream in range(2):
        for part in range(2):
            low = stream * n_dp + part * (n_dp // 2)

            @pl.when((step >= low) & (step < low + n_dp // 2))
            def _(stream=stream, part=part):
                one = refs[stream * 2 + part]
                two = refs[4 + stream * 2 + part]
                piece = out_ref.shape[1] // 4
                unit = piece // 3
                core = meta[M_CORE]

                def put(owner, single, src, col):
                    base = meta[M_OWN + owner] * piece
                    wide = unit if single else 2 * unit
                    at = base + (jnp.where(core == 0, 2 * unit, 0) if single else core * unit)
                    at = pl.multiple_of(at, LANES)
                    out_ref[:, pl.ds(at, wide)] = src[:, col : col + wide].astype(F32)

                put(0, False, one, 0)
                put(1, False, one, 2 * unit)
                put(2, True, one, 4 * unit)
                put(3, True, one, 5 * unit)
                put(0, True, two, 0)
                put(1, True, two, unit)
                put(2, False, two, 2 * unit)
                put(3, False, two, 4 * unit)


def place(meta, parts1, parts2, n_dp, features, columns):
    rows = features // 2 // n_dp
    half = n_dp // 2
    specs = []
    for _ in range(2):
        for stream in range(2):
            for part in range(2):
                low = stream * n_dp + part * half
                specs.append(
                    pl.BlockSpec(
                        (rows, columns // 2),
                        lambda i, m, low=low: (jnp.clip(i - low, 0, half - 1), 0),
                    )
                )

    def where_to(i, m):
        stream = i // n_dp
        return (stream * n_dp + (i % n_dp ^ m[M_RHO + stream]), 0)

    return call(
        functools.partial(place_kernel, n_dp),
        meta,
        (*parts1, *parts2),
        (2 * n_dp,),
        specs,
        pl.BlockSpec((rows, columns), where_to),
        struct((features, columns), F32),
        cost=cost(features * columns, 6 * features * columns),
    )


M_GATE, M_CORE, M_H1, M_H2 = 0, 1, 2, 3
M_S1, M_S2 = 4, 7
M_SEND, M_KEEP = 10, 12
M_OUT, M_IN = 14, 16
M_OWN, M_RHO = 18, 22


def shards(
    n_dp,
    n_gate,
    inputs,
    weight,
    ln_gain,
    ln_bias,
    forget_peep,
    reset_peep,
    forget_bias,
    reset_bias,
    resets,
    padding,
    grad_out,
):
    rows, tokens, features = inputs.shape
    assert rows == 1 and n_gate == 4
    channels = forget_peep.shape[0]
    unit = channels // 4
    piece = 3 * unit
    bits = n_dp.bit_length() - 1
    assert 1 << bits == n_dp
    gate = lax.axis_index("gate")
    dp = lax.axis_index("dp")
    hi, core = gate // 2, gate % 2
    other = 1 - core

    orders = [list(range(bits)), [1, 0, *range(2, bits)]]

    def bit(b):
        return (dp >> b) & 1

    def rho(order):
        value = 0
        for b in order:
            value = value * 2 + bit(b)
        return value

    def streams(h):
        return [core + h, other + h, 2 * (1 - h)]

    h1, h2 = hi, 1 - hi
    s1, s2 = streams(h1), streams(h2)
    far = (1 - hi) * 2
    meta = jnp.stack(
        [gate, core, h1, h2, *s1, *s2]
        + [1 - bit(order[0]) for order in orders]
        + [bit(order[0]) for order in orders]
        + [far + other, hi * 2 + other, far + core, hi * 2 + core]
        + [gate, hi * 2 + other, far + core, far + other]
        + [rho(order) for order in orders]
    ).astype(jnp.int32)

    def over_gate(value, delta):
        return lax.ppermute(value, "gate", [(g, g ^ delta) for g in range(n_gate)])

    def over_dp(value, b):
        return lax.ppermute(value, "dp", [(d, d ^ (1 << b)) for d in range(n_dp)])

    def columns(start, width):
        return lax.dynamic_slice_in_dim(weight, start, width, 1)

    single = jnp.where(core == 0, 2 * unit, 0)
    pair = core * unit

    sent2 = over_gate(columns((far + core) * piece + single, unit), 2)
    sent3 = over_gate(columns((far + other) * piece + single, unit), 3)
    near = (hi * 2 + other) * piece
    got_pair = over_gate(columns(near + pair, 2 * unit), 1)
    got_single = over_gate(columns(near + single, unit), 1)
    late2 = over_gate(columns((far + core) * piece + pair, 2 * unit), 2)
    late3 = over_gate(columns((far + other) * piece + pair, 2 * unit), 3)
    own_pair = columns(gate * piece + pair, 2 * unit)
    own_single = columns(gate * piece + single, unit)
    w1 = [own_pair, got_pair, jnp.concatenate([sent2, sent3], axis=1)]
    w2 = [late2, late3, jnp.concatenate([own_single, got_single], axis=1)]

    x = inputs.reshape(tokens, features)
    grad = grad_out.reshape(tokens, channels)
    normed, mu, inv = norm(meta, x, ln_gain, ln_bias)

    keep = jnp.broadcast_to((1 - resets).astype(F32).reshape(tokens, 1), (tokens, LANES))
    live = jnp.broadcast_to(padding.astype(F32).reshape(tokens, 1), (tokens, LANES))
    params = jnp.concatenate(
        [jnp.stack([forget_peep, reset_peep, forget_bias, reset_bias]), jnp.zeros((4, channels), F32)]
    )

    u1 = project(meta, normed, w1[:2], [M_S1, M_S1 + 1], [False, False], None)
    u1 = project(meta, normed, w1[2:], [M_S1 + 2], [True], u1)
    hidden, ds1, direct, vecs = scan(meta, M_H1, u1, x, grad, keep, live, params, None)
    send1 = wgrad(meta, normed, ds1, M_SEND)
    keep1 = wgrad(meta, normed, ds1, M_KEEP)
    u2 = project(meta, normed, w2[2:], [M_S2 + 2], [True], None)
    u2 = project(meta, normed, w2[:2], [M_S2, M_S2 + 1], [False, False], u2)
    hidden, ds2, direct, vecs = scan(
        meta, M_H2, u2, x, grad, keep, live, params, (hidden, direct, vecs)
    )
    send2 = wgrad(meta, normed, ds2, M_SEND)
    keep2 = wgrad(meta, normed, ds2, M_KEEP)

    def add(a, b):
        return (a.astype(F32) + b.astype(F32)).astype(BF16)

    def rows_of(v, start, count):
        return lax.dynamic_slice_in_dim(v, start, count, 1)

    def reduce_scatter(send, kept, order):
        got = over_dp(send, order[0])
        for b in order[1:]:
            half = kept.shape[1] // 2
            away, stay = (1 - bit(b)) * half, bit(b) * half
            send = add(rows_of(kept, away, half), rows_of(got, away, half))
            nxt = over_dp(send, b)
            kept = add(rows_of(kept, stay, half), rows_of(got, stay, half))
            got = nxt
        return add(kept, got)

    def lanes(v, start, width):
        return lax.dynamic_slice_in_dim(v, start, width, 1)

    def plane(v, s):
        return lax.dynamic_index_in_dim(v, s, 0, keepdims=False)

    def to_storage(shard, s, late):
        p, q, m = (plane(shard, n) for n in s)
        mine, theirs = lanes(m, core * unit, unit), lanes(m, other * unit, unit)
        if late:
            kept, out = mine, [theirs, p, q]
        else:
            kept, out = p, [q, mine, theirs]
        return jnp.concatenate([kept] + [over_gate(v, n + 1) for n, v in enumerate(out)], axis=1)

    def all_gather(shard, order):
        for b in reversed(order[1:]):
            shard = jnp.concatenate([shard, over_dp(shard, b)], axis=0)
        return [shard, over_dp(shard, order[0])]

    def reduce_all(sends, keeps, s, late):
        parts = [reduce_scatter(a, k, order) for a, k, order in zip(sends, keeps, orders)]
        stored = to_storage(jnp.concatenate(parts, axis=1), s, late)
        each = parts[0].shape[1]
        out = []
        for n, order in enumerate(orders):
            out += all_gather(stored[n * each : (n + 1) * each], order)
        return out

    parts1 = reduce_all(send1, keep1, s1, False)

    send = back(meta, ds1, ds2, w1, w2, M_OUT)
    got = over_gate(send, 1)
    kept = back(meta, ds1, ds2, w1, w2, M_IN)
    far_part = over_gate(add(kept[0], got[0]), 2)

    parts2 = reduce_all(send2, keep2, s2, True)

    dn, row_sums, col_sums = tail_sums(meta, kept, got, far_part, x, mu, inv, ln_gain)
    row_sums = row_sums[:2]
    for delta in (1, 2):
        row_sums = row_sums + over_gate(row_sums, delta)
    row_sums = jnp.concatenate([row_sums, jnp.zeros((6, tokens), F32)])
    dinputs = tail(meta, dn, row_sums, x, mu, inv, ln_gain, direct, features)

    totals = jnp.concatenate([col_sums[:2], vecs[:4]], axis=0)
    for b in range(bits):
        totals = totals + over_dp(totals, b)

    grad_weight = place(meta, parts1, parts2, n_dp, features, weight.shape[1])
    return (
        hidden.reshape(rows, tokens, channels),
        dinputs.reshape(rows, tokens, channels),
        grad_weight,
        totals[0],
        totals[1],
        totals[2],
        totals[3],
        totals[4],
        totals[5],
    )


def solution(mesh):
    return jax.shard_map(
        functools.partial(shards, mesh.shape["dp"], mesh.shape["gate"]),
        mesh=mesh,
        in_specs=(
            P("dp", None, None),
            P(None, "gate"),
            P(),
            P(),
            P("gate"),
            P("gate"),
            P("gate"),
            P("gate"),
            P("dp", None),
            P("dp", None),
            P("dp", None, "gate"),
        ),
        out_specs=(
            P("dp", None, "gate"),
            P("dp", None, "gate"),
            P(None, "gate"),
            P("gate"),
            P("gate"),
            P("gate"),
            P("gate"),
            P("gate"),
            P("gate"),
        ),
        check_vma=False,
    )
```

```python
import functools

import jax
import jax.numpy as jnp
from jax import lax
from jax.experimental import pallas as pl
from jax.experimental.pallas import tpu as pltpu
from jax.sharding import PartitionSpec as P

epsilon = 1e-05
F32 = jnp.float32
BF16 = jnp.bfloat16
LANES = 128
VMEM_LIMIT = 60 * 1024 * 1024


def call(kernel, meta, args, grid, in_specs, out_specs, out_shape, scratch=(), aliases=None, cost=None):
    return pl.pallas_call(
        kernel,
        grid_spec=pltpu.PrefetchScalarGridSpec(
            num_scalar_prefetch=1,
            grid=grid,
            in_specs=in_specs,
            out_specs=out_specs,
            scratch_shapes=list(scratch),
        ),
        out_shape=out_shape,
        input_output_aliases=aliases or {},
        compiler_params=pltpu.CompilerParams(
            dimension_semantics=("arbitrary",) * len(grid), vmem_limit_bytes=VMEM_LIMIT
        ),
        cost_estimate=cost,
    )(meta, *args)


def cost(flops, nbytes, trans=0):
    return pl.CostEstimate(flops=int(flops), bytes_accessed=int(nbytes), transcendentals=int(trans))


def struct(shape, dtype):
    return jax.ShapeDtypeStruct(shape, dtype)


TILE = 256


def order_matrix():
    row = lax.broadcasted_iota(jnp.int32, (TILE, TILE), 0)
    token = lax.broadcasted_iota(jnp.int32, (TILE, TILE), 1)
    return jnp.where(token == (row % 8) * (TILE // 8) + row // 8, 1.0, 0.0).astype(BF16)


def to_rows(order, value):
    return jnp.dot(order, value, preferred_element_type=F32)


def to_tokens(order, value):
    return lax.dot_general(order, value, (((0,), (0,)), ((), ())), preferred_element_type=F32)


def norm_kernel(
    meta, x_ref, gain_ref, bias_ref, res_ref, pad_ref, out_ref, mu_ref, inv_ref, own_ref, keep_ref, live_ref, PM, XP, S1, S2
):
    @pl.when(pl.program_id(0) == 0)
    def _():
        PM[...] = order_matrix()

    order = PM[...]
    features = x_ref.shape[1]
    groups = features // LANES
    wide = 2 * LANES
    ones = jnp.ones((TILE, LANES), BF16)
    keep_ref[...] = jnp.dot(order * (1 - res_ref[0]).astype(F32).astype(BF16), ones, preferred_element_type=F32)
    live_ref[...] = jnp.dot(order * pad_ref[0].astype(F32).astype(BF16), ones, preferred_element_type=F32)
    shift = None
    first = second = None
    for g in range(0, features, wide):
        value = to_rows(order, x_ref[:, g : g + wide])
        XP[:, g : g + wide] = value
        if shift is None:
            shift = jnp.broadcast_to(value[:, 0:1], (TILE, LANES))
            S1[...] = shift
        one, two = value[:, :LANES] - shift, value[:, LANES:] - shift
        first = one + two if first is None else first + (one + two)
        squares = one * one + two * two
        second = squares if second is None else second + squares
    drift = jnp.sum(first, axis=1, keepdims=True) * (1.0 / features)
    spread = jnp.sum(second, axis=1, keepdims=True) * (1.0 / features) - drift * drift
    mu_ref[...] = shift + drift
    inv_ref[...] = jnp.broadcast_to(lax.rsqrt(jnp.maximum(spread, 0.0) + epsilon), inv_ref.shape)
    tall = 16

    def scaled(i, carry):
        rows = pl.ds(pl.multiple_of(i * tall, tall), tall)
        mean = mu_ref[rows, :]
        scale = inv_ref[rows, :]
        for g in range(groups):
            at = slice(g * LANES, (g + 1) * LANES)
            value = (XP[rows, at] - mean) * scale * gain_ref[0:1, at] + bias_ref[0:1, at]
            out_ref[rows, at] = value.astype(BF16)
        return carry

    lax.fori_loop(0, TILE // tall, scaled, 0, unroll=2)
    channels = own_ref.shape[1]
    own_ref[...] = XP[:, pl.ds(pl.multiple_of(meta[M_GATE] * channels, channels), channels)].astype(BF16)


def norm(meta, x, gain, bias, resets, padding, channels):
    tokens, features = x.shape
    tiles = tokens // TILE
    row = pl.BlockSpec((TILE, features), lambda t, m: (t, 0))
    whole = pl.BlockSpec((1, features), lambda t, m: (0, 0))
    flag = pl.BlockSpec((1, 1, TILE), lambda t, m: (t, 0, 0))
    stat = pl.BlockSpec((TILE, LANES), lambda t, m: (t, 0))
    stats = struct((tokens, LANES), F32)
    return call(
        norm_kernel,
        meta,
        (x, gain[None], bias[None], resets.reshape(tiles, 1, TILE), padding.reshape(tiles, 1, TILE)),
        (tiles,),
        [row, whole, whole, flag, flag],
        [row, stat, stat, pl.BlockSpec((TILE, channels), lambda t, m: (t, 0)), stat, stat],
        [struct(x.shape, BF16), stats, stats, struct((tokens, channels), BF16), stats, stats],
        scratch=[pltpu.VMEM((TILE, TILE), BF16), pltpu.VMEM((TILE, features), F32)] + [pltpu.VMEM((TILE, LANES), F32)] * 2,
        cost=cost(8 * tokens * features, 4 * tokens * features),
    )


def column_of(meta, table, plane, block):
    blk = block ^ meta[M_CORE] if plane == 2 else block
    return pl.multiple_of((blk * 3 + meta[table + plane]) * LANES, LANES)


def cut_kernel(widths, meta, *refs):
    for n, width in enumerate(widths):
        out_ref = refs[sum(widths) + n]
        for b in range(width):
            out_ref[:, b * LANES : (b + 1) * LANES] = refs[sum(widths[:n]) + b][...]


def cut(meta, weight, pieces, tb=512):
    rows = weight.shape[0]
    widths = [width for _, width in pieces]
    specs = [
        pl.BlockSpec((tb, LANES), lambda t, m, at=at, b=b: (t, m[at] + b)) for at, width in pieces for b in range(width)
    ]
    return call(
        functools.partial(cut_kernel, widths),
        meta,
        [weight] * len(specs),
        (rows // tb,),
        specs,
        [pl.BlockSpec((tb, width * LANES), lambda t, m: (t, 0)) for width in widths],
        [struct((rows, width * LANES), BF16) for width in widths],
        cost=cost(0, 4 * rows * LANES * sum(widths)),
    )


def unit_specs(units, rows, row_of):
    return [pl.BlockSpec((rows, LANES), lambda *i, at=at, b=b: (row_of(*i), (i[-1][at] if at else 0) + b)) for _, at, b in units]


def gather_units(meta, table, refs, W, base):
    for n, ref in enumerate(refs):
        at = pl.multiple_of(base + column_of(meta, table, n // 2, n % 2), LANES)
        W[:, pl.ds(at, LANES)] = ref[...]


def project_kernel(table, meta, normed_ref, *refs):
    out_ref, W = refs[-2:]

    @pl.when(pl.program_id(0) == 0)
    def _():
        gather_units(meta, table, refs[:6], W, 0)

    out_ref[...] = jnp.dot(normed_ref[...], W[...], preferred_element_type=F32).astype(BF16)


def project(meta, table, normed, units, tb=512):
    tokens, features = normed.shape
    columns = 6 * LANES
    return call(
        functools.partial(project_kernel, table),
        meta,
        [normed] + [array for array, _, _ in units],
        (tokens // tb,),
        [pl.BlockSpec((tb, features), lambda t, m: (t, 0))] + unit_specs(units, features, lambda t, m: 0),
        pl.BlockSpec((tb, columns), lambda t, m: (t, 0)),
        struct((tokens, columns), BF16),
        scratch=[pltpu.VMEM((features, columns), BF16)],
        cost=cost(2 * tokens * features * columns, 2 * tokens * (features + 2 * columns)),
    )


def sigmoid(z):
    return 0.5 * jnp.tanh(0.5 * z) + 0.5


def scan_kernel(meta, u_ref, x_ref, g_ref, keep_ref, live_ref, prm_ref, *refs):
    (hid_ref, ds_ref, direct_ref, vec_ref, PM, A, B, FG, R, PV, GL, XF, UT, HP, CE, PE, CI, EI) = refs[-18:]
    length = x_ref.shape[0]
    tiles = length // TILE
    seg = TILE // 8
    rows_in = 64
    each = TILE // rows_in
    groups = rows_in // 8
    pf, pr, bf, br = (jnp.broadcast_to(prm_ref[i : i + 1, :], (rows_in, LANES)) for i in range(4))

    @pl.when(pl.program_id(0) == 0)
    def _():
        PM[...] = order_matrix()

    order = PM[...]
    for q in range(tiles):
        GL[q * TILE : (q + 1) * TILE, :] = to_rows(order, g_ref[q * TILE : (q + 1) * TILE, :])

    zeros = jnp.zeros((8, LANES), F32)
    ones = jnp.ones((8, LANES), F32)

    def rows_at(i):
        return pl.ds(pl.multiple_of(i * rows_in, rows_in), rows_in)

    def tile_at(i):
        return pl.ds(pl.multiple_of((i // each) * 8, 8), 8)

    def gates(i, carry):
        rows = rows_at(i)
        x = x_ref[rows, :].astype(F32)
        ut = u_ref[rows, 0:LANES].astype(F32)
        forget = sigmoid(u_ref[rows, LANES : 2 * LANES].astype(F32) + pf * x + bf)
        reset = sigmoid(u_ref[rows, 2 * LANES :].astype(F32) + pr * x + br)
        a = forget * keep_ref[rows, :]
        b = (1.0 - forget) * ut
        gl = GL[rows, :] * live_ref[rows, :]
        d = gl * reset
        XF[rows, :] = x
        UT[rows, :] = ut
        FG[rows, :] = forget
        R[rows, :] = reset
        A[rows, :] = a
        B[rows, :] = b
        GL[rows, :] = gl
        fresh = i % each == 0
        c, p, e = (jnp.where(fresh, start, old) for start, old in zip((zeros, ones, zeros), carry))
        for j in range(groups):
            at = slice(8 * j, 8 * j + 8)
            c = a[at] * c + b[at]
            p = a[at] * p
            e = e + p * d[at]
        CE[tile_at(i), :] = c
        PE[tile_at(i), :] = p
        EI[tile_at(i), :] = e
        return (c, p, e)

    lax.fori_loop(0, tiles * each, gates, (zeros, ones, zeros))

    count = 8 * tiles
    c = jnp.zeros((1, LANES), F32)
    e = jnp.zeros((1, LANES), F32)
    for j in range(count):
        CI[j : j + 1, :] = c
        c = CE[j : j + 1, :] + PE[j : j + 1, :] * c
        r = count - 1 - j
        own = EI[r : r + 1, :]
        EI[r : r + 1, :] = e
        e = own + PE[r : r + 1, :] * e

    def forward(i, carry):
        out = []
        for q in range(tiles):
            rows = pl.ds(pl.multiple_of(q * TILE + i * 8, 8), 8)
            PV[rows, :] = carry[q]
            out.append(A[rows, :] * carry[q] + B[rows, :])
        return tuple(out)

    lax.fori_loop(0, seg, forward, tuple(CI[8 * q : 8 * q + 8, :] for q in range(tiles)), unroll=4)

    def fold(v):
        return v.reshape(groups, 8, LANES).sum(axis=0)

    def grads(n, carry):
        i = tiles * each - 1 - n
        rows = rows_at(i)
        e, s0, s1, s2, s3 = carry
        e = jnp.where(n % each == 0, EI[tile_at(i), :], e)
        g = GL[rows, :]
        reset = R[rows, :]
        a = A[rows, :]
        d = g * reset
        dcs = [None] * groups
        for j in reversed(range(groups)):
            at = slice(8 * j, 8 * j + 8)
            dcs[j] = d[at] + e
            e = a[at] * dcs[j]
        dc = jnp.concatenate(dcs, axis=0)
        x = XF[rows, :]
        forget = FG[rows, :]
        prev = PV[rows, :]
        gap = a * prev + B[rows, :] - x
        HP[rows, :] = (live_ref[rows, :] * (x + reset * gap)).astype(BF16)
        rest = 1.0 - reset
        dreset = g * gap * (reset * rest)
        dtilde = dc * (1.0 - forget)
        dforget = dtilde * forget * (prev * keep_ref[rows, :] - UT[rows, :])
        ds_ref[rows, 0:LANES] = dtilde.astype(BF16)
        ds_ref[rows, LANES : 2 * LANES] = dforget.astype(BF16)
        ds_ref[rows, 2 * LANES :] = dreset.astype(BF16)
        direct_ref[rows, :] = (g * rest + dforget * pf + dreset * pr).astype(BF16)
        return (e, s0 + fold(dforget * x), s1 + fold(dreset * x), s2 + fold(dforget), s3 + fold(dreset))

    sums = lax.fori_loop(0, tiles * each, grads, (zeros,) * 5)[1:]
    for n, s in enumerate(sums):
        vec_ref[n : n + 1, :] = jnp.sum(s, axis=0, keepdims=True)
    vec_ref[4:8, :] = jnp.zeros((4, LANES), F32)
    for q in range(tiles):
        at = slice(q * TILE, (q + 1) * TILE)
        hid_ref[at, :] = to_tokens(order, HP[at, :]).astype(BF16)


def scan(meta, half, u, x, grad, keep, live, params, earlier):
    length, channels = x.shape
    blocks = u.shape[1] // (3 * LANES)
    col = lambda k, m: (0, m[half] * blocks + k)
    tall = (length, LANES)
    chunk = pl.BlockSpec((length, 3 * LANES), lambda k, m: (0, k))
    fixed = pl.BlockSpec(tall, lambda k, m: (0, 0))
    own = pl.BlockSpec(tall, col)
    small = pl.BlockSpec((8, LANES), col)
    in_specs = [chunk, own, own, fixed, fixed, small]
    args = [u, x, grad, keep, live, params]
    aliases = None
    if earlier is not None:
        aliases = {len(args) + 1: 0, len(args) + 2: 2, len(args) + 3: 3}
        args += list(earlier)
        in_specs += [pl.BlockSpec(memory_space=pl.ANY)] * 3
    ends = pltpu.VMEM((8 * length // TILE, LANES), F32)
    return call(
        scan_kernel,
        meta,
        args,
        (blocks,),
        in_specs,
        [own, chunk, own, small],
        [
            struct((length, channels), BF16),
            struct(u.shape, BF16),
            struct((length, channels), BF16),
            struct((8, channels), F32),
        ],
        scratch=[pltpu.VMEM((TILE, TILE), BF16)]
        + [pltpu.VMEM(tall, F32)] * 8
        + [pltpu.VMEM(tall, BF16)]
        + [ends] * 4,
        aliases=aliases,
        cost=cost(60 * length * channels // 2, 9 * length * channels, length * channels),
    )


def wgrad_kernel(meta, normed_ref, ds_ref, a_ref, b_ref):
    first = pl.program_id(0) < pl.num_programs(0) // 2
    dims = (((0,), (0,)), ((), ()))

    @pl.when(first)
    def _():
        a_ref[...] = lax.dot_general(normed_ref[...], ds_ref[...], dims, preferred_element_type=F32).astype(BF16)

    @pl.when(jnp.logical_not(first))
    def _():
        b_ref[...] = lax.dot_general(normed_ref[...], ds_ref[...], dims, preferred_element_type=F32).astype(BF16)


def wgrad(meta, normed, ds, first, mb=512):
    tokens, features = normed.shape
    width = ds.shape[1]
    rows = features // 4
    steps = rows // mb

    def lhs(i, m):
        return (0, m[first + i // steps] * steps + i % steps)

    return call(
        wgrad_kernel,
        meta,
        (normed, ds),
        (2 * steps,),
        [
            pl.BlockSpec((tokens, mb), lhs),
            pl.BlockSpec((tokens, width), lambda i, m: (0, 0)),
        ],
        [
            pl.BlockSpec((mb, width), lambda i, m: (jnp.minimum(i, steps - 1), 0)),
            pl.BlockSpec((mb, width), lambda i, m: (jnp.maximum(i - steps, 0), 0)),
        ],
        [struct((rows, width), BF16)] * 2,
        cost=cost(4 * tokens * rows * width, 2 * tokens * (features // 2 + width)),
    )


def back_kernel(meta, ds1_ref, ds2_ref, *refs):
    out_ref, W = refs[-2:]
    chunk = ds1_ref.shape[1]

    @pl.when(pl.program_id(1) == 0)
    def _():
        gather_units(meta, M_S1, refs[:6], W, 0)
        gather_units(meta, M_S2, refs[6:12], W, chunk)

    dims = (((1,), (1,)), ((), ()))
    value = lax.dot_general(ds1_ref[...], W[:, :chunk], dims, preferred_element_type=F32)
    value += lax.dot_general(ds2_ref[...], W[:, chunk:], dims, preferred_element_type=F32)
    out_ref[0] = value.astype(BF16)


def back(meta, ds1, ds2, units, first, tb=1024):
    tokens, width = ds1.shape
    features = units[0][0].shape[0]
    block = features // 4
    dspec = pl.BlockSpec((tb, width), lambda n, t, m: (t, 0))
    return call(
        back_kernel,
        meta,
        [ds1, ds2] + [array for array, _, _ in units],
        (2, tokens // tb),
        [dspec, dspec] + unit_specs(units, block, lambda n, t, m: m[first + n]),
        pl.BlockSpec((1, tb, block), lambda n, t, m: (n, t, 0)),
        struct((2, tokens, block), BF16),
        scratch=[pltpu.VMEM((block, 2 * width), BF16)],
        cost=cost(8 * tokens * block * width, 8 * tokens * width),
    )


def unit_of(x_ref, mu_ref, inv_ref):
    repeat = x_ref.shape[1] // LANES
    mu = jnp.concatenate([mu_ref[...]] * repeat, axis=1)
    inv = jnp.concatenate([inv_ref[...]] * repeat, axis=1)
    return (x_ref[...].astype(F32) - mu) * inv, inv


def lane_sums(value):
    part = value[:, :LANES]
    for g in range(1, value.shape[1] // LANES):
        part = part + value[:, g * LANES : (g + 1) * LANES]
    return jnp.sum(part.T, axis=0, keepdims=True)


def tail_sums_kernel(meta, k_ref, rc_ref, ry_ref, x_ref, mu_ref, inv_ref, gain_ref, dn_ref, row_ref, col_ref):
    unit, _ = unit_of(x_ref, mu_ref, inv_ref)
    dn = k_ref[0].astype(F32) + rc_ref[0].astype(F32) + ry_ref[...].astype(F32)
    dn_ref[...] = dn
    gu = dn * gain_ref[...]
    row_ref[0:1, :] = lane_sums(gu)
    row_ref[1:2, :] = lane_sums(gu * unit)
    row_ref[2:8, :] = jnp.zeros((6, row_ref.shape[1]), F32)

    @pl.when(pl.program_id(0) == 0)
    def _():
        col_ref[...] = jnp.zeros_like(col_ref)

    col_ref[0:1, :] += jnp.sum(dn * unit, axis=0, keepdims=True)
    col_ref[1:2, :] += jnp.sum(dn, axis=0, keepdims=True)


def tail_sums(meta, keep, got, far, x, mu, inv, gain, tb=512):
    tokens, channels = far.shape
    part = pl.BlockSpec((1, tb, channels), lambda t, m: (1, t, 0))
    wide = pl.BlockSpec((tb, channels), lambda t, m: (t, 0))
    stat = pl.BlockSpec((tb, LANES), lambda t, m: (t, 0))
    return call(
        tail_sums_kernel,
        meta,
        (keep, got, far, x, mu, inv, gain[None]),
        (tokens // tb,),
        [part, part, wide, wide, stat, stat, pl.BlockSpec((1, channels), lambda t, m: (0, m[M_GATE]))],
        [
            wide,
            pl.BlockSpec((8, tb), lambda t, m: (0, t)),
            pl.BlockSpec((8, channels), lambda t, m: (0, 0)),
        ],
        [struct((tokens, channels), F32), struct((8, tokens), F32), struct((8, channels), F32)],
        cost=cost(20 * tokens * channels, 12 * tokens * channels),
    )


def tail_kernel(features, meta, dn_ref, row_ref, x_ref, mu_ref, inv_ref, gain_ref, direct_ref, out_ref, PM):
    @pl.when(pl.program_id(0) == 0)
    def _():
        PM[...] = order_matrix()

    unit, inv = unit_of(x_ref, mu_ref, inv_ref)
    repeat = x_ref.shape[1] // LANES
    tb = x_ref.shape[0]

    def mean(n):
        row = row_ref[n : n + 1, :] * (1.0 / features)
        return jnp.concatenate([jnp.broadcast_to(row, (LANES, tb)).T] * repeat, axis=1)

    gu = dn_ref[...] * gain_ref[...]
    value = (inv * (gu - mean(0) - unit * mean(1)) + direct_ref[...].astype(F32)).astype(BF16)
    for q in range(tb // TILE):
        at = slice(q * TILE, (q + 1) * TILE)
        out_ref[at, :] = to_tokens(PM[...], value[at]).astype(BF16)


def tail(meta, dn, rows, x, mu, inv, gain, direct, features, tb=512):
    tokens, channels = dn.shape
    wide = pl.BlockSpec((tb, channels), lambda t, m: (t, 0))
    stat = pl.BlockSpec((tb, LANES), lambda t, m: (t, 0))
    return call(
        functools.partial(tail_kernel, features),
        meta,
        (dn, rows, x, mu, inv, gain[None], direct),
        (tokens // tb,),
        [
            wide,
            pl.BlockSpec((rows.shape[0], tb), lambda t, m: (0, t)),
            wide,
            stat,
            stat,
            pl.BlockSpec((1, channels), lambda t, m: (0, m[M_GATE])),
            wide,
        ],
        wide,
        struct((tokens, channels), BF16),
        scratch=[pltpu.VMEM((TILE, TILE), BF16)],
        cost=cost(10 * tokens * channels, 12 * tokens * channels),
    )


def halve_kernel(meta, *refs):
    ins, (away_ref, stay_ref) = refs[:-2], refs[-2:]
    for n, out_ref in ((0, away_ref), (1, stay_ref)):
        part = ins[n * len(ins) // 2 : (n + 1) * len(ins) // 2]
        if len(part) == 4:
            for o in range(2):
                out_ref[o] = (part[o][...].astype(F32) + part[2 + o][...].astype(F32)).astype(BF16)
        else:
            out_ref[...] = (part[0][...].astype(F32) + part[1][...].astype(F32)).astype(BF16)


def halve(meta, at, kept, got, parts=2):
    if len(kept) == 2:
        rows, width = kept[0].shape
        lead = ()
    else:
        lead, rows, width = kept[0].shape
        lead = (lead,)
    half = rows // 2
    tb = half // parts
    zeros = (0,) * len(lead)
    specs, args = [], []
    for side in range(2):
        for array in (*kept, *got):
            specs.append(
                pl.BlockSpec((*lead, tb, width), lambda i, m, side=side: (*zeros, (m[at] ^ (1 - side)) * parts + i, 0))
            )
            args.append(array)
    out = pl.BlockSpec((2, tb, width), lambda i, m: (0, i, 0))
    return call(
        halve_kernel,
        meta,
        args,
        (parts,),
        specs,
        [out, out],
        [struct((2, half, width), BF16)] * 2,
        cost=cost(4 * rows * width, 12 * rows * width),
    )


def split_kernel(late, half, meta, a_ref, b_ref, near_ref, far_ref):
    core = meta[M_CORE]
    h = meta[half]
    pair_ref, single_ref = (far_ref, near_ref) if late else (near_ref, far_ref)

    def take(owner, stream, block):
        col = pl.ds(pl.multiple_of((block * 3 + stream) * LANES, LANES), LANES)
        return (a_ref[owner, :, col].astype(F32) + b_ref[owner, :, col].astype(F32)).astype(BF16)

    for store in range(2):
        k = core ^ store
        for owner in range(2):
            for block in range(2):
                at = (2 * owner + block) * LANES
                pair_ref[store, :, at : at + LANES] = take(owner, k + h, block)
            single_ref[store, :, owner * LANES : (owner + 1) * LANES] = take(owner, 2 * (1 - h), k)


def split(meta, half, late, kept, got):
    _, rows, width = kept.shape
    pair, single = 4 * LANES, 2 * LANES
    widths = (single, pair) if late else (pair, single)
    whole = pl.BlockSpec((2, rows, width), lambda i, m: (0, 0, 0))
    return call(
        functools.partial(split_kernel, late, half),
        meta,
        (kept, got),
        (1,),
        [whole] * 2,
        [pl.BlockSpec((2, rows, w), lambda i, m: (0, 0, 0)) for w in widths],
        [struct((2, rows, w), BF16) for w in widths],
        cost=cost(2 * rows * width, 12 * rows * width),
    )


def join_kernel(meta, a_ref, b_ref, *outs):
    rows = a_ref.shape[1]
    for n, out_ref in enumerate(outs):
        out_ref[:rows, :] = a_ref[n]
        out_ref[rows:, :] = b_ref[n]


def join(meta, a, b):
    _, rows, width = a.shape
    whole = pl.BlockSpec((2, rows, width), lambda i, m: (0, 0, 0))
    out = pl.BlockSpec((2 * rows, width), lambda i, m: (0, 0))
    return call(
        join_kernel,
        meta,
        (a, b),
        (1,),
        [whole] * 2,
        [out] * 2,
        [struct((2 * rows, width), BF16)] * 2,
        cost=cost(0, 16 * rows * width),
    )


def place_kernel(blocks, meta, *refs):
    out_ref = refs[-1]
    step = pl.program_id(0)
    piece = out_ref.shape[1] // 4
    unit = piece // 3
    rows = out_ref.shape[0] // blocks
    core = meta[M_CORE]
    for stream in range(2):
        for part in range(2):

            @pl.when(step == stream * 2 + part)
            def _(stream=stream, part=part):
                one = refs[stream * 2 + part]
                two = refs[4 + stream * 2 + part]
                inner = meta[M_RHO + stream] % blocks

                def put(owner, single, src, col):
                    base = meta[M_OWN + (owner ^ stream)] * piece
                    wide = unit if single else 2 * unit
                    at = base + (jnp.where(core == 0, 2 * unit, 0) if single else core * unit)
                    at = pl.ds(pl.multiple_of(at, LANES), wide)
                    for j in range(blocks):
                        to = pl.ds(pl.multiple_of((inner ^ j) * rows, rows), rows)
                        out_ref[to, at] = src[j * rows : (j + 1) * rows, col : col + wide].astype(F32)

                put(0, False, one, 0)
                put(1, False, one, 2 * unit)
                put(2, True, one, 4 * unit)
                put(3, True, one, 5 * unit)
                put(0, True, two, 0)
                put(1, True, two, unit)
                put(2, False, two, 2 * unit)
                put(3, False, two, 4 * unit)


def place(meta, parts1, parts2, n_dp, features, columns):
    blocks = n_dp // 2
    whole = pl.BlockSpec((features // 4, columns // 2), lambda i, m: (0, 0))

    def where_to(i, m):
        stream = i // 2
        return ((m[M_CORE] ^ stream) * 2 + (i % 2 ^ m[M_RHO + stream] // blocks), 0)

    return call(
        functools.partial(place_kernel, blocks),
        meta,
        (*parts1, *parts2),
        (4,),
        [whole] * 8,
        pl.BlockSpec((features // 4, columns), where_to),
        struct((features, columns), F32),
        cost=cost(features * columns, 6 * features * columns),
    )


M_GATE, M_CORE, M_H1, M_H2 = 0, 1, 2, 3
M_S1, M_S2 = 4, 7
M_SEND, M_KEEP = 10, 12
M_OUT, M_IN = 14, 16
M_OWN, M_RHO = 18, 22
M_TO2, M_TO3, M_NEAR, M_LATE2, M_LATE3 = 24, 25, 26, 27, 28
M_PAIR, M_SINGLE, M_GOT_PAIR, M_GOT_SINGLE = 29, 30, 31, 32
M_BIT = 33


def shards(
    n_dp,
    n_gate,
    inputs,
    weight,
    ln_gain,
    ln_bias,
    forget_peep,
    reset_peep,
    forget_bias,
    reset_bias,
    resets,
    padding,
    grad_out,
):
    rows, tokens, features = inputs.shape
    assert rows == 1 and n_gate == 4
    channels = forget_peep.shape[0]
    assert channels == 4 * LANES
    bits = n_dp.bit_length() - 1
    assert 1 << bits == n_dp
    gate = lax.axis_index("gate")
    dp = lax.axis_index("dp")
    hi, core = gate // 2, gate % 2
    other = 1 - core

    orders = [list(range(bits)), [1, 0, *range(2, bits)]]

    def bit(stream, step):
        return (dp >> jnp.where(stream == 0, orders[0][step], orders[1][step])) & 1

    def rho(stream):
        value = 0
        for step in range(bits):
            value = value * 2 + bit(stream, step)
        return value

    def streams(h):
        return [core + h, other + h, 2 * (1 - h)]

    h1, h2 = hi, 1 - hi
    far = (1 - hi) * 2
    single, pair = 2 * other, core
    meta = jnp.stack(
        [gate, core, h1, h2, *streams(h1), *streams(h2)]
        + [other * 2 + 1 - bit(other, 0), core * 2 + 1 - bit(core, 0)]
        + [other * 2 + bit(other, 0), core * 2 + bit(core, 0)]
        + [far + other, hi * 2 + other, far + core, hi * 2 + core]
        + [gate, hi * 2 + other, far + core, far + other]
        + [rho(core), rho(other)]
        + [(far + core) * 3 + single, (far + other) * 3 + single, (hi * 2 + other) * 3]
        + [(far + core) * 3 + pair, (far + other) * 3 + pair]
        + [gate * 3 + pair, gate * 3 + single, other, 2 * core]
        + [bit(core, step) for step in range(bits)]
    ).astype(jnp.int32)

    def over_gate(value, delta):
        return lax.ppermute(value, "gate", [(g, g ^ delta) for g in range(n_gate)])

    def over_dp(value, step):
        pairs = [
            (d * n_gate + g, (d ^ (1 << orders[g % 2][step])) * n_gate + g) for d in range(n_dp) for g in range(n_gate)
        ]
        return lax.ppermute(value, ("dp", "gate"), pairs)

    def after(value, *others):
        return lax.optimization_barrier((value, *others))[0]

    x = inputs.reshape(tokens, features)
    grad = grad_out.reshape(tokens, channels)
    params = jnp.concatenate(
        [jnp.stack([forget_peep, reset_peep, forget_bias, reset_bias]), jnp.zeros((4, channels), F32)]
    )

    to2, to3 = cut(meta, weight, [(M_TO2, 1), (M_TO3, 1)])
    sent2, sent3 = over_gate(to2, 2), over_gate(to3, 3)
    normed, mu, inv, own_x, keep, live = norm(
        after(meta, to2, to3), x, ln_gain, ln_bias, resets, padding, channels
    )
    near, away2, away3 = cut(after(meta, normed), weight, [(M_NEAR, 3), (M_LATE2, 2), (M_LATE3, 2)])
    near = over_gate(near, 1)
    late2, late3 = over_gate(away2, 2), over_gate(away3, 3)
    units1 = [(weight, M_PAIR, 0), (weight, M_PAIR, 1), (near, M_GOT_PAIR, 0), (near, M_GOT_PAIR, 1)]
    units1 += [(sent2, None, 0), (sent3, None, 0)]
    units2 = [(late2, None, 0), (late2, None, 1), (late3, None, 0), (late3, None, 1)]
    units2 += [(weight, M_SINGLE, 0), (near, M_GOT_SINGLE, 0)]
    units = units1 + units2

    def first_sends(meta, ds):
        theirs, mine = wgrad(meta, normed, ds, M_SEND)
        return mine, [over_dp(mine, 0), over_dp(over_gate(theirs, 1), 0)]

    def first_keeps(meta, ds):
        theirs, mine = wgrad(meta, normed, ds, M_KEEP)
        return [mine, over_gate(theirs, 1)]

    def gathered(meta, half, late, kept, got):
        near, far = split(meta, half, late, kept, got)
        return near, over_gate(far, 2)

    def last_steps(meta, shard):
        for step in reversed(range(2, bits)):
            shard = jnp.concatenate([shard, over_dp(shard, step)], axis=1)
        return shard

    u1 = project(after(meta, away2, away3), M_S1, normed, units1)
    hidden, ds1, direct, vecs = scan(meta, M_H1, u1, own_x, grad, keep, live, params, None)
    mine1, got1 = first_sends(meta, ds1)
    kept1 = first_keeps(after(meta, mine1), ds1)
    u2 = project(after(meta, kept1[0]), M_S2, normed, units2)
    away1, stay1 = halve(after(meta, u2), M_BIT + 1, kept1, got1)
    step1 = over_dp(away1, 1)
    hidden, ds2, direct, vecs = scan(
        after(meta, away1), M_H2, u2, own_x, grad, keep, live, params, (hidden, direct, vecs)
    )
    for step in range(2, bits):
        away1, stay1 = halve(after(meta, ds2), M_BIT + step, [stay1], [step1])
        step1 = over_dp(away1, step)
    mine2, got2 = first_sends(after(meta, away1), ds2)
    kept2 = first_keeps(after(meta, mine2), ds2)
    send = back(after(meta, kept2[0]), ds1, ds2, units, M_OUT)
    got = over_gate(send, 1)
    near1, far1 = gathered(after(meta, send), M_H1, False, stay1, step1)
    away2, stay2 = halve(after(meta, near1), M_BIT + 1, kept2, got2)
    step2 = over_dp(away2, 1)
    shard1 = jnp.concatenate([near1, far1], axis=2)
    kept = back(after(meta, away2, shard1), ds1, ds2, units, M_IN)
    far_send = (kept[0].astype(F32) + got[0].astype(F32)).astype(BF16)
    far_part = over_gate(far_send, 2)

    def all_gather(meta, shard):
        for step in reversed(range(2, bits)):
            shard = jnp.concatenate([shard, over_dp(shard, step)], axis=1)
        mine, theirs = join(meta, shard, over_dp(shard, 1))
        moved = over_dp(theirs, 0)
        return [mine, over_dp(mine, 0), over_gate(theirs, 1), over_gate(moved, 1)]

    for step in range(2, bits):
        away2, stay2 = halve(after(meta, kept), M_BIT + step, [stay2], [step2])
        step2 = over_dp(away2, step)
    parts1 = all_gather(meta, shard1)
    near2, far2 = gathered(meta, M_H2, True, stay2, step2)
    shard2 = jnp.concatenate([near2, far2], axis=2)
    parts2 = all_gather(meta, shard2)

    dn, row_sums, col_sums = tail_sums(meta, kept, got, far_part, own_x, mu, inv, ln_gain)
    for delta in (1, 2):
        row_sums = row_sums + over_gate(row_sums, delta)
    dinputs = tail(meta, dn, row_sums, own_x, mu, inv, ln_gain, direct, features)

    totals = jnp.concatenate([col_sums[:2], vecs[:4]], axis=0)
    for step in range(bits):
        totals = totals + lax.ppermute(totals, "dp", [(d, d ^ (1 << step)) for d in range(n_dp)])

    grad_weight = place(meta, parts1, parts2, n_dp, features, weight.shape[1])
    return (
        hidden.reshape(rows, tokens, channels),
        dinputs.reshape(rows, tokens, channels),
        grad_weight,
        totals[0],
        totals[1],
        totals[2],
        totals[3],
        totals[4],
        totals[5],
    )


def solution(mesh):
    return jax.shard_map(
        functools.partial(shards, mesh.shape["dp"], mesh.shape["gate"]),
        mesh=mesh,
        in_specs=(
            P("dp", None, None),
            P(None, "gate"),
            P(),
            P(),
            P("gate"),
            P("gate"),
            P("gate"),
            P("gate"),
            P("dp", None),
            P("dp", None),
            P("dp", None, "gate"),
        ),
        out_specs=(
            P("dp", None, "gate"),
            P("dp", None, "gate"),
            P(None, "gate"),
            P("gate"),
            P("gate"),
            P("gate"),
            P("gate"),
            P("gate"),
            P("gate"),
        ),
        check_vma=False,
    )
```

```python
import functools

import jax
import jax.numpy as jnp
from jax import lax
from jax.experimental import pallas as pl
from jax.experimental.pallas import tpu as pltpu
from jax.sharding import PartitionSpec as P

epsilon = 1e-05
F32 = jnp.float32
BF16 = jnp.bfloat16
LANES = 128
VMEM_LIMIT = 60 * 1024 * 1024
COVER = 20


def call(kernel, meta, args, grid, in_specs, out_specs, out_shape, scratch=(), aliases=None, cost=None):
    return pl.pallas_call(
        kernel,
        grid_spec=pltpu.PrefetchScalarGridSpec(
            num_scalar_prefetch=1,
            grid=grid,
            in_specs=in_specs,
            out_specs=out_specs,
            scratch_shapes=list(scratch),
        ),
        out_shape=out_shape,
        input_output_aliases=aliases or {},
        compiler_params=pltpu.CompilerParams(
            dimension_semantics=("arbitrary",) * len(grid), vmem_limit_bytes=VMEM_LIMIT
        ),
        cost_estimate=cost,
    )(meta, *args)


def cost(flops, nbytes, trans=0, weight=1):
    return pl.CostEstimate(flops=int(weight * flops), bytes_accessed=int(weight * nbytes), transcendentals=int(trans))


def struct(shape, dtype):
    return jax.ShapeDtypeStruct(shape, dtype)


TILE = 256


def order_matrix():
    row = lax.broadcasted_iota(jnp.int32, (TILE, TILE), 0)
    token = lax.broadcasted_iota(jnp.int32, (TILE, TILE), 1)
    return jnp.where(token == (row % 8) * (TILE // 8) + row // 8, 1.0, 0.0).astype(BF16)


def to_rows(order, value):
    return jnp.dot(order, value, preferred_element_type=F32)


def to_tokens(order, value):
    return lax.dot_general(order, value, (((0,), (0,)), ((), ())), preferred_element_type=F32)


def norm_kernel(
    meta, x_ref, gain_ref, bias_ref, res_ref, pad_ref, out_ref, mu_ref, inv_ref, own_ref, keep_ref, live_ref, PM, XP, S1, S2
):
    @pl.when(pl.program_id(0) == 0)
    def _():
        PM[...] = order_matrix()

    order = PM[...]
    features = x_ref.shape[1]
    groups = features // LANES
    wide = 2 * LANES
    ones = jnp.ones((TILE, LANES), BF16)
    keep_ref[...] = jnp.dot(order * (1 - res_ref[0]).astype(F32).astype(BF16), ones, preferred_element_type=F32)
    live_ref[...] = jnp.dot(order * pad_ref[0].astype(F32).astype(BF16), ones, preferred_element_type=F32)
    shift = None
    first = second = None
    for g in range(0, features, wide):
        value = to_rows(order, x_ref[:, g : g + wide])
        XP[:, g : g + wide] = value
        if shift is None:
            shift = jnp.broadcast_to(value[:, 0:1], (TILE, LANES))
            S1[...] = shift
        one, two = value[:, :LANES] - shift, value[:, LANES:] - shift
        first = one + two if first is None else first + (one + two)
        squares = one * one + two * two
        second = squares if second is None else second + squares
    drift = jnp.sum(first, axis=1, keepdims=True) * (1.0 / features)
    spread = jnp.sum(second, axis=1, keepdims=True) * (1.0 / features) - drift * drift
    mu_ref[...] = shift + drift
    inv_ref[...] = jnp.broadcast_to(lax.rsqrt(jnp.maximum(spread, 0.0) + epsilon), inv_ref.shape)
    tall = 16

    def scaled(i, carry):
        rows = pl.ds(pl.multiple_of(i * tall, tall), tall)
        mean = mu_ref[rows, :]
        scale = inv_ref[rows, :]
        for g in range(groups):
            at = slice(g * LANES, (g + 1) * LANES)
            value = (XP[rows, at] - mean) * scale * gain_ref[0:1, at] + bias_ref[0:1, at]
            out_ref[rows, at] = value.astype(BF16)
        return carry

    lax.fori_loop(0, TILE // tall, scaled, 0, unroll=2)
    channels = own_ref.shape[1]
    own_ref[...] = XP[:, pl.ds(pl.multiple_of(meta[M_GATE] * channels, channels), channels)].astype(BF16)


def norm(meta, x, gain, bias, resets, padding, channels):
    tokens, features = x.shape
    tiles = tokens // TILE
    row = pl.BlockSpec((TILE, features), lambda t, m: (t, 0))
    whole = pl.BlockSpec((1, features), lambda t, m: (0, 0))
    flag = pl.BlockSpec((1, 1, TILE), lambda t, m: (t, 0, 0))
    stat = pl.BlockSpec((TILE, LANES), lambda t, m: (t, 0))
    stats = struct((tokens, LANES), F32)
    return call(
        norm_kernel,
        meta,
        (x, gain[None], bias[None], resets.reshape(tiles, 1, TILE), padding.reshape(tiles, 1, TILE)),
        (tiles,),
        [row, whole, whole, flag, flag],
        [row, stat, stat, pl.BlockSpec((TILE, channels), lambda t, m: (t, 0)), stat, stat],
        [struct(x.shape, BF16), stats, stats, struct((tokens, channels), BF16), stats, stats],
        scratch=[pltpu.VMEM((TILE, TILE), BF16), pltpu.VMEM((TILE, features), F32)] + [pltpu.VMEM((TILE, LANES), F32)] * 2,
        cost=cost(8 * tokens * features, 4 * tokens * features, weight=COVER),
    )


def column_of(meta, table, plane, block):
    blk = block ^ meta[M_CORE] if plane == 2 else block
    return pl.multiple_of((blk * 3 + meta[table + plane]) * LANES, LANES)


def cut_kernel(widths, meta, *refs):
    for n, width in enumerate(widths):
        out_ref = refs[sum(widths) + n]
        for b in range(width):
            out_ref[:, b * LANES : (b + 1) * LANES] = refs[sum(widths[:n]) + b][...]


def cut(meta, weight, pieces, tb=512):
    rows = weight.shape[0]
    widths = [width for _, width in pieces]
    specs = [
        pl.BlockSpec((tb, LANES), lambda t, m, at=at, b=b: (t, m[at] + b)) for at, width in pieces for b in range(width)
    ]
    return call(
        functools.partial(cut_kernel, widths),
        meta,
        [weight] * len(specs),
        (rows // tb,),
        specs,
        [pl.BlockSpec((tb, width * LANES), lambda t, m: (t, 0)) for width in widths],
        [struct((rows, width * LANES), BF16) for width in widths],
        cost=cost(0, 4 * rows * LANES * sum(widths)),
    )


def unit_specs(units, rows, row_of):
    return [pl.BlockSpec((rows, LANES), lambda *i, at=at, b=b: (row_of(*i), (i[-1][at] if at else 0) + b)) for _, at, b in units]


def gather_units(meta, table, refs, W, base):
    for n, ref in enumerate(refs):
        at = pl.multiple_of(base + column_of(meta, table, n // 2, n % 2), LANES)
        W[:, pl.ds(at, LANES)] = ref[...]


def project_kernel(table, meta, normed_ref, *refs):
    out_ref, W = refs[-2:]

    @pl.when(pl.program_id(0) == 0)
    def _():
        gather_units(meta, table, refs[:6], W, 0)

    out_ref[...] = jnp.dot(normed_ref[...], W[...], preferred_element_type=F32).astype(BF16)


def project(meta, table, normed, units, tb=512):
    tokens, features = normed.shape
    columns = 6 * LANES
    return call(
        functools.partial(project_kernel, table),
        meta,
        [normed] + [array for array, _, _ in units],
        (tokens // tb,),
        [pl.BlockSpec((tb, features), lambda t, m: (t, 0))] + unit_specs(units, features, lambda t, m: 0),
        pl.BlockSpec((tb, columns), lambda t, m: (t, 0)),
        struct((tokens, columns), BF16),
        scratch=[pltpu.VMEM((features, columns), BF16)],
        cost=cost(2 * tokens * features * columns, 2 * tokens * (features + 2 * columns), weight=COVER),
    )


def sigmoid(z):
    return 0.5 * jnp.tanh(0.5 * z) + 0.5


def scan_kernel(meta, u_ref, x_ref, g_ref, keep_ref, live_ref, prm_ref, *refs):
    (hid_ref, ds_ref, direct_ref, vec_ref, PM, A, B, FG, R, PV, GL, XF, UT, HP, CE, PE, CI, EI) = refs[-18:]
    length = x_ref.shape[0]
    tiles = length // TILE
    seg = TILE // 8
    rows_in = 64
    each = TILE // rows_in
    groups = rows_in // 8
    pf, pr, bf, br = (jnp.broadcast_to(prm_ref[i : i + 1, :], (rows_in, LANES)) for i in range(4))

    @pl.when(pl.program_id(0) == 0)
    def _():
        PM[...] = order_matrix()

    order = PM[...]
    for q in range(tiles):
        GL[q * TILE : (q + 1) * TILE, :] = to_rows(order, g_ref[q * TILE : (q + 1) * TILE, :])

    zeros = jnp.zeros((8, LANES), F32)
    ones = jnp.ones((8, LANES), F32)

    def rows_at(i):
        return pl.ds(pl.multiple_of(i * rows_in, rows_in), rows_in)

    def tile_at(i):
        return pl.ds(pl.multiple_of((i // each) * 8, 8), 8)

    def gates(i, carry):
        rows = rows_at(i)
        x = x_ref[rows, :].astype(F32)
        ut = u_ref[rows, 0:LANES].astype(F32)
        forget = sigmoid(u_ref[rows, LANES : 2 * LANES].astype(F32) + pf * x + bf)
        reset = sigmoid(u_ref[rows, 2 * LANES :].astype(F32) + pr * x + br)
        a = forget * keep_ref[rows, :]
        b = (1.0 - forget) * ut
        gl = GL[rows, :] * live_ref[rows, :]
        d = gl * reset
        XF[rows, :] = x
        UT[rows, :] = ut
        FG[rows, :] = forget
        R[rows, :] = reset
        A[rows, :] = a
        B[rows, :] = b
        GL[rows, :] = gl
        fresh = i % each == 0
        c, p, e = (jnp.where(fresh, start, old) for start, old in zip((zeros, ones, zeros), carry))
        for j in range(groups):
            at = slice(8 * j, 8 * j + 8)
            c = a[at] * c + b[at]
            p = a[at] * p
            e = e + p * d[at]
        CE[tile_at(i), :] = c
        PE[tile_at(i), :] = p
        EI[tile_at(i), :] = e
        return (c, p, e)

    lax.fori_loop(0, tiles * each, gates, (zeros, ones, zeros))

    count = 8 * tiles
    c = jnp.zeros((1, LANES), F32)
    e = jnp.zeros((1, LANES), F32)
    for j in range(count):
        CI[j : j + 1, :] = c
        c = CE[j : j + 1, :] + PE[j : j + 1, :] * c
        r = count - 1 - j
        own = EI[r : r + 1, :]
        EI[r : r + 1, :] = e
        e = own + PE[r : r + 1, :] * e

    def forward(i, carry):
        out = []
        for q in range(tiles):
            rows = pl.ds(pl.multiple_of(q * TILE + i * 8, 8), 8)
            PV[rows, :] = carry[q]
            out.append(A[rows, :] * carry[q] + B[rows, :])
        return tuple(out)

    lax.fori_loop(0, seg, forward, tuple(CI[8 * q : 8 * q + 8, :] for q in range(tiles)), unroll=4)

    def fold(v):
        return v.reshape(groups, 8, LANES).sum(axis=0)

    def grads(n, carry):
        i = tiles * each - 1 - n
        rows = rows_at(i)
        e, s0, s1, s2, s3 = carry
        e = jnp.where(n % each == 0, EI[tile_at(i), :], e)
        g = GL[rows, :]
        reset = R[rows, :]
        a = A[rows, :]
        d = g * reset
        dcs = [None] * groups
        for j in reversed(range(groups)):
            at = slice(8 * j, 8 * j + 8)
            dcs[j] = d[at] + e
            e = a[at] * dcs[j]
        dc = jnp.concatenate(dcs, axis=0)
        x = XF[rows, :]
        forget = FG[rows, :]
        prev = PV[rows, :]
        gap = a * prev + B[rows, :] - x
        HP[rows, :] = (live_ref[rows, :] * (x + reset * gap)).astype(BF16)
        rest = 1.0 - reset
        dreset = g * gap * (reset * rest)
        dtilde = dc * (1.0 - forget)
        dforget = dtilde * forget * (prev * keep_ref[rows, :] - UT[rows, :])
        ds_ref[rows, 0:LANES] = dtilde.astype(BF16)
        ds_ref[rows, LANES : 2 * LANES] = dforget.astype(BF16)
        ds_ref[rows, 2 * LANES :] = dreset.astype(BF16)
        direct_ref[rows, :] = (g * rest + dforget * pf + dreset * pr).astype(BF16)
        return (e, s0 + fold(dforget * x), s1 + fold(dreset * x), s2 + fold(dforget), s3 + fold(dreset))

    sums = lax.fori_loop(0, tiles * each, grads, (zeros,) * 5)[1:]
    for n, s in enumerate(sums):
        vec_ref[n : n + 1, :] = jnp.sum(s, axis=0, keepdims=True)
    vec_ref[4:8, :] = jnp.zeros((4, LANES), F32)
    for q in range(tiles):
        at = slice(q * TILE, (q + 1) * TILE)
        hid_ref[at, :] = to_tokens(order, HP[at, :]).astype(BF16)


def scan(meta, half, u, x, grad, keep, live, params, earlier):
    length, channels = x.shape
    blocks = u.shape[1] // (3 * LANES)
    col = lambda k, m: (0, m[half] * blocks + k)
    tall = (length, LANES)
    chunk = pl.BlockSpec((length, 3 * LANES), lambda k, m: (0, k))
    fixed = pl.BlockSpec(tall, lambda k, m: (0, 0))
    own = pl.BlockSpec(tall, col)
    small = pl.BlockSpec((8, LANES), col)
    in_specs = [chunk, own, own, fixed, fixed, small]
    args = [u, x, grad, keep, live, params]
    aliases = None
    if earlier is not None:
        aliases = {len(args) + 1: 0, len(args) + 2: 2, len(args) + 3: 3}
        args += list(earlier)
        in_specs += [pl.BlockSpec(memory_space=pl.ANY)] * 3
    ends = pltpu.VMEM((8 * length // TILE, LANES), F32)
    return call(
        scan_kernel,
        meta,
        args,
        (blocks,),
        in_specs,
        [own, chunk, own, small],
        [
            struct((length, channels), BF16),
            struct(u.shape, BF16),
            struct((length, channels), BF16),
            struct((8, channels), F32),
        ],
        scratch=[pltpu.VMEM((TILE, TILE), BF16)]
        + [pltpu.VMEM(tall, F32)] * 8
        + [pltpu.VMEM(tall, BF16)]
        + [ends] * 4,
        aliases=aliases,
        cost=cost(60 * length * channels // 2, 9 * length * channels, length * channels, weight=COVER),
    )


def wgrad_kernel(meta, normed_ref, ds_ref, a_ref, b_ref):
    first = pl.program_id(0) < pl.num_programs(0) // 2
    dims = (((0,), (0,)), ((), ()))

    @pl.when(first)
    def _():
        a_ref[...] = lax.dot_general(normed_ref[...], ds_ref[...], dims, preferred_element_type=F32).astype(BF16)

    @pl.when(jnp.logical_not(first))
    def _():
        b_ref[...] = lax.dot_general(normed_ref[...], ds_ref[...], dims, preferred_element_type=F32).astype(BF16)


def wgrad(meta, normed, ds, first, mb=512):
    tokens, features = normed.shape
    width = ds.shape[1]
    rows = features // 4
    steps = rows // mb

    def lhs(i, m):
        return (0, m[first + i // steps] * steps + i % steps)

    return call(
        wgrad_kernel,
        meta,
        (normed, ds),
        (2 * steps,),
        [
            pl.BlockSpec((tokens, mb), lhs),
            pl.BlockSpec((tokens, width), lambda i, m: (0, 0)),
        ],
        [
            pl.BlockSpec((mb, width), lambda i, m: (jnp.minimum(i, steps - 1), 0)),
            pl.BlockSpec((mb, width), lambda i, m: (jnp.maximum(i - steps, 0), 0)),
        ],
        [struct((rows, width), BF16)] * 2,
        cost=cost(4 * tokens * rows * width, 2 * tokens * (features // 2 + width), weight=COVER),
    )


def back_kernel(meta, ds1_ref, ds2_ref, *refs):
    out_ref, W = refs[-2:]
    chunk = ds1_ref.shape[1]

    @pl.when(pl.program_id(1) == 0)
    def _():
        gather_units(meta, M_S1, refs[:6], W, 0)
        gather_units(meta, M_S2, refs[6:12], W, chunk)

    dims = (((1,), (1,)), ((), ()))
    value = lax.dot_general(ds1_ref[...], W[:, :chunk], dims, preferred_element_type=F32)
    value += lax.dot_general(ds2_ref[...], W[:, chunk:], dims, preferred_element_type=F32)
    out_ref[0] = value.astype(BF16)


def back(meta, ds1, ds2, units, first, count, tb=1024):
    tokens, width = ds1.shape
    features = units[0][0].shape[0]
    block = features // 4
    dspec = pl.BlockSpec((tb, width), lambda n, t, m: (t, 0))
    return call(
        back_kernel,
        meta,
        [ds1, ds2] + [array for array, _, _ in units],
        (count, tokens // tb),
        [dspec, dspec] + unit_specs(units, block, lambda n, t, m: m[first + n]),
        pl.BlockSpec((1, tb, block), lambda n, t, m: (n, t, 0)),
        struct((count, tokens, block), BF16),
        scratch=[pltpu.VMEM((block, 2 * width), BF16)],
        cost=cost(4 * count * tokens * block * width, 4 * count * tokens * width, weight=COVER),
    )


def unit_of(x_ref, mu_ref, inv_ref):
    repeat = x_ref.shape[1] // LANES
    mu = jnp.concatenate([mu_ref[...]] * repeat, axis=1)
    inv = jnp.concatenate([inv_ref[...]] * repeat, axis=1)
    return (x_ref[...].astype(F32) - mu) * inv, inv


def lane_sums(value):
    part = value[:, :LANES]
    for g in range(1, value.shape[1] // LANES):
        part = part + value[:, g * LANES : (g + 1) * LANES]
    return jnp.sum(part.T, axis=0, keepdims=True)


def tail_sums_kernel(meta, k_ref, rc_ref, r1_ref, r2_ref, x_ref, mu_ref, inv_ref, gain_ref, dn_ref, row_ref, col_ref):
    unit, _ = unit_of(x_ref, mu_ref, inv_ref)
    early = pl.program_id(0) < pl.num_programs(0) // 2
    far = jnp.where(early, r1_ref[...].astype(F32), r2_ref[...].astype(F32))
    dn = k_ref[0].astype(F32) + rc_ref[0].astype(F32) + far
    dn_ref[...] = dn
    gu = dn * gain_ref[...]
    row_ref[0:1, :] = lane_sums(gu)
    row_ref[1:2, :] = lane_sums(gu * unit)
    row_ref[2:8, :] = jnp.zeros((6, row_ref.shape[1]), F32)

    @pl.when(pl.program_id(0) == 0)
    def _():
        col_ref[...] = jnp.zeros_like(col_ref)

    col_ref[0:1, :] += jnp.sum(dn * unit, axis=0, keepdims=True)
    col_ref[1:2, :] += jnp.sum(dn, axis=0, keepdims=True)


def tail_sums(meta, keep, got, far, x, mu, inv, gain, tb=512):
    tokens, channels = x.shape
    half = tokens // tb // 2
    wide = pl.BlockSpec((tb, channels), lambda t, m: (t, 0))
    stat = pl.BlockSpec((tb, LANES), lambda t, m: (t, 0))
    return call(
        tail_sums_kernel,
        meta,
        (keep, got, *far, x, mu, inv, gain[None]),
        (tokens // tb,),
        [
            pl.BlockSpec((1, tb, channels), lambda t, m: (0, t, 0)),
            pl.BlockSpec((1, tb, channels), lambda t, m: (1, t, 0)),
            pl.BlockSpec((tb, channels), lambda t, m: (jnp.minimum(t, half - 1), 0)),
            pl.BlockSpec((tb, channels), lambda t, m: (jnp.maximum(t - half, 0), 0)),
            wide,
            stat,
            stat,
            pl.BlockSpec((1, channels), lambda t, m: (0, m[M_GATE])),
        ],
        [
            wide,
            pl.BlockSpec((8, tb), lambda t, m: (0, t)),
            pl.BlockSpec((8, channels), lambda t, m: (0, 0)),
        ],
        [struct((tokens, channels), F32), struct((8, tokens), F32), struct((8, channels), F32)],
        cost=cost(20 * tokens * channels, 12 * tokens * channels),
    )


def tail_kernel(features, meta, dn_ref, row_ref, x_ref, mu_ref, inv_ref, gain_ref, direct_ref, out_ref, PM):
    @pl.when(pl.program_id(0) == 0)
    def _():
        PM[...] = order_matrix()

    unit, inv = unit_of(x_ref, mu_ref, inv_ref)
    repeat = x_ref.shape[1] // LANES
    tb = x_ref.shape[0]

    def mean(n):
        row = row_ref[n : n + 1, :] * (1.0 / features)
        return jnp.concatenate([jnp.broadcast_to(row, (LANES, tb)).T] * repeat, axis=1)

    gu = dn_ref[...] * gain_ref[...]
    value = (inv * (gu - mean(0) - unit * mean(1)) + direct_ref[...].astype(F32)).astype(BF16)
    for q in range(tb // TILE):
        at = slice(q * TILE, (q + 1) * TILE)
        out_ref[at, :] = to_tokens(PM[...], value[at]).astype(BF16)


def tail(meta, dn, rows, x, mu, inv, gain, direct, features, tb=512):
    tokens, channels = dn.shape
    wide = pl.BlockSpec((tb, channels), lambda t, m: (t, 0))
    stat = pl.BlockSpec((tb, LANES), lambda t, m: (t, 0))
    return call(
        functools.partial(tail_kernel, features),
        meta,
        (dn, rows, x, mu, inv, gain[None], direct),
        (tokens // tb,),
        [
            wide,
            pl.BlockSpec((rows.shape[0], tb), lambda t, m: (0, t)),
            wide,
            stat,
            stat,
            pl.BlockSpec((1, channels), lambda t, m: (0, m[M_GATE])),
            wide,
        ],
        wide,
        struct((tokens, channels), BF16),
        scratch=[pltpu.VMEM((TILE, TILE), BF16)],
        cost=cost(10 * tokens * channels, 12 * tokens * channels),
    )


def halve_kernel(meta, *refs):
    ins, (away_ref, stay_ref) = refs[:-2], refs[-2:]
    for n, out_ref in ((0, away_ref), (1, stay_ref)):
        part = ins[n * len(ins) // 2 : (n + 1) * len(ins) // 2]
        if len(part) == 4:
            for o in range(2):
                out_ref[o] = (part[o][...].astype(F32) + part[2 + o][...].astype(F32)).astype(BF16)
        else:
            out_ref[...] = (part[0][...].astype(F32) + part[1][...].astype(F32)).astype(BF16)


def halve(meta, at, kept, got, parts=2):
    if len(kept) == 2:
        rows, width = kept[0].shape
        lead = ()
    else:
        lead, rows, width = kept[0].shape
        lead = (lead,)
    half = rows // 2
    tb = half // parts
    zeros = (0,) * len(lead)
    specs, args = [], []
    for side in range(2):
        for array in (*kept, *got):
            specs.append(
                pl.BlockSpec((*lead, tb, width), lambda i, m, side=side: (*zeros, (m[at] ^ (1 - side)) * parts + i, 0))
            )
            args.append(array)
    out = pl.BlockSpec((2, tb, width), lambda i, m: (0, i, 0))
    return call(
        halve_kernel,
        meta,
        args,
        (parts,),
        specs,
        [out, out],
        [struct((2, half, width), BF16)] * 2,
        cost=cost(4 * rows * width, 12 * rows * width),
    )


def split_kernel(late, half, meta, a_ref, b_ref, near_ref, far_ref):
    core = meta[M_CORE]
    h = meta[half]
    pair_ref, single_ref = (far_ref, near_ref) if late else (near_ref, far_ref)

    def take(owner, stream, block):
        col = pl.ds(pl.multiple_of((block * 3 + stream) * LANES, LANES), LANES)
        return (a_ref[owner, :, col].astype(F32) + b_ref[owner, :, col].astype(F32)).astype(BF16)

    for store in range(2):
        k = core ^ store
        for owner in range(2):
            for block in range(2):
                at = (2 * owner + block) * LANES
                pair_ref[store, :, at : at + LANES] = take(owner, k + h, block)
            single_ref[store, :, owner * LANES : (owner + 1) * LANES] = take(owner, 2 * (1 - h), k)


def split(meta, half, late, kept, got):
    _, rows, width = kept.shape
    pair, single = 4 * LANES, 2 * LANES
    widths = (single, pair) if late else (pair, single)
    whole = pl.BlockSpec((2, rows, width), lambda i, m: (0, 0, 0))
    return call(
        functools.partial(split_kernel, late, half),
        meta,
        (kept, got),
        (1,),
        [whole] * 2,
        [pl.BlockSpec((2, rows, w), lambda i, m: (0, 0, 0)) for w in widths],
        [struct((2, rows, w), BF16) for w in widths],
        cost=cost(2 * rows * width, 12 * rows * width),
    )


def join_kernel(meta, a_ref, b_ref, *outs):
    rows = a_ref.shape[1]
    for n, out_ref in enumerate(outs):
        out_ref[:rows, :] = a_ref[n]
        out_ref[rows:, :] = b_ref[n]


def join(meta, a, b):
    _, rows, width = a.shape
    whole = pl.BlockSpec((2, rows, width), lambda i, m: (0, 0, 0))
    out = pl.BlockSpec((2 * rows, width), lambda i, m: (0, 0))
    return call(
        join_kernel,
        meta,
        (a, b),
        (1,),
        [whole] * 2,
        [out] * 2,
        [struct((2 * rows, width), BF16)] * 2,
        cost=cost(0, 16 * rows * width),
    )


def place_kernel(blocks, meta, *refs):
    out_ref = refs[-1]
    step = pl.program_id(0)
    piece = out_ref.shape[1] // 4
    unit = piece // 3
    rows = out_ref.shape[0] // blocks
    core = meta[M_CORE]
    for stream in range(2):
        for part in range(2):

            @pl.when(step == stream * 2 + part)
            def _(stream=stream, part=part):
                one = refs[stream * 2 + part]
                two = refs[4 + stream * 2 + part]
                inner = meta[M_RHO + stream] % blocks

                def put(owner, single, src, col):
                    base = meta[M_OWN + (owner ^ stream)] * piece
                    wide = unit if single else 2 * unit
                    at = base + (jnp.where(core == 0, 2 * unit, 0) if single else core * unit)
                    at = pl.ds(pl.multiple_of(at, LANES), wide)
                    for j in range(blocks):
                        to = pl.ds(pl.multiple_of((inner ^ j) * rows, rows), rows)
                        out_ref[to, at] = src[j * rows : (j + 1) * rows, col : col + wide].astype(F32)

                put(0, False, one, 0)
                put(1, False, one, 2 * unit)
                put(2, True, one, 4 * unit)
                put(3, True, one, 5 * unit)
                put(0, True, two, 0)
                put(1, True, two, unit)
                put(2, False, two, 2 * unit)
                put(3, False, two, 4 * unit)


def place(meta, parts1, parts2, n_dp, features, columns):
    blocks = n_dp // 2
    whole = pl.BlockSpec((features // 4, columns // 2), lambda i, m: (0, 0))

    def where_to(i, m):
        stream = i // 2
        return ((m[M_CORE] ^ stream) * 2 + (i % 2 ^ m[M_RHO + stream] // blocks), 0)

    return call(
        functools.partial(place_kernel, blocks),
        meta,
        (*parts1, *parts2),
        (4,),
        [whole] * 8,
        pl.BlockSpec((features // 4, columns), where_to),
        struct((features, columns), F32),
        cost=cost(features * columns, 6 * features * columns),
    )


M_GATE, M_CORE, M_H1, M_H2 = 0, 1, 2, 3
M_S1, M_S2 = 4, 7
M_SEND, M_KEEP = 10, 12
M_OUT, M_IN = 14, 16
M_OWN, M_RHO = 18, 22
M_TO2, M_TO3, M_NEAR, M_LATE2, M_LATE3 = 24, 25, 26, 27, 28
M_PAIR, M_SINGLE, M_GOT_PAIR, M_GOT_SINGLE = 29, 30, 31, 32
M_BIT = 33


def shards(
    n_dp,
    n_gate,
    inputs,
    weight,
    ln_gain,
    ln_bias,
    forget_peep,
    reset_peep,
    forget_bias,
    reset_bias,
    resets,
    padding,
    grad_out,
):
    rows, tokens, features = inputs.shape
    assert rows == 1 and n_gate == 4
    channels = forget_peep.shape[0]
    assert channels == 4 * LANES
    bits = n_dp.bit_length() - 1
    assert 1 << bits == n_dp
    gate = lax.axis_index("gate")
    dp = lax.axis_index("dp")
    hi, core = gate // 2, gate % 2
    other = 1 - core

    orders = [list(range(bits)), [1, 0, *range(2, bits)]]

    def bit(stream, step):
        return (dp >> jnp.where(stream == 0, orders[0][step], orders[1][step])) & 1

    def rho(stream):
        value = 0
        for step in range(bits):
            value = value * 2 + bit(stream, step)
        return value

    def streams(h):
        return [core + h, other + h, 2 * (1 - h)]

    h1, h2 = hi, 1 - hi
    far = (1 - hi) * 2
    single, pair = 2 * other, core
    meta = jnp.stack(
        [gate, core, h1, h2, *streams(h1), *streams(h2)]
        + [other * 2 + 1 - bit(other, 0), core * 2 + 1 - bit(core, 0)]
        + [other * 2 + bit(other, 0), core * 2 + bit(core, 0)]
        + [far + other, hi * 2 + other, far + core, hi * 2 + core]
        + [gate, hi * 2 + other, far + core, far + other]
        + [rho(core), rho(other)]
        + [(far + core) * 3 + single, (far + other) * 3 + single, (hi * 2 + other) * 3]
        + [(far + core) * 3 + pair, (far + other) * 3 + pair]
        + [gate * 3 + pair, gate * 3 + single, other, 2 * core]
        + [bit(core, step) for step in range(bits)]
    ).astype(jnp.int32)

    def over_gate(value, delta):
        return lax.ppermute(value, "gate", [(g, g ^ delta) for g in range(n_gate)])

    def over_dp(value, step):
        pairs = [
            (d * n_gate + g, (d ^ (1 << orders[g % 2][step])) * n_gate + g) for d in range(n_dp) for g in range(n_gate)
        ]
        return lax.ppermute(value, ("dp", "gate"), pairs)

    def after(value, *others):
        return lax.optimization_barrier((value, *others))[0]

    x = inputs.reshape(tokens, features)
    grad = grad_out.reshape(tokens, channels)
    params = jnp.concatenate(
        [jnp.stack([forget_peep, reset_peep, forget_bias, reset_bias]), jnp.zeros((4, channels), F32)]
    )

    to2, to3, near = cut(meta, weight, [(M_TO2, 1), (M_TO3, 1), (M_NEAR, 3)])
    sent2, sent3, near = over_gate(to2, 2), over_gate(to3, 3), over_gate(near, 1)
    normed, mu, inv, own_x, keep, live = norm(
        after(meta, to2, to3), x, ln_gain, ln_bias, resets, padding, channels
    )
    away2, away3 = cut(after(meta, normed), weight, [(M_LATE2, 2), (M_LATE3, 2)])
    late2, late3 = over_gate(away2, 2), over_gate(away3, 3)
    units1 = [(weight, M_PAIR, 0), (weight, M_PAIR, 1), (near, M_GOT_PAIR, 0), (near, M_GOT_PAIR, 1)]
    units1 += [(sent2, None, 0), (sent3, None, 0)]
    units2 = [(late2, None, 0), (late2, None, 1), (late3, None, 0), (late3, None, 1)]
    units2 += [(weight, M_SINGLE, 0), (near, M_GOT_SINGLE, 0)]
    units = units1 + units2

    def first_sends(meta, ds):
        theirs, mine = wgrad(meta, normed, ds, M_SEND)
        return mine, [over_dp(mine, 0), over_dp(over_gate(theirs, 1), 0)]

    def first_keeps(meta, ds):
        theirs, mine = wgrad(meta, normed, ds, M_KEEP)
        return [mine, over_gate(theirs, 1)]

    def gathered(meta, half, late, kept, got):
        near, far = split(meta, half, late, kept, got)
        return near, over_gate(far, 2)

    def last_steps(shard, *others):
        for step in reversed(range(2, bits)):
            shard = jnp.concatenate([after(shard, *others), over_dp(shard, step)], axis=1)
        return shard

    u1 = project(after(meta, away2, away3), M_S1, normed, units1)
    hidden, ds1, direct, vecs = scan(meta, M_H1, u1, own_x, grad, keep, live, params, None)
    mine1, got1 = first_sends(meta, ds1)
    kept1 = first_keeps(after(meta, mine1), ds1)
    u2 = project(after(meta, kept1[0]), M_S2, normed, units2)
    away1, stay1 = halve(after(meta, u2), M_BIT + 1, kept1, got1)
    step1 = over_dp(away1, 1)
    hidden, ds2, direct, vecs = scan(
        after(meta, away1), M_H2, u2, own_x, grad, keep, live, params, (hidden, direct, vecs)
    )
    for step in range(2, bits):
        away1, stay1 = halve(after(meta, ds2), M_BIT + step, [stay1], [step1])
        step1 = over_dp(away1, step)
    mine2, got2 = first_sends(after(meta, away1), ds2)
    kept2 = first_keeps(after(meta, mine2), ds2)
    send = back(after(meta, kept2[0]), ds1, ds2, units, M_OUT, 2)
    got = over_gate(send, 1)
    near1, far1 = gathered(after(meta, send), M_H1, False, stay1, step1)
    away2, stay2 = halve(after(meta, near1), M_BIT + 1, kept2, got2)
    step2 = over_dp(away2, 1)
    shard1 = jnp.concatenate([near1, far1], axis=2)

    def last_doubling(meta, shard):
        mine, theirs = join(meta, shard, over_dp(shard, 1))
        moved = over_dp(theirs, 0)
        return [mine, over_dp(mine, 0), over_gate(theirs, 1), over_gate(moved, 1)]

    kept_far = back(after(meta, away2, shard1), ds1, ds2, units, M_IN, 1)
    half = tokens // 2
    far_send = [(kept_far[0, at : at + half].astype(F32) + got[0, at : at + half].astype(F32)).astype(BF16) for at in (0, half)]
    far_part = [over_gate(part, 2) for part in far_send]
    kept = back(after(meta, *far_send), ds1, ds2, units, M_IN + 1, 1)
    shard1 = last_steps(shard1, kept)
    for step in range(2, bits):
        away2, stay2 = halve(after(meta, shard1, kept), M_BIT + step, [stay2], [step2])
        step2 = over_dp(away2, step)
    near2, far2 = gathered(after(meta, far_part[0]), M_H2, True, stay2, step2)
    parts1 = last_doubling(after(meta, near2), shard1)
    shard2 = last_steps(jnp.concatenate([near2, far2], axis=2))
    parts2 = last_doubling(meta, shard2)

    dn, row_sums, col_sums = tail_sums(meta, kept, got, far_part, own_x, mu, inv, ln_gain)
    for delta in (1, 2):
        row_sums = row_sums + over_gate(row_sums, delta)
    dinputs = tail(meta, dn, row_sums, own_x, mu, inv, ln_gain, direct, features)

    totals = jnp.concatenate([col_sums[:2], vecs[:4]], axis=0)
    for step in range(bits):
        totals = totals + lax.ppermute(totals, "dp", [(d, d ^ (1 << step)) for d in range(n_dp)])

    grad_weight = place(meta, parts1, parts2, n_dp, features, weight.shape[1])
    return (
        hidden.reshape(rows, tokens, channels),
        dinputs.reshape(rows, tokens, channels),
        grad_weight,
        totals[0],
        totals[1],
        totals[2],
        totals[3],
        totals[4],
        totals[5],
    )


def solution(mesh):
    return jax.shard_map(
        functools.partial(shards, mesh.shape["dp"], mesh.shape["gate"]),
        mesh=mesh,
        in_specs=(
            P("dp", None, None),
            P(None, "gate"),
            P(),
            P(),
            P("gate"),
            P("gate"),
            P("gate"),
            P("gate"),
            P("dp", None),
            P("dp", None),
            P("dp", None, "gate"),
        ),
        out_specs=(
            P("dp", None, "gate"),
            P("dp", None, "gate"),
            P(None, "gate"),
            P("gate"),
            P("gate"),
            P("gate"),
            P("gate"),
            P("gate"),
            P("gate"),
        ),
        check_vma=False,
    )
```

```python
import functools

import jax
import jax.numpy as jnp
from jax import lax
from jax.experimental import pallas as pl
from jax.experimental.pallas import tpu as pltpu
from jax.sharding import PartitionSpec as P

epsilon = 1e-05
F32 = jnp.float32
BF16 = jnp.bfloat16
LANES = 128
VMEM_LIMIT = 60 * 1024 * 1024
COVER = 20
FIRST = 2


def call(kernel, meta, args, grid, in_specs, out_specs, out_shape, scratch=(), aliases=None, cost=None):
    return pl.pallas_call(
        kernel,
        grid_spec=pltpu.PrefetchScalarGridSpec(
            num_scalar_prefetch=1,
            grid=grid,
            in_specs=in_specs,
            out_specs=out_specs,
            scratch_shapes=list(scratch),
        ),
        out_shape=out_shape,
        input_output_aliases=aliases or {},
        compiler_params=pltpu.CompilerParams(
            dimension_semantics=("arbitrary",) * len(grid), vmem_limit_bytes=VMEM_LIMIT
        ),
        cost_estimate=cost,
    )(meta, *args)


def cost(flops, nbytes, trans=0, weight=1):
    return pl.CostEstimate(flops=int(weight * flops), bytes_accessed=int(weight * nbytes), transcendentals=int(trans))


def struct(shape, dtype):
    return jax.ShapeDtypeStruct(shape, dtype)


TILE = 256


def order_matrix():
    row = lax.broadcasted_iota(jnp.int32, (TILE, TILE), 0)
    token = lax.broadcasted_iota(jnp.int32, (TILE, TILE), 1)
    return jnp.where(token == (row % 8) * (TILE // 8) + row // 8, 1.0, 0.0).astype(BF16)


def to_rows(order, value):
    return jnp.dot(order, value, preferred_element_type=F32)


def to_tokens(order, value):
    return lax.dot_general(order, value, (((0,), (0,)), ((), ())), preferred_element_type=F32)


def norm_kernel(
    meta, x_ref, gain_ref, bias_ref, res_ref, pad_ref, out_ref, mu_ref, inv_ref, own_ref, keep_ref, live_ref, PM, XP, S1, S2
):
    @pl.when(pl.program_id(0) == 0)
    def _():
        PM[...] = order_matrix()

    order = PM[...]
    features = x_ref.shape[1]
    groups = features // LANES
    wide = 2 * LANES
    ones = jnp.ones((TILE, LANES), BF16)
    keep_ref[...] = jnp.dot(order * (1 - res_ref[0]).astype(F32).astype(BF16), ones, preferred_element_type=F32)
    live_ref[...] = jnp.dot(order * pad_ref[0].astype(F32).astype(BF16), ones, preferred_element_type=F32)
    shift = None
    first = second = None
    for g in range(0, features, wide):
        value = to_rows(order, x_ref[:, g : g + wide])
        XP[:, g : g + wide] = value
        if shift is None:
            shift = jnp.broadcast_to(value[:, 0:1], (TILE, LANES))
            S1[...] = shift
        one, two = value[:, :LANES] - shift, value[:, LANES:] - shift
        first = one + two if first is None else first + (one + two)
        squares = one * one + two * two
        second = squares if second is None else second + squares
    drift = jnp.sum(first, axis=1, keepdims=True) * (1.0 / features)
    spread = jnp.sum(second, axis=1, keepdims=True) * (1.0 / features) - drift * drift
    mu_ref[...] = shift + drift
    inv_ref[...] = jnp.broadcast_to(lax.rsqrt(jnp.maximum(spread, 0.0) + epsilon), inv_ref.shape)
    tall = 16

    def scaled(i, carry):
        rows = pl.ds(pl.multiple_of(i * tall, tall), tall)
        mean = mu_ref[rows, :]
        scale = inv_ref[rows, :]
        for g in range(groups):
            at = slice(g * LANES, (g + 1) * LANES)
            value = (XP[rows, at] - mean) * scale * gain_ref[0:1, at] + bias_ref[0:1, at]
            out_ref[rows, at] = value.astype(BF16)
        return carry

    lax.fori_loop(0, TILE // tall, scaled, 0, unroll=2)
    channels = own_ref.shape[1]
    own_ref[...] = XP[:, pl.ds(pl.multiple_of(meta[M_GATE] * channels, channels), channels)].astype(BF16)


def norm(meta, x, gain, bias, resets, padding, channels):
    tokens, features = x.shape
    tiles = tokens // TILE
    row = pl.BlockSpec((TILE, features), lambda t, m: (t, 0))
    whole = pl.BlockSpec((1, features), lambda t, m: (0, 0))
    flag = pl.BlockSpec((1, 1, TILE), lambda t, m: (t, 0, 0))
    stat = pl.BlockSpec((TILE, LANES), lambda t, m: (t, 0))
    stats = struct((tokens, LANES), F32)
    return call(
        norm_kernel,
        meta,
        (x, gain[None], bias[None], resets.reshape(tiles, 1, TILE), padding.reshape(tiles, 1, TILE)),
        (tiles,),
        [row, whole, whole, flag, flag],
        [row, stat, stat, pl.BlockSpec((TILE, channels), lambda t, m: (t, 0)), stat, stat],
        [struct(x.shape, BF16), stats, stats, struct((tokens, channels), BF16), stats, stats],
        scratch=[pltpu.VMEM((TILE, TILE), BF16), pltpu.VMEM((TILE, features), F32)] + [pltpu.VMEM((TILE, LANES), F32)] * 2,
        cost=cost(8 * tokens * features, 4 * tokens * features, weight=COVER),
    )


def column_of(meta, table, plane, block):
    blk = block ^ meta[M_CORE] if plane == 2 else block
    return pl.multiple_of((blk * 3 + meta[table + plane]) * LANES, LANES)


def cut_kernel(widths, meta, *refs):
    for n, width in enumerate(widths):
        out_ref = refs[sum(widths) + n]
        for b in range(width):
            out_ref[:, b * LANES : (b + 1) * LANES] = refs[sum(widths[:n]) + b][...]


def cut(meta, weight, pieces, tb=512):
    rows = weight.shape[0]
    widths = [width for _, width in pieces]
    specs = [
        pl.BlockSpec((tb, LANES), lambda t, m, at=at, b=b: (t, m[at] + b)) for at, width in pieces for b in range(width)
    ]
    return call(
        functools.partial(cut_kernel, widths),
        meta,
        [weight] * len(specs),
        (rows // tb,),
        specs,
        [pl.BlockSpec((tb, width * LANES), lambda t, m: (t, 0)) for width in widths],
        [struct((rows, width * LANES), BF16) for width in widths],
        cost=cost(0, 4 * rows * LANES * sum(widths)),
    )


def unit_specs(units, rows, row_of):
    return [pl.BlockSpec((rows, LANES), lambda *i, at=at, b=b: (row_of(*i), (i[-1][at] if at else 0) + b)) for _, at, b in units]


def gather_units(meta, table, refs, W, base):
    for n, ref in enumerate(refs):
        at = pl.multiple_of(base + column_of(meta, table, n // 2, n % 2), LANES)
        W[:, pl.ds(at, LANES)] = ref[...]


def project_kernel(table, meta, normed_ref, *refs):
    out_ref, W = refs[-2:]

    @pl.when(pl.program_id(0) == 0)
    def _():
        gather_units(meta, table, refs[:6], W, 0)

    out_ref[...] = jnp.dot(normed_ref[...], W[...], preferred_element_type=F32).astype(BF16)


def project(meta, table, normed, units, tb=512):
    tokens, features = normed.shape
    columns = 6 * LANES
    return call(
        functools.partial(project_kernel, table),
        meta,
        [normed] + [array for array, _, _ in units],
        (tokens // tb,),
        [pl.BlockSpec((tb, features), lambda t, m: (t, 0))] + unit_specs(units, features, lambda t, m: 0),
        pl.BlockSpec((tb, columns), lambda t, m: (t, 0)),
        struct((tokens, columns), BF16),
        scratch=[pltpu.VMEM((features, columns), BF16)],
        cost=cost(2 * tokens * features * columns, 2 * tokens * (features + 2 * columns), weight=COVER),
    )


def sigmoid(z):
    return 0.5 * jnp.tanh(0.5 * z) + 0.5


def scan_kernel(meta, u_ref, x_ref, g_ref, keep_ref, live_ref, prm_ref, *refs):
    (hid_ref, ds_ref, direct_ref, vec_ref, PM, A, B, FG, R, PV, GL, XF, UT, HP, CE, PE, CI, EI) = refs[-18:]
    length = x_ref.shape[0]
    tiles = length // TILE
    seg = TILE // 8
    rows_in = 64
    each = TILE // rows_in
    groups = rows_in // 8
    pf, pr, bf, br = (jnp.broadcast_to(prm_ref[i : i + 1, :], (rows_in, LANES)) for i in range(4))

    @pl.when(pl.program_id(0) == 0)
    def _():
        PM[...] = order_matrix()

    order = PM[...]
    for q in range(tiles):
        GL[q * TILE : (q + 1) * TILE, :] = to_rows(order, g_ref[q * TILE : (q + 1) * TILE, :])

    zeros = jnp.zeros((8, LANES), F32)
    ones = jnp.ones((8, LANES), F32)

    def rows_at(i):
        return pl.ds(pl.multiple_of(i * rows_in, rows_in), rows_in)

    def tile_at(i):
        return pl.ds(pl.multiple_of((i // each) * 8, 8), 8)

    def gates(i, carry):
        rows = rows_at(i)
        x = x_ref[rows, :].astype(F32)
        ut = u_ref[rows, 0:LANES].astype(F32)
        forget = sigmoid(u_ref[rows, LANES : 2 * LANES].astype(F32) + pf * x + bf)
        reset = sigmoid(u_ref[rows, 2 * LANES :].astype(F32) + pr * x + br)
        a = forget * keep_ref[rows, :]
        b = (1.0 - forget) * ut
        gl = GL[rows, :] * live_ref[rows, :]
        d = gl * reset
        XF[rows, :] = x
        UT[rows, :] = ut
        FG[rows, :] = forget
        R[rows, :] = reset
        A[rows, :] = a
        B[rows, :] = b
        GL[rows, :] = gl
        fresh = i % each == 0
        c, p, e = (jnp.where(fresh, start, old) for start, old in zip((zeros, ones, zeros), carry))
        for j in range(groups):
            at = slice(8 * j, 8 * j + 8)
            c = a[at] * c + b[at]
            p = a[at] * p
            e = e + p * d[at]
        CE[tile_at(i), :] = c
        PE[tile_at(i), :] = p
        EI[tile_at(i), :] = e
        return (c, p, e)

    lax.fori_loop(0, tiles * each, gates, (zeros, ones, zeros))

    count = 8 * tiles
    c = jnp.zeros((1, LANES), F32)
    e = jnp.zeros((1, LANES), F32)
    for j in range(count):
        CI[j : j + 1, :] = c
        c = CE[j : j + 1, :] + PE[j : j + 1, :] * c
        r = count - 1 - j
        own = EI[r : r + 1, :]
        EI[r : r + 1, :] = e
        e = own + PE[r : r + 1, :] * e

    def forward(i, carry):
        out = []
        for q in range(tiles):
            rows = pl.ds(pl.multiple_of(q * TILE + i * 8, 8), 8)
            PV[rows, :] = carry[q]
            out.append(A[rows, :] * carry[q] + B[rows, :])
        return tuple(out)

    lax.fori_loop(0, seg, forward, tuple(CI[8 * q : 8 * q + 8, :] for q in range(tiles)), unroll=4)

    def fold(v):
        return v.reshape(groups, 8, LANES).sum(axis=0)

    def grads(n, carry):
        i = tiles * each - 1 - n
        rows = rows_at(i)
        e, s0, s1, s2, s3 = carry
        e = jnp.where(n % each == 0, EI[tile_at(i), :], e)
        g = GL[rows, :]
        reset = R[rows, :]
        a = A[rows, :]
        d = g * reset
        dcs = [None] * groups
        for j in reversed(range(groups)):
            at = slice(8 * j, 8 * j + 8)
            dcs[j] = d[at] + e
            e = a[at] * dcs[j]
        dc = jnp.concatenate(dcs, axis=0)
        x = XF[rows, :]
        forget = FG[rows, :]
        prev = PV[rows, :]
        gap = a * prev + B[rows, :] - x
        HP[rows, :] = (live_ref[rows, :] * (x + reset * gap)).astype(BF16)
        rest = 1.0 - reset
        dreset = g * gap * (reset * rest)
        dtilde = dc * (1.0 - forget)
        dforget = dtilde * forget * (prev * keep_ref[rows, :] - UT[rows, :])
        ds_ref[rows, 0:LANES] = dtilde.astype(BF16)
        ds_ref[rows, LANES : 2 * LANES] = dforget.astype(BF16)
        ds_ref[rows, 2 * LANES :] = dreset.astype(BF16)
        direct_ref[rows, :] = (g * rest + dforget * pf + dreset * pr).astype(BF16)
        return (e, s0 + fold(dforget * x), s1 + fold(dreset * x), s2 + fold(dforget), s3 + fold(dreset))

    sums = lax.fori_loop(0, tiles * each, grads, (zeros,) * 5)[1:]
    for n, s in enumerate(sums):
        vec_ref[n : n + 1, :] = jnp.sum(s, axis=0, keepdims=True)
    vec_ref[4:8, :] = jnp.zeros((4, LANES), F32)
    for q in range(tiles):
        at = slice(q * TILE, (q + 1) * TILE)
        hid_ref[at, :] = to_tokens(order, HP[at, :]).astype(BF16)


def scan(meta, half, u, x, grad, keep, live, params, earlier):
    length, channels = x.shape
    blocks = u.shape[1] // (3 * LANES)
    col = lambda k, m: (0, m[half] * blocks + k)
    tall = (length, LANES)
    chunk = pl.BlockSpec((length, 3 * LANES), lambda k, m: (0, k))
    fixed = pl.BlockSpec(tall, lambda k, m: (0, 0))
    own = pl.BlockSpec(tall, col)
    small = pl.BlockSpec((8, LANES), col)
    in_specs = [chunk, own, own, fixed, fixed, small]
    args = [u, x, grad, keep, live, params]
    aliases = None
    if earlier is not None:
        aliases = {len(args) + 1: 0, len(args) + 2: 2, len(args) + 3: 3}
        args += list(earlier)
        in_specs += [pl.BlockSpec(memory_space=pl.ANY)] * 3
    ends = pltpu.VMEM((8 * length // TILE, LANES), F32)
    return call(
        scan_kernel,
        meta,
        args,
        (blocks,),
        in_specs,
        [own, chunk, own, small],
        [
            struct((length, channels), BF16),
            struct(u.shape, BF16),
            struct((length, channels), BF16),
            struct((8, channels), F32),
        ],
        scratch=[pltpu.VMEM((TILE, TILE), BF16)]
        + [pltpu.VMEM(tall, F32)] * 8
        + [pltpu.VMEM(tall, BF16)]
        + [ends] * 4,
        aliases=aliases,
        cost=cost(60 * length * channels // 2, 9 * length * channels, length * channels, weight=COVER),
    )


def wgrad_kernel(meta, normed_ref, ds_ref, a_ref, b_ref):
    first = pl.program_id(0) < pl.num_programs(0) // 2
    dims = (((0,), (0,)), ((), ()))

    @pl.when(first)
    def _():
        a_ref[...] = lax.dot_general(normed_ref[...], ds_ref[...], dims, preferred_element_type=F32).astype(BF16)

    @pl.when(jnp.logical_not(first))
    def _():
        b_ref[...] = lax.dot_general(normed_ref[...], ds_ref[...], dims, preferred_element_type=F32).astype(BF16)


def wgrad(meta, normed, ds, first, mb=512):
    tokens, features = normed.shape
    width = ds.shape[1]
    rows = features // 4
    steps = rows // mb

    def lhs(i, m):
        return (0, m[first + i // steps] * steps + i % steps)

    return call(
        wgrad_kernel,
        meta,
        (normed, ds),
        (2 * steps,),
        [
            pl.BlockSpec((tokens, mb), lhs),
            pl.BlockSpec((tokens, width), lambda i, m: (0, 0)),
        ],
        [
            pl.BlockSpec((mb, width), lambda i, m: (jnp.minimum(i, steps - 1), 0)),
            pl.BlockSpec((mb, width), lambda i, m: (jnp.maximum(i - steps, 0), 0)),
        ],
        [struct((rows, width), BF16)] * 2,
        cost=cost(4 * tokens * rows * width, 2 * tokens * (features // 2 + width), weight=COVER),
    )


def back_kernel(meta, ds1_ref, ds2_ref, *refs):
    outs, W = refs[-3:-1], refs[-1]
    chunk = ds1_ref.shape[1]

    @pl.when(pl.program_id(1) == 0)
    def _():
        gather_units(meta, M_S1, refs[:6], W, 0)
        gather_units(meta, M_S2, refs[6:12], W, chunk)

    dims = (((1,), (1,)), ((), ()))
    for n, out_ref in enumerate(outs):

        @pl.when(pl.program_id(0) == n)
        def _(out_ref=out_ref):
            value = lax.dot_general(ds1_ref[...], W[:, :chunk], dims, preferred_element_type=F32)
            value += lax.dot_general(ds2_ref[...], W[:, chunk:], dims, preferred_element_type=F32)
            out_ref[...] = value.astype(BF16)


def back(meta, ds1, ds2, units, first, tb=1024):
    tokens, width = ds1.shape
    features = units[0][0].shape[0]
    block = features // 4
    steps = tokens // tb
    dspec = pl.BlockSpec((tb, width), lambda n, t, m: (t, 0))
    return call(
        back_kernel,
        meta,
        [ds1, ds2] + [array for array, _, _ in units],
        (2, steps),
        [dspec, dspec] + unit_specs(units, block, lambda n, t, m: m[first + n]),
        [
            pl.BlockSpec((tb, block), lambda n, t, m: (jnp.where(n == 0, t, steps - 1), 0)),
            pl.BlockSpec((tb, block), lambda n, t, m: (jnp.where(n == 0, 0, t), 0)),
        ],
        [struct((tokens, block), BF16)] * 2,
        scratch=[pltpu.VMEM((block, 2 * width), BF16)],
        cost=cost(8 * tokens * block * width, 8 * tokens * width, weight=COVER),
    )


def unit_of(x_ref, mu_ref, inv_ref):
    repeat = x_ref.shape[1] // LANES
    mu = jnp.concatenate([mu_ref[...]] * repeat, axis=1)
    inv = jnp.concatenate([inv_ref[...]] * repeat, axis=1)
    return (x_ref[...].astype(F32) - mu) * inv, inv


def lane_sums(value):
    part = value[:, :LANES]
    for g in range(1, value.shape[1] // LANES):
        part = part + value[:, g * LANES : (g + 1) * LANES]
    return jnp.sum(part.T, axis=0, keepdims=True)


def tail_sums_kernel(meta, k_ref, rc_ref, r1_ref, r2_ref, x_ref, mu_ref, inv_ref, gain_ref, dn_ref, row_ref, col_ref):
    unit, _ = unit_of(x_ref, mu_ref, inv_ref)
    early = pl.program_id(0) < pl.num_programs(0) * FIRST // 4
    far = jnp.where(early, r1_ref[...].astype(F32), r2_ref[...].astype(F32))
    dn = k_ref[...].astype(F32) + rc_ref[...].astype(F32) + far
    dn_ref[...] = dn
    gu = dn * gain_ref[...]
    row_ref[0:1, :] = lane_sums(gu)
    row_ref[1:2, :] = lane_sums(gu * unit)
    row_ref[2:8, :] = jnp.zeros((6, row_ref.shape[1]), F32)

    @pl.when(pl.program_id(0) == 0)
    def _():
        col_ref[...] = jnp.zeros_like(col_ref)

    col_ref[0:1, :] += jnp.sum(dn * unit, axis=0, keepdims=True)
    col_ref[1:2, :] += jnp.sum(dn, axis=0, keepdims=True)


def tail_sums(meta, keep, got, far, x, mu, inv, gain, tb=512):
    tokens, channels = x.shape
    first = tokens // tb * FIRST // 4
    wide = pl.BlockSpec((tb, channels), lambda t, m: (t, 0))
    stat = pl.BlockSpec((tb, LANES), lambda t, m: (t, 0))
    return call(
        tail_sums_kernel,
        meta,
        (keep, got, *far, x, mu, inv, gain[None]),
        (tokens // tb,),
        [
            wide,
            wide,
            pl.BlockSpec((tb, channels), lambda t, m: (jnp.minimum(t, first - 1), 0)),
            pl.BlockSpec((tb, channels), lambda t, m: (jnp.maximum(t - first, 0), 0)),
            wide,
            stat,
            stat,
            pl.BlockSpec((1, channels), lambda t, m: (0, m[M_GATE])),
        ],
        [
            wide,
            pl.BlockSpec((8, tb), lambda t, m: (0, t)),
            pl.BlockSpec((8, channels), lambda t, m: (0, 0)),
        ],
        [struct((tokens, channels), F32), struct((8, tokens), F32), struct((8, channels), F32)],
        cost=cost(20 * tokens * channels, 12 * tokens * channels),
    )


def tail_kernel(features, meta, dn_ref, row_ref, x_ref, mu_ref, inv_ref, gain_ref, direct_ref, out_ref, PM):
    @pl.when(pl.program_id(0) == 0)
    def _():
        PM[...] = order_matrix()

    unit, inv = unit_of(x_ref, mu_ref, inv_ref)
    repeat = x_ref.shape[1] // LANES
    tb = x_ref.shape[0]

    def mean(n):
        row = row_ref[n : n + 1, :] * (1.0 / features)
        return jnp.concatenate([jnp.broadcast_to(row, (LANES, tb)).T] * repeat, axis=1)

    gu = dn_ref[...] * gain_ref[...]
    value = (inv * (gu - mean(0) - unit * mean(1)) + direct_ref[...].astype(F32)).astype(BF16)
    for q in range(tb // TILE):
        at = slice(q * TILE, (q + 1) * TILE)
        out_ref[at, :] = to_tokens(PM[...], value[at]).astype(BF16)


def tail(meta, dn, rows, x, mu, inv, gain, direct, features, tb=512):
    tokens, channels = dn.shape
    wide = pl.BlockSpec((tb, channels), lambda t, m: (t, 0))
    stat = pl.BlockSpec((tb, LANES), lambda t, m: (t, 0))
    return call(
        functools.partial(tail_kernel, features),
        meta,
        (dn, rows, x, mu, inv, gain[None], direct),
        (tokens // tb,),
        [
            wide,
            pl.BlockSpec((rows.shape[0], tb), lambda t, m: (0, t)),
            wide,
            stat,
            stat,
            pl.BlockSpec((1, channels), lambda t, m: (0, m[M_GATE])),
            wide,
        ],
        wide,
        struct((tokens, channels), BF16),
        scratch=[pltpu.VMEM((TILE, TILE), BF16)],
        cost=cost(10 * tokens * channels, 12 * tokens * channels),
    )


def halve_kernel(meta, *refs):
    ins, (away_ref, stay_ref) = refs[:-2], refs[-2:]
    for n, out_ref in ((0, away_ref), (1, stay_ref)):
        part = ins[n * len(ins) // 2 : (n + 1) * len(ins) // 2]
        if len(part) == 4:
            for o in range(2):
                out_ref[o] = (part[o][...].astype(F32) + part[2 + o][...].astype(F32)).astype(BF16)
        else:
            out_ref[...] = (part[0][...].astype(F32) + part[1][...].astype(F32)).astype(BF16)


def halve(meta, at, kept, got, parts=2):
    if len(kept) == 2:
        rows, width = kept[0].shape
        lead = ()
    else:
        lead, rows, width = kept[0].shape
        lead = (lead,)
    half = rows // 2
    tb = half // parts
    zeros = (0,) * len(lead)
    specs, args = [], []
    for side in range(2):
        for array in (*kept, *got):
            specs.append(
                pl.BlockSpec((*lead, tb, width), lambda i, m, side=side: (*zeros, (m[at] ^ (1 - side)) * parts + i, 0))
            )
            args.append(array)
    out = pl.BlockSpec((2, tb, width), lambda i, m: (0, i, 0))
    return call(
        halve_kernel,
        meta,
        args,
        (parts,),
        specs,
        [out, out],
        [struct((2, half, width), BF16)] * 2,
        cost=cost(4 * rows * width, 12 * rows * width),
    )


def split_kernel(late, half, meta, a_ref, b_ref, near_ref, far_ref):
    core = meta[M_CORE]
    h = meta[half]
    pair_ref, single_ref = (far_ref, near_ref) if late else (near_ref, far_ref)

    def take(owner, stream, block):
        col = pl.ds(pl.multiple_of((block * 3 + stream) * LANES, LANES), LANES)
        return (a_ref[owner, :, col].astype(F32) + b_ref[owner, :, col].astype(F32)).astype(BF16)

    for store in range(2):
        k = core ^ store
        for owner in range(2):
            for block in range(2):
                at = (2 * owner + block) * LANES
                pair_ref[store, :, at : at + LANES] = take(owner, k + h, block)
            single_ref[store, :, owner * LANES : (owner + 1) * LANES] = take(owner, 2 * (1 - h), k)


def split(meta, half, late, kept, got):
    _, rows, width = kept.shape
    pair, single = 4 * LANES, 2 * LANES
    widths = (single, pair) if late else (pair, single)
    whole = pl.BlockSpec((2, rows, width), lambda i, m: (0, 0, 0))
    return call(
        functools.partial(split_kernel, late, half),
        meta,
        (kept, got),
        (1,),
        [whole] * 2,
        [pl.BlockSpec((2, rows, w), lambda i, m: (0, 0, 0)) for w in widths],
        [struct((2, rows, w), BF16) for w in widths],
        cost=cost(2 * rows * width, 12 * rows * width),
    )


def join_kernel(meta, a_ref, b_ref, *outs):
    rows = a_ref.shape[1]
    for n, out_ref in enumerate(outs):
        out_ref[:rows, :] = a_ref[n]
        out_ref[rows:, :] = b_ref[n]


def join(meta, a, b):
    _, rows, width = a.shape
    whole = pl.BlockSpec((2, rows, width), lambda i, m: (0, 0, 0))
    out = pl.BlockSpec((2 * rows, width), lambda i, m: (0, 0))
    return call(
        join_kernel,
        meta,
        (a, b),
        (1,),
        [whole] * 2,
        [out] * 2,
        [struct((2 * rows, width), BF16)] * 2,
        cost=cost(0, 16 * rows * width),
    )


def place_kernel(blocks, meta, *refs):
    out_ref = refs[-1]
    step = pl.program_id(0)
    piece = out_ref.shape[1] // 4
    unit = piece // 3
    rows = out_ref.shape[0] // blocks
    core = meta[M_CORE]
    for stream in range(2):
        for part in range(2):

            @pl.when(step == stream * 2 + part)
            def _(stream=stream, part=part):
                one = refs[stream * 2 + part]
                two = refs[4 + stream * 2 + part]
                inner = meta[M_RHO + stream] % blocks

                def put(owner, single, src, col):
                    base = meta[M_OWN + (owner ^ stream)] * piece
                    wide = unit if single else 2 * unit
                    at = base + (jnp.where(core == 0, 2 * unit, 0) if single else core * unit)
                    at = pl.ds(pl.multiple_of(at, LANES), wide)
                    for j in range(blocks):
                        to = pl.ds(pl.multiple_of((inner ^ j) * rows, rows), rows)
                        out_ref[to, at] = src[j * rows : (j + 1) * rows, col : col + wide].astype(F32)

                put(0, False, one, 0)
                put(1, False, one, 2 * unit)
                put(2, True, one, 4 * unit)
                put(3, True, one, 5 * unit)
                put(0, True, two, 0)
                put(1, True, two, unit)
                put(2, False, two, 2 * unit)
                put(3, False, two, 4 * unit)


def place(meta, parts1, parts2, n_dp, features, columns):
    blocks = n_dp // 2
    whole = pl.BlockSpec((features // 4, columns // 2), lambda i, m: (0, 0))

    def where_to(i, m):
        stream = i // 2
        return ((m[M_CORE] ^ stream) * 2 + (i % 2 ^ m[M_RHO + stream] // blocks), 0)

    return call(
        functools.partial(place_kernel, blocks),
        meta,
        (*parts1, *parts2),
        (4,),
        [whole] * 8,
        pl.BlockSpec((features // 4, columns), where_to),
        struct((features, columns), F32),
        cost=cost(features * columns, 6 * features * columns),
    )


M_GATE, M_CORE, M_H1, M_H2 = 0, 1, 2, 3
M_S1, M_S2 = 4, 7
M_SEND, M_KEEP = 10, 12
M_FAR, M_HERE = 14, 16
M_OWN, M_RHO = 18, 22
M_TO2, M_TO3, M_NEAR, M_LATE2, M_LATE3 = 24, 25, 26, 27, 28
M_PAIR, M_SINGLE, M_GOT_PAIR, M_GOT_SINGLE = 29, 30, 31, 32
M_BIT = 33


def shards(
    n_dp,
    n_gate,
    inputs,
    weight,
    ln_gain,
    ln_bias,
    forget_peep,
    reset_peep,
    forget_bias,
    reset_bias,
    resets,
    padding,
    grad_out,
):
    rows, tokens, features = inputs.shape
    assert rows == 1 and n_gate == 4
    channels = forget_peep.shape[0]
    assert channels == 4 * LANES
    bits = n_dp.bit_length() - 1
    assert 1 << bits == n_dp
    gate = lax.axis_index("gate")
    dp = lax.axis_index("dp")
    hi, core = gate // 2, gate % 2
    other = 1 - core

    orders = [list(range(bits)), [1, 0, *range(2, bits)]]

    def bit(stream, step):
        return (dp >> jnp.where(stream == 0, orders[0][step], orders[1][step])) & 1

    def rho(stream):
        value = 0
        for step in range(bits):
            value = value * 2 + bit(stream, step)
        return value

    def streams(h):
        return [core + h, other + h, 2 * (1 - h)]

    h1, h2 = hi, 1 - hi
    far = (1 - hi) * 2
    single, pair = 2 * other, core
    meta = jnp.stack(
        [gate, core, h1, h2, *streams(h1), *streams(h2)]
        + [other * 2 + 1 - bit(other, 0), core * 2 + 1 - bit(core, 0)]
        + [other * 2 + bit(other, 0), core * 2 + bit(core, 0)]
        + [far + other, far + core, hi * 2 + other, hi * 2 + core]
        + [gate, hi * 2 + other, far + core, far + other]
        + [rho(core), rho(other)]
        + [(far + core) * 3 + single, (far + other) * 3 + single, (hi * 2 + other) * 3]
        + [(far + core) * 3 + pair, (far + other) * 3 + pair]
        + [gate * 3 + pair, gate * 3 + single, other, 2 * core]
        + [bit(core, step) for step in range(bits)]
    ).astype(jnp.int32)

    def over_gate(value, delta):
        return lax.ppermute(value, "gate", [(g, g ^ delta) for g in range(n_gate)])

    def over_dp(value, step):
        pairs = [
            (d * n_gate + g, (d ^ (1 << orders[g % 2][step])) * n_gate + g) for d in range(n_dp) for g in range(n_gate)
        ]
        return lax.ppermute(value, ("dp", "gate"), pairs)

    def after(value, *others):
        return lax.optimization_barrier((value, *others))[0]

    x = inputs.reshape(tokens, features)
    grad = grad_out.reshape(tokens, channels)
    params = jnp.concatenate(
        [jnp.stack([forget_peep, reset_peep, forget_bias, reset_bias]), jnp.zeros((4, channels), F32)]
    )

    to2, to3, near = cut(meta, weight, [(M_TO2, 1), (M_TO3, 1), (M_NEAR, 3)])
    sent2, sent3, near = over_gate(to2, 2), over_gate(to3, 3), over_gate(near, 1)
    normed, mu, inv, own_x, keep, live = norm(
        after(meta, to2, to3), x, ln_gain, ln_bias, resets, padding, channels
    )
    away2, away3 = cut(after(meta, normed), weight, [(M_LATE2, 2), (M_LATE3, 2)])
    late2, late3 = over_gate(away2, 2), over_gate(away3, 3)
    units1 = [(weight, M_PAIR, 0), (weight, M_PAIR, 1), (near, M_GOT_PAIR, 0), (near, M_GOT_PAIR, 1)]
    units1 += [(sent2, None, 0), (sent3, None, 0)]
    units2 = [(late2, None, 0), (late2, None, 1), (late3, None, 0), (late3, None, 1)]
    units2 += [(weight, M_SINGLE, 0), (near, M_GOT_SINGLE, 0)]
    units = units1 + units2

    def first_sends(meta, ds):
        theirs, mine = wgrad(meta, normed, ds, M_SEND)
        return mine, [over_dp(mine, 0), over_dp(over_gate(theirs, 1), 0)]

    def first_keeps(meta, ds):
        theirs, mine = wgrad(meta, normed, ds, M_KEEP)
        return [mine, over_gate(theirs, 1)]

    def gathered(meta, half, late, kept, got):
        near, far = split(meta, half, late, kept, got)
        return near, over_gate(far, 2)

    def last_steps(shard, *others):
        for step in reversed(range(2, bits)):
            shard = jnp.concatenate([after(shard, *others), over_dp(shard, step)], axis=1)
        return shard

    u1 = project(after(meta, away2, away3), M_S1, normed, units1)
    hidden, ds1, direct, vecs = scan(meta, M_H1, u1, own_x, grad, keep, live, params, None)
    mine1, got1 = first_sends(meta, ds1)
    kept1 = first_keeps(after(meta, mine1), ds1)
    u2 = project(after(meta, kept1[0]), M_S2, normed, units2)
    away1, stay1 = halve(after(meta, u2), M_BIT + 1, kept1, got1)
    step1 = over_dp(away1, 1)
    hidden, ds2, direct, vecs = scan(
        after(meta, away1), M_H2, u2, own_x, grad, keep, live, params, (hidden, direct, vecs)
    )
    for step in range(2, bits):
        away1, stay1 = halve(after(meta, ds2), M_BIT + step, [stay1], [step1])
        step1 = over_dp(away1, step)
    mine2, got2 = first_sends(after(meta, away1), ds2)
    kept2 = first_keeps(after(meta, mine2), ds2)
    far_theirs, far_mine = back(after(meta, kept2[0]), ds1, ds2, units, M_FAR)
    far_got = over_gate(far_theirs, 1)
    near1, far1 = gathered(after(meta, far_mine), M_H1, False, stay1, step1)
    away2, stay2 = halve(after(meta, near1), M_BIT + 1, kept2, got2)
    step2 = over_dp(away2, 1)
    shard1 = jnp.concatenate([near1, far1], axis=2)
    theirs, mine = back(after(meta, away2, shard1), ds1, ds2, units, M_HERE)
    cut_at = tokens * FIRST // 4
    far_send = [
        (far_mine[at].astype(F32) + far_got[at].astype(F32)).astype(BF16) for at in (slice(cut_at), slice(cut_at, None))
    ]
    far_part = [over_gate(part, 2) for part in far_send]
    shard1 = last_steps(shard1, mine)
    for step in range(2, bits):
        away2, stay2 = halve(after(meta, shard1, *far_send), M_BIT + step, [stay2], [step2])
        step2 = over_dp(away2, step)

    got = over_gate(after(theirs, away2), 1)

    def last_doubling(meta, shard):
        mine, theirs = join(meta, shard, over_dp(shard, 1))
        moved = over_dp(theirs, 0)
        return [mine, over_dp(mine, 0), over_gate(theirs, 1), over_gate(moved, 1)]

    near2, far2 = gathered(after(meta, shard1, far_part[0]), M_H2, True, stay2, step2)
    parts1 = last_doubling(after(meta, near2), shard1)
    dn, row_sums, col_sums = tail_sums(after(meta, parts1[0]), mine, got, far_part, own_x, mu, inv, ln_gain)
    shard2 = last_steps(jnp.concatenate([near2, far2], axis=2), dn)
    parts2 = last_doubling(meta, shard2)

    for delta in (1, 2):
        row_sums = row_sums + over_gate(row_sums, delta)
    dinputs = tail(after(meta, parts2[0]), dn, row_sums, own_x, mu, inv, ln_gain, direct, features)

    totals = jnp.concatenate([col_sums[:2], vecs[:4]], axis=0)
    for step in range(bits):
        totals = totals + lax.ppermute(totals, "dp", [(d, d ^ (1 << step)) for d in range(n_dp)])

    grad_weight = place(meta, parts1, parts2, n_dp, features, weight.shape[1])
    return (
        hidden.reshape(rows, tokens, channels),
        dinputs.reshape(rows, tokens, channels),
        grad_weight,
        totals[0],
        totals[1],
        totals[2],
        totals[3],
        totals[4],
        totals[5],
    )


def solution(mesh):
    return jax.shard_map(
        functools.partial(shards, mesh.shape["dp"], mesh.shape["gate"]),
        mesh=mesh,
        in_specs=(
            P("dp", None, None),
            P(None, "gate"),
            P(),
            P(),
            P("gate"),
            P("gate"),
            P("gate"),
            P("gate"),
            P("dp", None),
            P("dp", None),
            P("dp", None, "gate"),
        ),
        out_specs=(
            P("dp", None, "gate"),
            P("dp", None, "gate"),
            P(None, "gate"),
            P("gate"),
            P("gate"),
            P("gate"),
            P("gate"),
            P("gate"),
            P("gate"),
        ),
        check_vma=False,
    )
```

```python
import functools

import jax
import jax.numpy as jnp
from jax import lax
from jax.experimental import pallas as pl
from jax.experimental.pallas import tpu as pltpu
from jax.sharding import PartitionSpec as P

epsilon = 1e-05
F32 = jnp.float32
BF16 = jnp.bfloat16
LANES = 128
VMEM_LIMIT = 60 * 1024 * 1024
COVER = 20
FIRST = 2


def call(kernel, meta, args, grid, in_specs, out_specs, out_shape, scratch=(), aliases=None, cost=None):
    return pl.pallas_call(
        kernel,
        grid_spec=pltpu.PrefetchScalarGridSpec(
            num_scalar_prefetch=1,
            grid=grid,
            in_specs=in_specs,
            out_specs=out_specs,
            scratch_shapes=list(scratch),
        ),
        out_shape=out_shape,
        input_output_aliases=aliases or {},
        compiler_params=pltpu.CompilerParams(
            dimension_semantics=("arbitrary",) * len(grid), vmem_limit_bytes=VMEM_LIMIT
        ),
        cost_estimate=cost,
    )(meta, *args)


def cost(flops, nbytes, trans=0, weight=1):
    return pl.CostEstimate(flops=int(weight * flops), bytes_accessed=int(weight * nbytes), transcendentals=int(trans))


def struct(shape, dtype):
    return jax.ShapeDtypeStruct(shape, dtype)


TILE = 256


def order_matrix():
    row = lax.broadcasted_iota(jnp.int32, (TILE, TILE), 0)
    token = lax.broadcasted_iota(jnp.int32, (TILE, TILE), 1)
    return jnp.where(token == (row % 8) * (TILE // 8) + row // 8, 1.0, 0.0).astype(BF16)


def to_rows(order, value):
    return jnp.dot(order, value, preferred_element_type=F32)


def to_tokens(order, value):
    return lax.dot_general(order, value, (((0,), (0,)), ((), ())), preferred_element_type=F32)


def norm_kernel(
    meta, x_ref, gain_ref, bias_ref, res_ref, pad_ref, out_ref, mu_ref, inv_ref, own_ref, keep_ref, live_ref, PM, XP, S1, S2
):
    @pl.when(pl.program_id(0) == 0)
    def _():
        PM[...] = order_matrix()

    order = PM[...]
    features = x_ref.shape[1]
    groups = features // LANES
    wide = 2 * LANES
    ones = jnp.ones((TILE, LANES), BF16)
    keep_ref[...] = jnp.dot(order * (1 - res_ref[0]).astype(F32).astype(BF16), ones, preferred_element_type=F32)
    live_ref[...] = jnp.dot(order * pad_ref[0].astype(F32).astype(BF16), ones, preferred_element_type=F32)
    shift = None
    first = second = None
    for g in range(0, features, wide):
        value = to_rows(order, x_ref[:, g : g + wide])
        XP[:, g : g + wide] = value
        if shift is None:
            shift = jnp.broadcast_to(value[:, 0:1], (TILE, LANES))
            S1[...] = shift
        one, two = value[:, :LANES] - shift, value[:, LANES:] - shift
        first = one + two if first is None else first + (one + two)
        squares = one * one + two * two
        second = squares if second is None else second + squares
    drift = jnp.sum(first, axis=1, keepdims=True) * (1.0 / features)
    spread = jnp.sum(second, axis=1, keepdims=True) * (1.0 / features) - drift * drift
    mu_ref[...] = shift + drift
    inv_ref[...] = jnp.broadcast_to(lax.rsqrt(jnp.maximum(spread, 0.0) + epsilon), inv_ref.shape)
    tall = 16

    def scaled(i, carry):
        rows = pl.ds(pl.multiple_of(i * tall, tall), tall)
        mean = mu_ref[rows, :]
        scale = inv_ref[rows, :]
        for g in range(groups):
            at = slice(g * LANES, (g + 1) * LANES)
            value = (XP[rows, at] - mean) * scale * gain_ref[0:1, at] + bias_ref[0:1, at]
            out_ref[rows, at] = value.astype(BF16)
        return carry

    lax.fori_loop(0, TILE // tall, scaled, 0, unroll=2)
    channels = own_ref.shape[1]
    own_ref[...] = XP[:, pl.ds(pl.multiple_of(meta[M_GATE] * channels, channels), channels)].astype(BF16)


def norm(meta, x, gain, bias, resets, padding, channels):
    tokens, features = x.shape
    tiles = tokens // TILE
    row = pl.BlockSpec((TILE, features), lambda t, m: (t, 0))
    whole = pl.BlockSpec((1, features), lambda t, m: (0, 0))
    flag = pl.BlockSpec((1, 1, TILE), lambda t, m: (t, 0, 0))
    stat = pl.BlockSpec((TILE, LANES), lambda t, m: (t, 0))
    stats = struct((tokens, LANES), F32)
    return call(
        norm_kernel,
        meta,
        (x, gain[None], bias[None], resets.reshape(tiles, 1, TILE), padding.reshape(tiles, 1, TILE)),
        (tiles,),
        [row, whole, whole, flag, flag],
        [row, stat, stat, pl.BlockSpec((TILE, channels), lambda t, m: (t, 0)), stat, stat],
        [struct(x.shape, BF16), stats, stats, struct((tokens, channels), BF16), stats, stats],
        scratch=[pltpu.VMEM((TILE, TILE), BF16), pltpu.VMEM((TILE, features), F32)] + [pltpu.VMEM((TILE, LANES), F32)] * 2,
        cost=cost(8 * tokens * features, 4 * tokens * features, weight=COVER),
    )


def column_of(meta, table, plane, block):
    blk = block ^ meta[M_CORE] if plane == 2 else block
    return pl.multiple_of((blk * 3 + meta[table + plane]) * LANES, LANES)


def cut_kernel(widths, meta, *refs):
    for n, width in enumerate(widths):
        out_ref = refs[sum(widths) + n]
        for b in range(width):
            out_ref[:, b * LANES : (b + 1) * LANES] = refs[sum(widths[:n]) + b][...]


def cut(meta, weight, pieces, tb=512):
    rows = weight.shape[0]
    widths = [width for _, width in pieces]
    specs = [
        pl.BlockSpec((tb, LANES), lambda t, m, at=at, b=b: (t, m[at] + b)) for at, width in pieces for b in range(width)
    ]
    return call(
        functools.partial(cut_kernel, widths),
        meta,
        [weight] * len(specs),
        (rows // tb,),
        specs,
        [pl.BlockSpec((tb, width * LANES), lambda t, m: (t, 0)) for width in widths],
        [struct((rows, width * LANES), BF16) for width in widths],
        cost=cost(0, 4 * rows * LANES * sum(widths)),
    )


def unit_specs(units, rows, row_of):
    return [pl.BlockSpec((rows, LANES), lambda *i, at=at, b=b: (row_of(*i), (i[-1][at] if at else 0) + b)) for _, at, b in units]


def gather_units(meta, table, refs, W, base):
    for n, ref in enumerate(refs):
        at = pl.multiple_of(base + column_of(meta, table, n // 2, n % 2), LANES)
        W[:, pl.ds(at, LANES)] = ref[...]


def project_kernel(table, meta, normed_ref, *refs):
    out_ref, W = refs[-2:]

    @pl.when(pl.program_id(0) == 0)
    def _():
        gather_units(meta, table, refs[:6], W, 0)

    out_ref[...] = jnp.dot(normed_ref[...], W[...], preferred_element_type=F32).astype(BF16)


def project(meta, table, normed, units, tb=512):
    tokens, features = normed.shape
    columns = 6 * LANES
    return call(
        functools.partial(project_kernel, table),
        meta,
        [normed] + [array for array, _, _ in units],
        (tokens // tb,),
        [pl.BlockSpec((tb, features), lambda t, m: (t, 0))] + unit_specs(units, features, lambda t, m: 0),
        pl.BlockSpec((tb, columns), lambda t, m: (t, 0)),
        struct((tokens, columns), BF16),
        scratch=[pltpu.VMEM((features, columns), BF16)],
        cost=cost(2 * tokens * features * columns, 2 * tokens * (features + 2 * columns), weight=COVER),
    )


def sigmoid(z):
    return 0.5 * jnp.tanh(0.5 * z) + 0.5


def scan_kernel(meta, u_ref, x_ref, g_ref, keep_ref, live_ref, prm_ref, *refs):
    (hid_ref, ds_ref, direct_ref, vec_ref, PM, A, B, FG, R, PV, GL, XF, UT, HP, CE, PE, CI, EI) = refs[-18:]
    length = x_ref.shape[0]
    tiles = length // TILE
    seg = TILE // 8
    rows_in = 64
    each = TILE // rows_in
    groups = rows_in // 8
    pf, pr, bf, br = (jnp.broadcast_to(prm_ref[i : i + 1, :], (rows_in, LANES)) for i in range(4))

    @pl.when(pl.program_id(0) == 0)
    def _():
        PM[...] = order_matrix()

    order = PM[...]
    for q in range(tiles):
        GL[q * TILE : (q + 1) * TILE, :] = to_rows(order, g_ref[q * TILE : (q + 1) * TILE, :])

    zeros = jnp.zeros((8, LANES), F32)
    ones = jnp.ones((8, LANES), F32)

    def rows_at(i):
        return pl.ds(pl.multiple_of(i * rows_in, rows_in), rows_in)

    def tile_at(i):
        return pl.ds(pl.multiple_of((i // each) * 8, 8), 8)

    def gates(i, carry):
        rows = rows_at(i)
        x = x_ref[rows, :].astype(F32)
        ut = u_ref[rows, 0:LANES].astype(F32)
        forget = sigmoid(u_ref[rows, LANES : 2 * LANES].astype(F32) + pf * x + bf)
        reset = sigmoid(u_ref[rows, 2 * LANES :].astype(F32) + pr * x + br)
        a = forget * keep_ref[rows, :]
        b = (1.0 - forget) * ut
        gl = GL[rows, :] * live_ref[rows, :]
        d = gl * reset
        XF[rows, :] = x
        UT[rows, :] = ut
        FG[rows, :] = forget
        R[rows, :] = reset
        A[rows, :] = a
        B[rows, :] = b
        GL[rows, :] = gl
        fresh = i % each == 0
        c, p, e = (jnp.where(fresh, start, old) for start, old in zip((zeros, ones, zeros), carry))
        for j in range(groups):
            at = slice(8 * j, 8 * j + 8)
            c = a[at] * c + b[at]
            p = a[at] * p
            e = e + p * d[at]
        CE[tile_at(i), :] = c
        PE[tile_at(i), :] = p
        EI[tile_at(i), :] = e
        return (c, p, e)

    lax.fori_loop(0, tiles * each, gates, (zeros, ones, zeros))

    count = 8 * tiles
    c = jnp.zeros((1, LANES), F32)
    e = jnp.zeros((1, LANES), F32)
    for j in range(count):
        CI[j : j + 1, :] = c
        c = CE[j : j + 1, :] + PE[j : j + 1, :] * c
        r = count - 1 - j
        own = EI[r : r + 1, :]
        EI[r : r + 1, :] = e
        e = own + PE[r : r + 1, :] * e

    def forward(i, carry):
        out = []
        for q in range(tiles):
            rows = pl.ds(pl.multiple_of(q * TILE + i * 8, 8), 8)
            PV[rows, :] = carry[q]
            out.append(A[rows, :] * carry[q] + B[rows, :])
        return tuple(out)

    lax.fori_loop(0, seg, forward, tuple(CI[8 * q : 8 * q + 8, :] for q in range(tiles)), unroll=4)

    def fold(v):
        return v.reshape(groups, 8, LANES).sum(axis=0)

    def grads(n, carry):
        i = tiles * each - 1 - n
        rows = rows_at(i)
        e, s0, s1, s2, s3 = carry
        e = jnp.where(n % each == 0, EI[tile_at(i), :], e)
        g = GL[rows, :]
        reset = R[rows, :]
        a = A[rows, :]
        d = g * reset
        dcs = [None] * groups
        for j in reversed(range(groups)):
            at = slice(8 * j, 8 * j + 8)
            dcs[j] = d[at] + e
            e = a[at] * dcs[j]
        dc = jnp.concatenate(dcs, axis=0)
        x = XF[rows, :]
        forget = FG[rows, :]
        prev = PV[rows, :]
        gap = a * prev + B[rows, :] - x
        HP[rows, :] = (live_ref[rows, :] * (x + reset * gap)).astype(BF16)
        rest = 1.0 - reset
        dreset = g * gap * (reset * rest)
        dtilde = dc * (1.0 - forget)
        dforget = dtilde * forget * (prev * keep_ref[rows, :] - UT[rows, :])
        ds_ref[rows, 0:LANES] = dtilde.astype(BF16)
        ds_ref[rows, LANES : 2 * LANES] = dforget.astype(BF16)
        ds_ref[rows, 2 * LANES :] = dreset.astype(BF16)
        direct_ref[rows, :] = (g * rest + dforget * pf + dreset * pr).astype(BF16)
        return (e, s0 + fold(dforget * x), s1 + fold(dreset * x), s2 + fold(dforget), s3 + fold(dreset))

    sums = lax.fori_loop(0, tiles * each, grads, (zeros,) * 5)[1:]
    for n, s in enumerate(sums):
        vec_ref[n : n + 1, :] = jnp.sum(s, axis=0, keepdims=True)
    vec_ref[4:8, :] = jnp.zeros((4, LANES), F32)
    for q in range(tiles):
        at = slice(q * TILE, (q + 1) * TILE)
        hid_ref[at, :] = to_tokens(order, HP[at, :]).astype(BF16)


def scan(meta, half, u, x, grad, keep, live, params, earlier):
    length, channels = x.shape
    blocks = u.shape[1] // (3 * LANES)
    col = lambda k, m: (0, m[half] * blocks + k)
    tall = (length, LANES)
    chunk = pl.BlockSpec((length, 3 * LANES), lambda k, m: (0, k))
    fixed = pl.BlockSpec(tall, lambda k, m: (0, 0))
    own = pl.BlockSpec(tall, col)
    small = pl.BlockSpec((8, LANES), col)
    in_specs = [chunk, own, own, fixed, fixed, small]
    args = [u, x, grad, keep, live, params]
    aliases = None
    if earlier is not None:
        aliases = {len(args) + 1: 0, len(args) + 2: 2, len(args) + 3: 3}
        args += list(earlier)
        in_specs += [pl.BlockSpec(memory_space=pl.ANY)] * 3
    ends = pltpu.VMEM((8 * length // TILE, LANES), F32)
    return call(
        scan_kernel,
        meta,
        args,
        (blocks,),
        in_specs,
        [own, chunk, own, small],
        [
            struct((length, channels), BF16),
            struct(u.shape, BF16),
            struct((length, channels), BF16),
            struct((8, channels), F32),
        ],
        scratch=[pltpu.VMEM((TILE, TILE), BF16)]
        + [pltpu.VMEM(tall, F32)] * 8
        + [pltpu.VMEM(tall, BF16)]
        + [ends] * 4,
        aliases=aliases,
        cost=cost(60 * length * channels // 2, 9 * length * channels, length * channels, weight=COVER),
    )


def wgrad_kernel(meta, normed_ref, ds_ref, a_ref, b_ref):
    first = pl.program_id(0) < pl.num_programs(0) // 2
    dims = (((0,), (0,)), ((), ()))

    @pl.when(first)
    def _():
        a_ref[...] = lax.dot_general(normed_ref[...], ds_ref[...], dims, preferred_element_type=F32).astype(BF16)

    @pl.when(jnp.logical_not(first))
    def _():
        b_ref[...] = lax.dot_general(normed_ref[...], ds_ref[...], dims, preferred_element_type=F32).astype(BF16)


def wgrad(meta, normed, ds, first, mb=512):
    tokens, features = normed.shape
    width = ds.shape[1]
    rows = features // 4
    steps = rows // mb

    def lhs(i, m):
        return (0, m[first + i // steps] * steps + i % steps)

    return call(
        wgrad_kernel,
        meta,
        (normed, ds),
        (2 * steps,),
        [
            pl.BlockSpec((tokens, mb), lhs),
            pl.BlockSpec((tokens, width), lambda i, m: (0, 0)),
        ],
        [
            pl.BlockSpec((mb, width), lambda i, m: (jnp.minimum(i, steps - 1), 0)),
            pl.BlockSpec((mb, width), lambda i, m: (jnp.maximum(i - steps, 0), 0)),
        ],
        [struct((rows, width), BF16)] * 2,
        cost=cost(4 * tokens * rows * width, 2 * tokens * (features // 2 + width), weight=COVER),
    )


def back_kernel(meta, ds1_ref, ds2_ref, *refs):
    out_ref, W = refs[-2:]
    chunk = ds1_ref.shape[1]

    @pl.when(pl.program_id(0) == 0)
    def _():
        gather_units(meta, M_S1, refs[:6], W, 0)
        gather_units(meta, M_S2, refs[6:12], W, chunk)

    dims = (((1,), (1,)), ((), ()))
    value = lax.dot_general(ds1_ref[...], W[:, :chunk], dims, preferred_element_type=F32)
    value += lax.dot_general(ds2_ref[...], W[:, chunk:], dims, preferred_element_type=F32)
    out_ref[...] = value.astype(BF16)


def back(meta, ds1, ds2, units, at, tb=1024):
    tokens, width = ds1.shape
    features = units[0][0].shape[0]
    block = features // 4
    dspec = pl.BlockSpec((tb, width), lambda t, m: (t, 0))
    return call(
        back_kernel,
        meta,
        [ds1, ds2] + [array for array, _, _ in units],
        (tokens // tb,),
        [dspec, dspec] + unit_specs(units, block, lambda t, m: m[at]),
        pl.BlockSpec((tb, block), lambda t, m: (t, 0)),
        struct((tokens, block), BF16),
        scratch=[pltpu.VMEM((block, 2 * width), BF16)],
        cost=cost(4 * tokens * block * width, 4 * tokens * width, weight=COVER),
    )


def unit_of(x_ref, mu_ref, inv_ref):
    repeat = x_ref.shape[1] // LANES
    mu = jnp.concatenate([mu_ref[...]] * repeat, axis=1)
    inv = jnp.concatenate([inv_ref[...]] * repeat, axis=1)
    return (x_ref[...].astype(F32) - mu) * inv, inv


def lane_sums(value):
    part = value[:, :LANES]
    for g in range(1, value.shape[1] // LANES):
        part = part + value[:, g * LANES : (g + 1) * LANES]
    return jnp.sum(part.T, axis=0, keepdims=True)


def tail_sums_kernel(meta, k_ref, rc_ref, r1_ref, r2_ref, x_ref, mu_ref, inv_ref, gain_ref, dn_ref, row_ref, col_ref):
    unit, _ = unit_of(x_ref, mu_ref, inv_ref)
    early = pl.program_id(0) < pl.num_programs(0) * FIRST // 8
    far = jnp.where(early, r1_ref[...].astype(F32), r2_ref[...].astype(F32))
    dn = k_ref[...].astype(F32) + rc_ref[...].astype(F32) + far
    dn_ref[...] = dn
    gu = dn * gain_ref[...]
    row_ref[0:1, :] = lane_sums(gu)
    row_ref[1:2, :] = lane_sums(gu * unit)
    row_ref[2:8, :] = jnp.zeros((6, row_ref.shape[1]), F32)

    @pl.when(pl.program_id(0) == 0)
    def _():
        col_ref[...] = jnp.zeros_like(col_ref)

    col_ref[0:1, :] += jnp.sum(dn * unit, axis=0, keepdims=True)
    col_ref[1:2, :] += jnp.sum(dn, axis=0, keepdims=True)


def tail_sums(meta, keep, got, far, x, mu, inv, gain, tb=256):
    tokens, channels = x.shape
    first = tokens // tb * FIRST // 8
    wide = pl.BlockSpec((tb, channels), lambda t, m: (t, 0))
    stat = pl.BlockSpec((tb, LANES), lambda t, m: (t, 0))
    return call(
        tail_sums_kernel,
        meta,
        (keep, got, *far, x, mu, inv, gain[None]),
        (tokens // tb,),
        [
            wide,
            wide,
            pl.BlockSpec((tb, channels), lambda t, m: (jnp.minimum(t, first - 1), 0)),
            pl.BlockSpec((tb, channels), lambda t, m: (jnp.maximum(t - first, 0), 0)),
            wide,
            stat,
            stat,
            pl.BlockSpec((1, channels), lambda t, m: (0, m[M_GATE])),
        ],
        [
            wide,
            pl.BlockSpec((8, tb), lambda t, m: (0, t)),
            pl.BlockSpec((8, channels), lambda t, m: (0, 0)),
        ],
        [struct((tokens, channels), F32), struct((8, tokens), F32), struct((8, channels), F32)],
        cost=cost(20 * tokens * channels, 12 * tokens * channels),
    )


def tail_kernel(features, meta, dn_ref, row_ref, x_ref, mu_ref, inv_ref, gain_ref, direct_ref, out_ref, PM):
    @pl.when(pl.program_id(0) == 0)
    def _():
        PM[...] = order_matrix()

    unit, inv = unit_of(x_ref, mu_ref, inv_ref)
    repeat = x_ref.shape[1] // LANES
    tb = x_ref.shape[0]

    def mean(n):
        row = row_ref[n : n + 1, :] * (1.0 / features)
        return jnp.concatenate([jnp.broadcast_to(row, (LANES, tb)).T] * repeat, axis=1)

    gu = dn_ref[...] * gain_ref[...]
    value = (inv * (gu - mean(0) - unit * mean(1)) + direct_ref[...].astype(F32)).astype(BF16)
    for q in range(tb // TILE):
        at = slice(q * TILE, (q + 1) * TILE)
        out_ref[at, :] = to_tokens(PM[...], value[at]).astype(BF16)


def tail(meta, dn, rows, x, mu, inv, gain, direct, features, tb=512):
    tokens, channels = dn.shape
    wide = pl.BlockSpec((tb, channels), lambda t, m: (t, 0))
    stat = pl.BlockSpec((tb, LANES), lambda t, m: (t, 0))
    return call(
        functools.partial(tail_kernel, features),
        meta,
        (dn, rows, x, mu, inv, gain[None], direct),
        (tokens // tb,),
        [
            wide,
            pl.BlockSpec((rows.shape[0], tb), lambda t, m: (0, t)),
            wide,
            stat,
            stat,
            pl.BlockSpec((1, channels), lambda t, m: (0, m[M_GATE])),
            wide,
        ],
        wide,
        struct((tokens, channels), BF16),
        scratch=[pltpu.VMEM((TILE, TILE), BF16)],
        cost=cost(10 * tokens * channels, 12 * tokens * channels),
    )


def halve_kernel(meta, *refs):
    ins, (away_ref, stay_ref) = refs[:-2], refs[-2:]
    for n, out_ref in ((0, away_ref), (1, stay_ref)):
        part = ins[n * len(ins) // 2 : (n + 1) * len(ins) // 2]
        if len(part) == 4:
            for o in range(2):
                out_ref[o] = (part[o][...].astype(F32) + part[2 + o][...].astype(F32)).astype(BF16)
        else:
            out_ref[...] = (part[0][...].astype(F32) + part[1][...].astype(F32)).astype(BF16)


def halve(meta, at, kept, got, parts=2):
    if len(kept) == 2:
        rows, width = kept[0].shape
        lead = ()
    else:
        lead, rows, width = kept[0].shape
        lead = (lead,)
    half = rows // 2
    tb = half // parts
    zeros = (0,) * len(lead)
    specs, args = [], []
    for side in range(2):
        for array in (*kept, *got):
            specs.append(
                pl.BlockSpec((*lead, tb, width), lambda i, m, side=side: (*zeros, (m[at] ^ (1 - side)) * parts + i, 0))
            )
            args.append(array)
    out = pl.BlockSpec((2, tb, width), lambda i, m: (0, i, 0))
    return call(
        halve_kernel,
        meta,
        args,
        (parts,),
        specs,
        [out, out],
        [struct((2, half, width), BF16)] * 2,
        cost=cost(4 * rows * width, 12 * rows * width),
    )


def split_kernel(late, half, meta, a_ref, b_ref, near_ref, far_ref):
    core = meta[M_CORE]
    h = meta[half]
    pair_ref, single_ref = (far_ref, near_ref) if late else (near_ref, far_ref)

    def take(owner, stream, block):
        col = pl.ds(pl.multiple_of((block * 3 + stream) * LANES, LANES), LANES)
        return (a_ref[owner, :, col].astype(F32) + b_ref[owner, :, col].astype(F32)).astype(BF16)

    for store in range(2):
        k = core ^ store
        for owner in range(2):
            for block in range(2):
                at = (2 * owner + block) * LANES
                pair_ref[store, :, at : at + LANES] = take(owner, k + h, block)
            single_ref[store, :, owner * LANES : (owner + 1) * LANES] = take(owner, 2 * (1 - h), k)


def split(meta, half, late, kept, got):
    _, rows, width = kept.shape
    pair, single = 4 * LANES, 2 * LANES
    widths = (single, pair) if late else (pair, single)
    whole = pl.BlockSpec((2, rows, width), lambda i, m: (0, 0, 0))
    return call(
        functools.partial(split_kernel, late, half),
        meta,
        (kept, got),
        (1,),
        [whole] * 2,
        [pl.BlockSpec((2, rows, w), lambda i, m: (0, 0, 0)) for w in widths],
        [struct((2, rows, w), BF16) for w in widths],
        cost=cost(2 * rows * width, 12 * rows * width),
    )


def join_kernel(meta, a_ref, b_ref, *outs):
    rows = a_ref.shape[1]
    for n, out_ref in enumerate(outs):
        out_ref[:rows, :] = a_ref[n]
        out_ref[rows:, :] = b_ref[n]


def join(meta, a, b):
    _, rows, width = a.shape
    whole = pl.BlockSpec((2, rows, width), lambda i, m: (0, 0, 0))
    out = pl.BlockSpec((2 * rows, width), lambda i, m: (0, 0))
    return call(
        join_kernel,
        meta,
        (a, b),
        (1,),
        [whole] * 2,
        [out] * 2,
        [struct((2 * rows, width), BF16)] * 2,
        cost=cost(0, 16 * rows * width),
    )


def place_kernel(blocks, meta, *refs):
    out_ref = refs[-1]
    step = pl.program_id(0)
    piece = out_ref.shape[1] // 4
    unit = piece // 3
    rows = out_ref.shape[0] // blocks
    core = meta[M_CORE]
    for stream in range(2):
        for part in range(2):

            @pl.when(step == stream * 2 + part)
            def _(stream=stream, part=part):
                one = refs[stream * 2 + part]
                two = refs[4 + stream * 2 + part]
                inner = meta[M_RHO + stream] % blocks

                def put(owner, single, src, col):
                    base = meta[M_OWN + (owner ^ stream)] * piece
                    wide = unit if single else 2 * unit
                    at = base + (jnp.where(core == 0, 2 * unit, 0) if single else core * unit)
                    at = pl.ds(pl.multiple_of(at, LANES), wide)
                    for j in range(blocks):
                        to = pl.ds(pl.multiple_of((inner ^ j) * rows, rows), rows)
                        out_ref[to, at] = src[j * rows : (j + 1) * rows, col : col + wide].astype(F32)

                put(0, False, one, 0)
                put(1, False, one, 2 * unit)
                put(2, True, one, 4 * unit)
                put(3, True, one, 5 * unit)
                put(0, True, two, 0)
                put(1, True, two, unit)
                put(2, False, two, 2 * unit)
                put(3, False, two, 4 * unit)


def place(meta, parts1, parts2, n_dp, features, columns):
    blocks = n_dp // 2
    whole = pl.BlockSpec((features // 4, columns // 2), lambda i, m: (0, 0))

    def where_to(i, m):
        stream = i // 2
        return ((m[M_CORE] ^ stream) * 2 + (i % 2 ^ m[M_RHO + stream] // blocks), 0)

    return call(
        functools.partial(place_kernel, blocks),
        meta,
        (*parts1, *parts2),
        (4,),
        [whole] * 8,
        pl.BlockSpec((features // 4, columns), where_to),
        struct((features, columns), F32),
        cost=cost(features * columns, 6 * features * columns),
    )


M_GATE, M_CORE, M_H1, M_H2 = 0, 1, 2, 3
M_S1, M_S2 = 4, 7
M_SEND, M_KEEP = 10, 12
M_FAR, M_HERE = 14, 16
M_OWN, M_RHO = 18, 22
M_TO2, M_TO3, M_NEAR, M_LATE2, M_LATE3 = 24, 25, 26, 27, 28
M_PAIR, M_SINGLE, M_GOT_PAIR, M_GOT_SINGLE = 29, 30, 31, 32
M_BIT = 33


def shards(
    n_dp,
    n_gate,
    inputs,
    weight,
    ln_gain,
    ln_bias,
    forget_peep,
    reset_peep,
    forget_bias,
    reset_bias,
    resets,
    padding,
    grad_out,
):
    rows, tokens, features = inputs.shape
    assert rows == 1 and n_gate == 4
    channels = forget_peep.shape[0]
    assert channels == 4 * LANES
    bits = n_dp.bit_length() - 1
    assert 1 << bits == n_dp
    gate = lax.axis_index("gate")
    dp = lax.axis_index("dp")
    hi, core = gate // 2, gate % 2
    other = 1 - core

    orders = [list(range(bits)), [1, 0, *range(2, bits)]]

    def bit(stream, step):
        return (dp >> jnp.where(stream == 0, orders[0][step], orders[1][step])) & 1

    def rho(stream):
        value = 0
        for step in range(bits):
            value = value * 2 + bit(stream, step)
        return value

    def streams(h):
        return [core + h, other + h, 2 * (1 - h)]

    h1, h2 = hi, 1 - hi
    far = (1 - hi) * 2
    single, pair = 2 * other, core
    meta = jnp.stack(
        [gate, core, h1, h2, *streams(h1), *streams(h2)]
        + [other * 2 + 1 - bit(other, 0), core * 2 + 1 - bit(core, 0)]
        + [other * 2 + bit(other, 0), core * 2 + bit(core, 0)]
        + [far + other, far + core, hi * 2 + other, hi * 2 + core]
        + [gate, hi * 2 + other, far + core, far + other]
        + [rho(core), rho(other)]
        + [(far + core) * 3 + single, (far + other) * 3 + single, (hi * 2 + other) * 3]
        + [(far + core) * 3 + pair, (far + other) * 3 + pair]
        + [gate * 3 + pair, gate * 3 + single, other, 2 * core]
        + [bit(core, step) for step in range(bits)]
    ).astype(jnp.int32)

    def over_gate(value, delta):
        return lax.ppermute(value, "gate", [(g, g ^ delta) for g in range(n_gate)])

    def over_dp(value, step):
        pairs = [
            (d * n_gate + g, (d ^ (1 << orders[g % 2][step])) * n_gate + g) for d in range(n_dp) for g in range(n_gate)
        ]
        return lax.ppermute(value, ("dp", "gate"), pairs)

    def after(value, *others):
        return lax.optimization_barrier((value, *others))[0]

    x = inputs.reshape(tokens, features)
    grad = grad_out.reshape(tokens, channels)
    params = jnp.concatenate(
        [jnp.stack([forget_peep, reset_peep, forget_bias, reset_bias]), jnp.zeros((4, channels), F32)]
    )

    to2, to3, near = cut(meta, weight, [(M_TO2, 1), (M_TO3, 1), (M_NEAR, 3)])
    sent2, sent3, near = over_gate(to2, 2), over_gate(to3, 3), over_gate(near, 1)
    normed, mu, inv, own_x, keep, live = norm(
        after(meta, to2, to3), x, ln_gain, ln_bias, resets, padding, channels
    )
    away2, away3 = cut(after(meta, normed), weight, [(M_LATE2, 2), (M_LATE3, 2)])
    late2, late3 = over_gate(away2, 2), over_gate(away3, 3)
    units1 = [(weight, M_PAIR, 0), (weight, M_PAIR, 1), (near, M_GOT_PAIR, 0), (near, M_GOT_PAIR, 1)]
    units1 += [(sent2, None, 0), (sent3, None, 0)]
    units2 = [(late2, None, 0), (late2, None, 1), (late3, None, 0), (late3, None, 1)]
    units2 += [(weight, M_SINGLE, 0), (near, M_GOT_SINGLE, 0)]
    units = units1 + units2

    def first_sends(meta, ds):
        theirs, mine = wgrad(meta, normed, ds, M_SEND)
        return mine, [over_dp(mine, 0), over_dp(over_gate(theirs, 1), 0)]

    def first_keeps(meta, ds):
        theirs, mine = wgrad(meta, normed, ds, M_KEEP)
        return [mine, over_gate(theirs, 1)]

    def gathered(meta, half, late, kept, got):
        near, far = split(meta, half, late, kept, got)
        return near, over_gate(far, 2)

    def last_steps(shard, *others):
        for step in reversed(range(2, bits)):
            shard = jnp.concatenate([after(shard, *others), over_dp(shard, step)], axis=1)
        return shard

    u1 = project(after(meta, away2, away3), M_S1, normed, units1)
    hidden, ds1, direct, vecs = scan(meta, M_H1, u1, own_x, grad, keep, live, params, None)
    mine1, got1 = first_sends(meta, ds1)
    kept1 = first_keeps(after(meta, mine1), ds1)
    u2 = project(after(meta, kept1[0]), M_S2, normed, units2)
    away1, stay1 = halve(after(meta, u2), M_BIT + 1, kept1, got1)
    step1 = over_dp(away1, 1)
    hidden, ds2, direct, vecs = scan(
        after(meta, away1), M_H2, u2, own_x, grad, keep, live, params, (hidden, direct, vecs)
    )
    for step in range(2, bits):
        away1, stay1 = halve(after(meta, ds2), M_BIT + step, [stay1], [step1])
        step1 = over_dp(away1, step)
    mine2, got2 = first_sends(after(meta, away1), ds2)
    kept2 = first_keeps(after(meta, mine2), ds2)
    far_theirs = back(after(meta, kept2[0]), ds1, ds2, units, M_FAR)
    far_got = over_gate(far_theirs, 1)
    away2, stay2 = halve(after(meta, far_theirs), M_BIT + 1, kept2, got2)
    step2 = over_dp(away2, 1)
    near1, far1 = gathered(after(meta, away2), M_H1, False, stay1, step1)
    far_mine = back(after(meta, near1), ds1, ds2, units, M_FAR + 1)
    for step in range(2, bits):
        away2, stay2 = halve(after(meta, far_mine), M_BIT + step, [stay2], [step2])
        step2 = over_dp(away2, step)
    far_mine = after(far_mine, away2)
    cut_at = tokens * FIRST // 8
    far_send = [
        (far_mine[at].astype(F32) + far_got[at].astype(F32)).astype(BF16) for at in (slice(cut_at), slice(cut_at, None))
    ]
    far_part = [over_gate(part, 2) for part in far_send]
    theirs = back(after(meta, away2, *far_send), ds1, ds2, units, M_HERE)
    got = over_gate(theirs, 1)
    shard1 = jnp.concatenate([after(near1, theirs), far1], axis=2)
    mine = back(after(meta, theirs, shard1), ds1, ds2, units, M_HERE + 1)

    def last_doubling(meta, shard):
        mine, theirs = join(meta, shard, over_dp(shard, 1))
        moved = over_dp(theirs, 0)
        return [mine, over_dp(mine, 0), over_gate(theirs, 1), over_gate(moved, 1)]

    near2, far2 = gathered(after(meta, mine, far_part[0]), M_H2, True, stay2, step2)
    shard1 = last_steps(shard1, near2)
    shard2 = last_steps(jnp.concatenate([after(near2, shard1), far2], axis=2))
    parts1 = last_doubling(after(meta, shard2), shard1)
    parts2 = last_doubling(after(meta, parts1[0]), shard2)
    dn, row_sums, col_sums = tail_sums(after(meta, parts2[0]), mine, got, far_part, own_x, mu, inv, ln_gain)
    for delta in (1, 2):
        row_sums = row_sums + over_gate(row_sums, delta)
    dinputs = tail(after(meta, parts2[0]), dn, row_sums, own_x, mu, inv, ln_gain, direct, features)

    totals = jnp.concatenate([col_sums[:2], vecs[:4]], axis=0)
    for step in range(bits):
        totals = totals + lax.ppermute(totals, "dp", [(d, d ^ (1 << step)) for d in range(n_dp)])

    grad_weight = place(meta, parts1, parts2, n_dp, features, weight.shape[1])
    return (
        hidden.reshape(rows, tokens, channels),
        dinputs.reshape(rows, tokens, channels),
        grad_weight,
        totals[0],
        totals[1],
        totals[2],
        totals[3],
        totals[4],
        totals[5],
    )


def solution(mesh):
    return jax.shard_map(
        functools.partial(shards, mesh.shape["dp"], mesh.shape["gate"]),
        mesh=mesh,
        in_specs=(
            P("dp", None, None),
            P(None, "gate"),
            P(),
            P(),
            P("gate"),
            P("gate"),
            P("gate"),
            P("gate"),
            P("dp", None),
            P("dp", None),
            P("dp", None, "gate"),
        ),
        out_specs=(
            P("dp", None, "gate"),
            P("dp", None, "gate"),
            P(None, "gate"),
            P("gate"),
            P("gate"),
            P("gate"),
            P("gate"),
            P("gate"),
            P("gate"),
        ),
        check_vma=False,
    )
```

```python
import functools

import jax
import jax.numpy as jnp
from jax import lax
from jax.experimental import pallas as pl
from jax.experimental.pallas import tpu as pltpu
from jax.sharding import PartitionSpec as P

epsilon = 1e-05
F32 = jnp.float32
BF16 = jnp.bfloat16
LANES = 128
VMEM_LIMIT = 60 * 1024 * 1024
COVER = 20
FIRST = 3


def call(kernel, meta, args, grid, in_specs, out_specs, out_shape, scratch=(), aliases=None, cost=None):
    return pl.pallas_call(
        kernel,
        grid_spec=pltpu.PrefetchScalarGridSpec(
            num_scalar_prefetch=1,
            grid=grid,
            in_specs=in_specs,
            out_specs=out_specs,
            scratch_shapes=list(scratch),
        ),
        out_shape=out_shape,
        input_output_aliases=aliases or {},
        compiler_params=pltpu.CompilerParams(
            dimension_semantics=("arbitrary",) * len(grid), vmem_limit_bytes=VMEM_LIMIT
        ),
        cost_estimate=cost,
    )(meta, *args)


def cost(flops, nbytes, trans=0, weight=1):
    return pl.CostEstimate(flops=int(weight * flops), bytes_accessed=int(weight * nbytes), transcendentals=int(trans))


def struct(shape, dtype):
    return jax.ShapeDtypeStruct(shape, dtype)


TILE = 256


def order_matrix():
    row = lax.broadcasted_iota(jnp.int32, (TILE, TILE), 0)
    token = lax.broadcasted_iota(jnp.int32, (TILE, TILE), 1)
    return jnp.where(token == (row % 8) * (TILE // 8) + row // 8, 1.0, 0.0).astype(BF16)


def to_rows(order, value):
    return jnp.dot(order, value, preferred_element_type=F32)


def to_tokens(order, value):
    return lax.dot_general(order, value, (((0,), (0,)), ((), ())), preferred_element_type=F32)


def norm_kernel(
    meta, x_ref, gain_ref, bias_ref, res_ref, pad_ref, out_ref, mu_ref, inv_ref, own_ref, keep_ref, live_ref, PM, XP, S1, S2
):
    @pl.when(pl.program_id(0) == 0)
    def _():
        PM[...] = order_matrix()

    order = PM[...]
    features = x_ref.shape[1]
    groups = features // LANES
    wide = 2 * LANES
    ones = jnp.ones((TILE, LANES), BF16)
    keep_ref[...] = jnp.dot(order * (1 - res_ref[0]).astype(F32).astype(BF16), ones, preferred_element_type=F32)
    live_ref[...] = jnp.dot(order * pad_ref[0].astype(F32).astype(BF16), ones, preferred_element_type=F32)
    shift = None
    first = second = None
    for g in range(0, features, wide):
        value = to_rows(order, x_ref[:, g : g + wide])
        XP[:, g : g + wide] = value
        if shift is None:
            shift = jnp.broadcast_to(value[:, 0:1], (TILE, LANES))
            S1[...] = shift
        one, two = value[:, :LANES] - shift, value[:, LANES:] - shift
        first = one + two if first is None else first + (one + two)
        squares = one * one + two * two
        second = squares if second is None else second + squares
    drift = jnp.sum(first, axis=1, keepdims=True) * (1.0 / features)
    spread = jnp.sum(second, axis=1, keepdims=True) * (1.0 / features) - drift * drift
    mu_ref[...] = shift + drift
    inv_ref[...] = jnp.broadcast_to(lax.rsqrt(jnp.maximum(spread, 0.0) + epsilon), inv_ref.shape)
    tall = 16

    def scaled(i, carry):
        rows = pl.ds(pl.multiple_of(i * tall, tall), tall)
        mean = mu_ref[rows, :]
        scale = inv_ref[rows, :]
        for g in range(groups):
            at = slice(g * LANES, (g + 1) * LANES)
            value = (XP[rows, at] - mean) * scale * gain_ref[0:1, at] + bias_ref[0:1, at]
            out_ref[rows, at] = value.astype(BF16)
        return carry

    lax.fori_loop(0, TILE // tall, scaled, 0, unroll=2)
    channels = own_ref.shape[1]
    own_ref[...] = XP[:, pl.ds(pl.multiple_of(meta[M_GATE] * channels, channels), channels)].astype(BF16)


def norm(meta, x, gain, bias, resets, padding, channels):
    tokens, features = x.shape
    tiles = tokens // TILE
    row = pl.BlockSpec((TILE, features), lambda t, m: (t, 0))
    whole = pl.BlockSpec((1, features), lambda t, m: (0, 0))
    flag = pl.BlockSpec((1, 1, TILE), lambda t, m: (t, 0, 0))
    stat = pl.BlockSpec((TILE, LANES), lambda t, m: (t, 0))
    stats = struct((tokens, LANES), F32)
    return call(
        norm_kernel,
        meta,
        (x, gain[None], bias[None], resets.reshape(tiles, 1, TILE), padding.reshape(tiles, 1, TILE)),
        (tiles,),
        [row, whole, whole, flag, flag],
        [row, stat, stat, pl.BlockSpec((TILE, channels), lambda t, m: (t, 0)), stat, stat],
        [struct(x.shape, BF16), stats, stats, struct((tokens, channels), BF16), stats, stats],
        scratch=[pltpu.VMEM((TILE, TILE), BF16), pltpu.VMEM((TILE, features), F32)] + [pltpu.VMEM((TILE, LANES), F32)] * 2,
        cost=cost(8 * tokens * features, 4 * tokens * features, weight=COVER),
    )


def column_of(meta, table, plane, block):
    blk = block ^ meta[M_CORE] if plane == 2 else block
    return pl.multiple_of((blk * 3 + meta[table + plane]) * LANES, LANES)


def cut_kernel(widths, meta, *refs):
    for n, width in enumerate(widths):
        out_ref = refs[sum(widths) + n]
        for b in range(width):
            out_ref[:, b * LANES : (b + 1) * LANES] = refs[sum(widths[:n]) + b][...]


def cut(meta, weight, pieces, tb=512):
    rows = weight.shape[0]
    widths = [width for _, width in pieces]
    specs = [
        pl.BlockSpec((tb, LANES), lambda t, m, at=at, b=b: (t, m[at] + b)) for at, width in pieces for b in range(width)
    ]
    return call(
        functools.partial(cut_kernel, widths),
        meta,
        [weight] * len(specs),
        (rows // tb,),
        specs,
        [pl.BlockSpec((tb, width * LANES), lambda t, m: (t, 0)) for width in widths],
        [struct((rows, width * LANES), BF16) for width in widths],
        cost=cost(0, 4 * rows * LANES * sum(widths)),
    )


def unit_specs(units, rows, row_of):
    return [pl.BlockSpec((rows, LANES), lambda *i, at=at, b=b: (row_of(*i), (i[-1][at] if at else 0) + b)) for _, at, b in units]


def gather_units(meta, table, refs, W, base):
    for n, ref in enumerate(refs):
        at = pl.multiple_of(base + column_of(meta, table, n // 2, n % 2), LANES)
        W[:, pl.ds(at, LANES)] = ref[...]


def project_kernel(table, meta, normed_ref, *refs):
    out_ref, W = refs[-2:]

    @pl.when(pl.program_id(0) == 0)
    def _():
        gather_units(meta, table, refs[:6], W, 0)

    out_ref[...] = jnp.dot(normed_ref[...], W[...], preferred_element_type=F32).astype(BF16)


def project(meta, table, normed, units, tb=512):
    tokens, features = normed.shape
    columns = 6 * LANES
    return call(
        functools.partial(project_kernel, table),
        meta,
        [normed] + [array for array, _, _ in units],
        (tokens // tb,),
        [pl.BlockSpec((tb, features), lambda t, m: (t, 0))] + unit_specs(units, features, lambda t, m: 0),
        pl.BlockSpec((tb, columns), lambda t, m: (t, 0)),
        struct((tokens, columns), BF16),
        scratch=[pltpu.VMEM((features, columns), BF16)],
        cost=cost(2 * tokens * features * columns, 2 * tokens * (features + 2 * columns), weight=COVER),
    )


def sigmoid(z):
    return 0.5 * jnp.tanh(0.5 * z) + 0.5


def scan_kernel(meta, u_ref, x_ref, g_ref, keep_ref, live_ref, prm_ref, *refs):
    (hid_ref, ds_ref, direct_ref, vec_ref, PM, A, B, FG, R, PV, GL, XF, UT, HP, CE, PE, CI, EI) = refs[-18:]
    length = x_ref.shape[0]
    tiles = length // TILE
    seg = TILE // 8
    rows_in = 64
    each = TILE // rows_in
    groups = rows_in // 8
    pf, pr, bf, br = (jnp.broadcast_to(prm_ref[i : i + 1, :], (rows_in, LANES)) for i in range(4))

    @pl.when(pl.program_id(0) == 0)
    def _():
        PM[...] = order_matrix()

    order = PM[...]
    for q in range(tiles):
        GL[q * TILE : (q + 1) * TILE, :] = to_rows(order, g_ref[q * TILE : (q + 1) * TILE, :])

    zeros = jnp.zeros((8, LANES), F32)
    ones = jnp.ones((8, LANES), F32)

    def rows_at(i):
        return pl.ds(pl.multiple_of(i * rows_in, rows_in), rows_in)

    def tile_at(i):
        return pl.ds(pl.multiple_of((i // each) * 8, 8), 8)

    def gates(i, carry):
        rows = rows_at(i)
        x = x_ref[rows, :].astype(F32)
        ut = u_ref[rows, 0:LANES].astype(F32)
        forget = sigmoid(u_ref[rows, LANES : 2 * LANES].astype(F32) + pf * x + bf)
        reset = sigmoid(u_ref[rows, 2 * LANES :].astype(F32) + pr * x + br)
        a = forget * keep_ref[rows, :]
        b = (1.0 - forget) * ut
        gl = GL[rows, :] * live_ref[rows, :]
        d = gl * reset
        XF[rows, :] = x
        UT[rows, :] = ut
        FG[rows, :] = forget
        R[rows, :] = reset
        A[rows, :] = a
        B[rows, :] = b
        GL[rows, :] = gl
        fresh = i % each == 0
        c, p, e = (jnp.where(fresh, start, old) for start, old in zip((zeros, ones, zeros), carry))
        for j in range(groups):
            at = slice(8 * j, 8 * j + 8)
            c = a[at] * c + b[at]
            p = a[at] * p
            e = e + p * d[at]
        CE[tile_at(i), :] = c
        PE[tile_at(i), :] = p
        EI[tile_at(i), :] = e
        return (c, p, e)

    lax.fori_loop(0, tiles * each, gates, (zeros, ones, zeros))

    count = 8 * tiles
    c = jnp.zeros((1, LANES), F32)
    e = jnp.zeros((1, LANES), F32)
    for j in range(count):
        CI[j : j + 1, :] = c
        c = CE[j : j + 1, :] + PE[j : j + 1, :] * c
        r = count - 1 - j
        own = EI[r : r + 1, :]
        EI[r : r + 1, :] = e
        e = own + PE[r : r + 1, :] * e

    def forward(i, carry):
        out = []
        for q in range(tiles):
            rows = pl.ds(pl.multiple_of(q * TILE + i * 8, 8), 8)
            PV[rows, :] = carry[q]
            out.append(A[rows, :] * carry[q] + B[rows, :])
        return tuple(out)

    lax.fori_loop(0, seg, forward, tuple(CI[8 * q : 8 * q + 8, :] for q in range(tiles)), unroll=4)

    def fold(v):
        return v.reshape(groups, 8, LANES).sum(axis=0)

    def grads(n, carry):
        i = tiles * each - 1 - n
        rows = rows_at(i)
        e, s0, s1, s2, s3 = carry
        e = jnp.where(n % each == 0, EI[tile_at(i), :], e)
        g = GL[rows, :]
        reset = R[rows, :]
        a = A[rows, :]
        d = g * reset
        dcs = [None] * groups
        for j in reversed(range(groups)):
            at = slice(8 * j, 8 * j + 8)
            dcs[j] = d[at] + e
            e = a[at] * dcs[j]
        dc = jnp.concatenate(dcs, axis=0)
        x = XF[rows, :]
        forget = FG[rows, :]
        prev = PV[rows, :]
        gap = a * prev + B[rows, :] - x
        HP[rows, :] = (live_ref[rows, :] * (x + reset * gap)).astype(BF16)
        rest = 1.0 - reset
        dreset = g * gap * (reset * rest)
        dtilde = dc * (1.0 - forget)
        dforget = dtilde * forget * (prev * keep_ref[rows, :] - UT[rows, :])
        ds_ref[rows, 0:LANES] = dtilde.astype(BF16)
        ds_ref[rows, LANES : 2 * LANES] = dforget.astype(BF16)
        ds_ref[rows, 2 * LANES :] = dreset.astype(BF16)
        direct_ref[rows, :] = (g * rest + dforget * pf + dreset * pr).astype(BF16)
        return (e, s0 + fold(dforget * x), s1 + fold(dreset * x), s2 + fold(dforget), s3 + fold(dreset))

    sums = lax.fori_loop(0, tiles * each, grads, (zeros,) * 5)[1:]
    for n, s in enumerate(sums):
        vec_ref[n : n + 1, :] = jnp.sum(s, axis=0, keepdims=True)
    vec_ref[4:8, :] = jnp.zeros((4, LANES), F32)
    for q in range(tiles):
        at = slice(q * TILE, (q + 1) * TILE)
        hid_ref[at, :] = to_tokens(order, HP[at, :]).astype(BF16)


def scan(meta, half, u, x, grad, keep, live, params, earlier):
    length, channels = x.shape
    blocks = u.shape[1] // (3 * LANES)
    col = lambda k, m: (0, m[half] * blocks + k)
    tall = (length, LANES)
    chunk = pl.BlockSpec((length, 3 * LANES), lambda k, m: (0, k))
    fixed = pl.BlockSpec(tall, lambda k, m: (0, 0))
    own = pl.BlockSpec(tall, col)
    small = pl.BlockSpec((8, LANES), col)
    in_specs = [chunk, own, own, fixed, fixed, small]
    args = [u, x, grad, keep, live, params]
    aliases = None
    if earlier is not None:
        aliases = {len(args) + 1: 0, len(args) + 2: 2, len(args) + 3: 3}
        args += list(earlier)
        in_specs += [pl.BlockSpec(memory_space=pl.ANY)] * 3
    ends = pltpu.VMEM((8 * length // TILE, LANES), F32)
    return call(
        scan_kernel,
        meta,
        args,
        (blocks,),
        in_specs,
        [own, chunk, own, small],
        [
            struct((length, channels), BF16),
            struct(u.shape, BF16),
            struct((length, channels), BF16),
            struct((8, channels), F32),
        ],
        scratch=[pltpu.VMEM((TILE, TILE), BF16)]
        + [pltpu.VMEM(tall, F32)] * 8
        + [pltpu.VMEM(tall, BF16)]
        + [ends] * 4,
        aliases=aliases,
        cost=cost(60 * length * channels // 2, 9 * length * channels, length * channels, weight=COVER),
    )


def wgrad_kernel(meta, normed_ref, ds_ref, a_ref, b_ref):
    first = pl.program_id(0) < pl.num_programs(0) // 2
    dims = (((0,), (0,)), ((), ()))

    @pl.when(first)
    def _():
        a_ref[...] = lax.dot_general(normed_ref[...], ds_ref[...], dims, preferred_element_type=F32).astype(BF16)

    @pl.when(jnp.logical_not(first))
    def _():
        b_ref[...] = lax.dot_general(normed_ref[...], ds_ref[...], dims, preferred_element_type=F32).astype(BF16)


def wgrad(meta, normed, ds, first, mb=512):
    tokens, features = normed.shape
    width = ds.shape[1]
    rows = features // 4
    steps = rows // mb

    def lhs(i, m):
        return (0, m[first + i // steps] * steps + i % steps)

    return call(
        wgrad_kernel,
        meta,
        (normed, ds),
        (2 * steps,),
        [
            pl.BlockSpec((tokens, mb), lhs),
            pl.BlockSpec((tokens, width), lambda i, m: (0, 0)),
        ],
        [
            pl.BlockSpec((mb, width), lambda i, m: (jnp.minimum(i, steps - 1), 0)),
            pl.BlockSpec((mb, width), lambda i, m: (jnp.maximum(i - steps, 0), 0)),
        ],
        [struct((rows, width), BF16)] * 2,
        cost=cost(4 * tokens * rows * width, 2 * tokens * (features // 2 + width), weight=COVER),
    )


def back_kernel(meta, ds1_ref, ds2_ref, *refs):
    out_ref, W = refs[-2:]
    chunk = ds1_ref.shape[1]

    @pl.when(pl.program_id(0) == 0)
    def _():
        gather_units(meta, M_S1, refs[:6], W, 0)
        gather_units(meta, M_S2, refs[6:12], W, chunk)

    dims = (((1,), (1,)), ((), ()))
    value = lax.dot_general(ds1_ref[...], W[:, :chunk], dims, preferred_element_type=F32)
    value += lax.dot_general(ds2_ref[...], W[:, chunk:], dims, preferred_element_type=F32)
    out_ref[...] = value.astype(BF16)


def back(meta, ds1, ds2, units, at, tb=1024):
    tokens, width = ds1.shape
    features = units[0][0].shape[0]
    block = features // 4
    dspec = pl.BlockSpec((tb, width), lambda t, m: (t, 0))
    return call(
        back_kernel,
        meta,
        [ds1, ds2] + [array for array, _, _ in units],
        (tokens // tb,),
        [dspec, dspec] + unit_specs(units, block, lambda t, m: m[at]),
        pl.BlockSpec((tb, block), lambda t, m: (t, 0)),
        struct((tokens, block), BF16),
        scratch=[pltpu.VMEM((block, 2 * width), BF16)],
        cost=cost(4 * tokens * block * width, 4 * tokens * width, weight=COVER),
    )


def unit_of(x_ref, mu_ref, inv_ref):
    repeat = x_ref.shape[1] // LANES
    mu = jnp.concatenate([mu_ref[...]] * repeat, axis=1)
    inv = jnp.concatenate([inv_ref[...]] * repeat, axis=1)
    return (x_ref[...].astype(F32) - mu) * inv, inv


def lane_sums(value):
    part = value[:, :LANES]
    for g in range(1, value.shape[1] // LANES):
        part = part + value[:, g * LANES : (g + 1) * LANES]
    return jnp.sum(part.T, axis=0, keepdims=True)


def tail_sums_kernel(meta, k_ref, rc_ref, r1_ref, r2_ref, x_ref, mu_ref, inv_ref, gain_ref, dn_ref, row_ref, col_ref):
    unit, _ = unit_of(x_ref, mu_ref, inv_ref)
    early = pl.program_id(0) < pl.num_programs(0) * FIRST // 8
    far = jnp.where(early, r1_ref[...].astype(F32), r2_ref[...].astype(F32))
    dn = k_ref[...].astype(F32) + rc_ref[...].astype(F32) + far
    dn_ref[...] = dn
    gu = dn * gain_ref[...]
    row_ref[0:1, :] = lane_sums(gu)
    row_ref[1:2, :] = lane_sums(gu * unit)
    row_ref[2:8, :] = jnp.zeros((6, row_ref.shape[1]), F32)

    @pl.when(pl.program_id(0) == 0)
    def _():
        col_ref[...] = jnp.zeros_like(col_ref)

    col_ref[0:1, :] += jnp.sum(dn * unit, axis=0, keepdims=True)
    col_ref[1:2, :] += jnp.sum(dn, axis=0, keepdims=True)


def tail_sums(meta, keep, got, far, x, mu, inv, gain, tb=256):
    tokens, channels = x.shape
    first = tokens // tb * FIRST // 8
    wide = pl.BlockSpec((tb, channels), lambda t, m: (t, 0))
    stat = pl.BlockSpec((tb, LANES), lambda t, m: (t, 0))
    return call(
        tail_sums_kernel,
        meta,
        (keep, got, *far, x, mu, inv, gain[None]),
        (tokens // tb,),
        [
            wide,
            wide,
            pl.BlockSpec((tb, channels), lambda t, m: (jnp.minimum(t, first - 1), 0)),
            pl.BlockSpec((tb, channels), lambda t, m: (jnp.maximum(t - first, 0), 0)),
            wide,
            stat,
            stat,
            pl.BlockSpec((1, channels), lambda t, m: (0, m[M_GATE])),
        ],
        [
            wide,
            pl.BlockSpec((8, tb), lambda t, m: (0, t)),
            pl.BlockSpec((8, channels), lambda t, m: (0, 0)),
        ],
        [struct((tokens, channels), F32), struct((8, tokens), F32), struct((8, channels), F32)],
        cost=cost(20 * tokens * channels, 12 * tokens * channels, weight=COVER),
    )


def tail_kernel(features, meta, dn_ref, row_ref, x_ref, mu_ref, inv_ref, gain_ref, direct_ref, out_ref, PM):
    @pl.when(pl.program_id(0) == 0)
    def _():
        PM[...] = order_matrix()

    unit, inv = unit_of(x_ref, mu_ref, inv_ref)
    repeat = x_ref.shape[1] // LANES
    tb = x_ref.shape[0]

    def mean(n):
        row = row_ref[n : n + 1, :] * (1.0 / features)
        return jnp.concatenate([jnp.broadcast_to(row, (LANES, tb)).T] * repeat, axis=1)

    gu = dn_ref[...] * gain_ref[...]
    value = (inv * (gu - mean(0) - unit * mean(1)) + direct_ref[...].astype(F32)).astype(BF16)
    for q in range(tb // TILE):
        at = slice(q * TILE, (q + 1) * TILE)
        out_ref[at, :] = to_tokens(PM[...], value[at]).astype(BF16)


def tail(meta, dn, rows, x, mu, inv, gain, direct, features, tb=512):
    tokens, channels = dn.shape
    wide = pl.BlockSpec((tb, channels), lambda t, m: (t, 0))
    stat = pl.BlockSpec((tb, LANES), lambda t, m: (t, 0))
    return call(
        functools.partial(tail_kernel, features),
        meta,
        (dn, rows, x, mu, inv, gain[None], direct),
        (tokens // tb,),
        [
            wide,
            pl.BlockSpec((rows.shape[0], tb), lambda t, m: (0, t)),
            wide,
            stat,
            stat,
            pl.BlockSpec((1, channels), lambda t, m: (0, m[M_GATE])),
            wide,
        ],
        wide,
        struct((tokens, channels), BF16),
        scratch=[pltpu.VMEM((TILE, TILE), BF16)],
        cost=cost(10 * tokens * channels, 12 * tokens * channels),
    )


def halve_kernel(meta, *refs):
    ins, (away_ref, stay_ref) = refs[:-2], refs[-2:]
    for n, out_ref in ((0, away_ref), (1, stay_ref)):
        part = ins[n * len(ins) // 2 : (n + 1) * len(ins) // 2]
        if len(part) == 4:
            for o in range(2):
                out_ref[o] = (part[o][...].astype(F32) + part[2 + o][...].astype(F32)).astype(BF16)
        else:
            out_ref[...] = (part[0][...].astype(F32) + part[1][...].astype(F32)).astype(BF16)


def halve(meta, at, kept, got, parts=2):
    if len(kept) == 2:
        rows, width = kept[0].shape
        lead = ()
    else:
        lead, rows, width = kept[0].shape
        lead = (lead,)
    half = rows // 2
    tb = half // parts
    zeros = (0,) * len(lead)
    specs, args = [], []
    for side in range(2):
        for array in (*kept, *got):
            specs.append(
                pl.BlockSpec((*lead, tb, width), lambda i, m, side=side: (*zeros, (m[at] ^ (1 - side)) * parts + i, 0))
            )
            args.append(array)
    out = pl.BlockSpec((2, tb, width), lambda i, m: (0, i, 0))
    return call(
        halve_kernel,
        meta,
        args,
        (parts,),
        specs,
        [out, out],
        [struct((2, half, width), BF16)] * 2,
        cost=cost(4 * rows * width, 12 * rows * width),
    )


def split_kernel(late, half, meta, a_ref, b_ref, near_ref, far_ref):
    core = meta[M_CORE]
    h = meta[half]
    pair_ref, single_ref = (far_ref, near_ref) if late else (near_ref, far_ref)

    def take(owner, stream, block):
        col = pl.ds(pl.multiple_of((block * 3 + stream) * LANES, LANES), LANES)
        return (a_ref[owner, :, col].astype(F32) + b_ref[owner, :, col].astype(F32)).astype(BF16)

    for store in range(2):
        k = core ^ store
        for owner in range(2):
            for block in range(2):
                at = (2 * owner + block) * LANES
                pair_ref[store, :, at : at + LANES] = take(owner, k + h, block)
            single_ref[store, :, owner * LANES : (owner + 1) * LANES] = take(owner, 2 * (1 - h), k)


def split(meta, half, late, kept, got):
    _, rows, width = kept.shape
    pair, single = 4 * LANES, 2 * LANES
    widths = (single, pair) if late else (pair, single)
    whole = pl.BlockSpec((2, rows, width), lambda i, m: (0, 0, 0))
    return call(
        functools.partial(split_kernel, late, half),
        meta,
        (kept, got),
        (1,),
        [whole] * 2,
        [pl.BlockSpec((2, rows, w), lambda i, m: (0, 0, 0)) for w in widths],
        [struct((2, rows, w), BF16) for w in widths],
        cost=cost(2 * rows * width, 12 * rows * width),
    )


def join_kernel(meta, a_ref, b_ref, *outs):
    rows = a_ref.shape[1]
    for n, out_ref in enumerate(outs):
        out_ref[:rows, :] = a_ref[n]
        out_ref[rows:, :] = b_ref[n]


def join(meta, a, b):
    _, rows, width = a.shape
    whole = pl.BlockSpec((2, rows, width), lambda i, m: (0, 0, 0))
    out = pl.BlockSpec((2 * rows, width), lambda i, m: (0, 0))
    return call(
        join_kernel,
        meta,
        (a, b),
        (1,),
        [whole] * 2,
        [out] * 2,
        [struct((2 * rows, width), BF16)] * 2,
        cost=cost(0, 16 * rows * width),
    )


def place_kernel(blocks, meta, *refs):
    out_ref = refs[-1]
    step = pl.program_id(0)
    piece = out_ref.shape[1] // 4
    unit = piece // 3
    rows = out_ref.shape[0] // blocks
    core = meta[M_CORE]
    for stream in range(2):
        for part in range(2):

            @pl.when(step == stream * 2 + part)
            def _(stream=stream, part=part):
                one = refs[stream * 2 + part]
                two = refs[4 + stream * 2 + part]
                inner = meta[M_RHO + stream] % blocks

                def put(owner, single, src, col):
                    base = meta[M_OWN + (owner ^ stream)] * piece
                    wide = unit if single else 2 * unit
                    at = base + (jnp.where(core == 0, 2 * unit, 0) if single else core * unit)
                    at = pl.ds(pl.multiple_of(at, LANES), wide)
                    for j in range(blocks):
                        to = pl.ds(pl.multiple_of((inner ^ j) * rows, rows), rows)
                        out_ref[to, at] = src[j * rows : (j + 1) * rows, col : col + wide].astype(F32)

                put(0, False, one, 0)
                put(1, False, one, 2 * unit)
                put(2, True, one, 4 * unit)
                put(3, True, one, 5 * unit)
                put(0, True, two, 0)
                put(1, True, two, unit)
                put(2, False, two, 2 * unit)
                put(3, False, two, 4 * unit)


def place(meta, parts1, parts2, n_dp, features, columns):
    blocks = n_dp // 2
    whole = pl.BlockSpec((features // 4, columns // 2), lambda i, m: (0, 0))

    def where_to(i, m):
        stream = i // 2
        return ((m[M_CORE] ^ stream) * 2 + (i % 2 ^ m[M_RHO + stream] // blocks), 0)

    return call(
        functools.partial(place_kernel, blocks),
        meta,
        (*parts1, *parts2),
        (4,),
        [whole] * 8,
        pl.BlockSpec((features // 4, columns), where_to),
        struct((features, columns), F32),
        cost=cost(features * columns, 6 * features * columns),
    )


M_GATE, M_CORE, M_H1, M_H2 = 0, 1, 2, 3
M_S1, M_S2 = 4, 7
M_SEND, M_KEEP = 10, 12
M_FAR, M_HERE = 14, 16
M_OWN, M_RHO = 18, 22
M_TO2, M_TO3, M_NEAR, M_LATE2, M_LATE3 = 24, 25, 26, 27, 28
M_PAIR, M_SINGLE, M_GOT_PAIR, M_GOT_SINGLE = 29, 30, 31, 32
M_BIT = 33


def shards(
    n_dp,
    n_gate,
    inputs,
    weight,
    ln_gain,
    ln_bias,
    forget_peep,
    reset_peep,
    forget_bias,
    reset_bias,
    resets,
    padding,
    grad_out,
):
    rows, tokens, features = inputs.shape
    assert rows == 1 and n_gate == 4
    channels = forget_peep.shape[0]
    assert channels == 4 * LANES
    bits = n_dp.bit_length() - 1
    assert 1 << bits == n_dp
    gate = lax.axis_index("gate")
    dp = lax.axis_index("dp")
    hi, core = gate // 2, gate % 2
    other = 1 - core

    orders = [list(range(bits)), [1, 0, *range(2, bits)]]

    def bit(stream, step):
        return (dp >> jnp.where(stream == 0, orders[0][step], orders[1][step])) & 1

    def rho(stream):
        value = 0
        for step in range(bits):
            value = value * 2 + bit(stream, step)
        return value

    def streams(h):
        return [core + h, other + h, 2 * (1 - h)]

    h1, h2 = hi, 1 - hi
    far = (1 - hi) * 2
    single, pair = 2 * other, core
    meta = jnp.stack(
        [gate, core, h1, h2, *streams(h1), *streams(h2)]
        + [other * 2 + 1 - bit(other, 0), core * 2 + 1 - bit(core, 0)]
        + [other * 2 + bit(other, 0), core * 2 + bit(core, 0)]
        + [far + other, far + core, hi * 2 + other, hi * 2 + core]
        + [gate, hi * 2 + other, far + core, far + other]
        + [rho(core), rho(other)]
        + [(far + core) * 3 + single, (far + other) * 3 + single, (hi * 2 + other) * 3]
        + [(far + core) * 3 + pair, (far + other) * 3 + pair]
        + [gate * 3 + pair, gate * 3 + single, other, 2 * core]
        + [bit(core, step) for step in range(bits)]
    ).astype(jnp.int32)

    def over_gate(value, delta):
        return lax.ppermute(value, "gate", [(g, g ^ delta) for g in range(n_gate)])

    def over_dp(value, step):
        pairs = [
            (d * n_gate + g, (d ^ (1 << orders[g % 2][step])) * n_gate + g) for d in range(n_dp) for g in range(n_gate)
        ]
        return lax.ppermute(value, ("dp", "gate"), pairs)

    def after(value, *others):
        return lax.optimization_barrier((value, *others))[0]

    x = inputs.reshape(tokens, features)
    grad = grad_out.reshape(tokens, channels)
    params = jnp.concatenate(
        [jnp.stack([forget_peep, reset_peep, forget_bias, reset_bias]), jnp.zeros((4, channels), F32)]
    )

    to2, to3, near = cut(meta, weight, [(M_TO2, 1), (M_TO3, 1), (M_NEAR, 3)])
    sent2, sent3, near = over_gate(to2, 2), over_gate(to3, 3), over_gate(near, 1)
    normed, mu, inv, own_x, keep, live = norm(
        after(meta, to2, to3), x, ln_gain, ln_bias, resets, padding, channels
    )
    away2, away3 = cut(after(meta, normed), weight, [(M_LATE2, 2), (M_LATE3, 2)])
    late2, late3 = over_gate(away2, 2), over_gate(away3, 3)
    units1 = [(weight, M_PAIR, 0), (weight, M_PAIR, 1), (near, M_GOT_PAIR, 0), (near, M_GOT_PAIR, 1)]
    units1 += [(sent2, None, 0), (sent3, None, 0)]
    units2 = [(late2, None, 0), (late2, None, 1), (late3, None, 0), (late3, None, 1)]
    units2 += [(weight, M_SINGLE, 0), (near, M_GOT_SINGLE, 0)]
    units = units1 + units2

    def first_sends(meta, ds):
        theirs, mine = wgrad(meta, normed, ds, M_SEND)
        return mine, [over_dp(mine, 0), over_dp(over_gate(theirs, 1), 0)]

    def first_keeps(meta, ds):
        theirs, mine = wgrad(meta, normed, ds, M_KEEP)
        return [mine, over_gate(theirs, 1)]

    def gathered(meta, half, late, kept, got):
        near, far = split(meta, half, late, kept, got)
        return near, over_gate(far, 2)

    def last_steps(shard, *others):
        for step in reversed(range(2, bits)):
            shard = jnp.concatenate([after(shard, *others), over_dp(shard, step)], axis=1)
        return shard

    u1 = project(after(meta, away2, away3), M_S1, normed, units1)
    hidden, ds1, direct, vecs = scan(meta, M_H1, u1, own_x, grad, keep, live, params, None)
    mine1, got1 = first_sends(meta, ds1)
    kept1 = first_keeps(after(meta, mine1), ds1)
    u2 = project(after(meta, kept1[0]), M_S2, normed, units2)
    away1, stay1 = halve(after(meta, u2), M_BIT + 1, kept1, got1)
    step1 = over_dp(away1, 1)
    hidden, ds2, direct, vecs = scan(
        after(meta, away1), M_H2, u2, own_x, grad, keep, live, params, (hidden, direct, vecs)
    )
    for step in range(2, bits):
        away1, stay1 = halve(after(meta, ds2), M_BIT + step, [stay1], [step1])
        step1 = over_dp(away1, step)
    mine2, got2 = first_sends(after(meta, away1), ds2)
    kept2 = first_keeps(after(meta, mine2), ds2)
    far_theirs = back(after(meta, kept2[0]), ds1, ds2, units, M_FAR)
    far_got = over_gate(far_theirs, 1)
    near1, far1 = gathered(after(meta, far_theirs), M_H1, False, stay1, step1)
    away2, stay2 = halve(after(meta, near1), M_BIT + 1, kept2, got2)
    step2 = over_dp(away2, 1)
    far_mine = back(after(meta, away2), ds1, ds2, units, M_FAR + 1)
    for step in range(2, bits):
        away2, stay2 = halve(after(meta, far_mine), M_BIT + step, [stay2], [step2])
        step2 = over_dp(away2, step)
    far_mine = after(far_mine, away2)
    cut_at = tokens * FIRST // 8
    far_send = [
        (far_mine[at].astype(F32) + far_got[at].astype(F32)).astype(BF16) for at in (slice(cut_at), slice(cut_at, None))
    ]
    far_part = [over_gate(part, 2) for part in far_send]
    theirs = back(after(meta, away2, *far_send), ds1, ds2, units, M_HERE)
    got = over_gate(theirs, 1)
    shard1 = jnp.concatenate([after(near1, theirs), far1], axis=2)

    def last_doubling(meta, shard):
        mine, theirs = join(meta, shard, over_dp(shard, 1))
        moved = over_dp(theirs, 0)
        return [mine, over_dp(mine, 0), over_gate(theirs, 1), over_gate(moved, 1)]

    near2, far2 = gathered(after(meta, shard1, far_part[0]), M_H2, True, stay2, step2)
    mine = back(after(meta, theirs, near2), ds1, ds2, units, M_HERE + 1)
    shard2 = jnp.concatenate([after(near2, mine), far2], axis=2)
    shard1 = last_steps(shard1, shard2)
    parts1 = last_doubling(after(meta, shard2), shard1)
    shard2 = last_steps(shard2, parts1[0])
    parts2 = last_doubling(after(meta, far_part[1]), shard2)
    dn, row_sums, col_sums = tail_sums(
        after(meta, parts2[0], parts1[1]), mine, got, far_part, own_x, mu, inv, ln_gain
    )
    for delta in (1, 2):
        row_sums = row_sums + over_gate(row_sums, delta)
    dinputs = tail(after(meta, parts2[1], *parts1), dn, row_sums, own_x, mu, inv, ln_gain, direct, features)

    totals = jnp.concatenate([col_sums[:2], vecs[:4]], axis=0)
    for step in range(bits):
        totals = totals + lax.ppermute(totals, "dp", [(d, d ^ (1 << step)) for d in range(n_dp)])

    grad_weight = place(meta, parts1, parts2, n_dp, features, weight.shape[1])
    return (
        hidden.reshape(rows, tokens, channels),
        dinputs.reshape(rows, tokens, channels),
        grad_weight,
        totals[0],
        totals[1],
        totals[2],
        totals[3],
        totals[4],
        totals[5],
    )


def solution(mesh):
    return jax.shard_map(
        functools.partial(shards, mesh.shape["dp"], mesh.shape["gate"]),
        mesh=mesh,
        in_specs=(
            P("dp", None, None),
            P(None, "gate"),
            P(),
            P(),
            P("gate"),
            P("gate"),
            P("gate"),
            P("gate"),
            P("dp", None),
            P("dp", None),
            P("dp", None, "gate"),
        ),
        out_specs=(
            P("dp", None, "gate"),
            P("dp", None, "gate"),
            P(None, "gate"),
            P("gate"),
            P("gate"),
            P("gate"),
            P("gate"),
            P("gate"),
            P("gate"),
        ),
        check_vma=False,
    )
```

```python
import functools

import jax
import jax.numpy as jnp
from jax import lax
from jax.experimental import pallas as pl
from jax.experimental.pallas import tpu as pltpu
from jax.sharding import PartitionSpec as P

epsilon = 1e-05
F32 = jnp.float32
BF16 = jnp.bfloat16
LANES = 128
VMEM_LIMIT = 60 * 1024 * 1024
COVER = 20
FIRST = 3


def call(kernel, meta, args, grid, in_specs, out_specs, out_shape, scratch=(), aliases=None, cost=None):
    return pl.pallas_call(
        kernel,
        grid_spec=pltpu.PrefetchScalarGridSpec(
            num_scalar_prefetch=1,
            grid=grid,
            in_specs=in_specs,
            out_specs=out_specs,
            scratch_shapes=list(scratch),
        ),
        out_shape=out_shape,
        input_output_aliases=aliases or {},
        compiler_params=pltpu.CompilerParams(
            dimension_semantics=("arbitrary",) * len(grid), vmem_limit_bytes=VMEM_LIMIT
        ),
        cost_estimate=cost,
    )(meta, *args)


def cost(flops, nbytes, trans=0, weight=1):
    return pl.CostEstimate(flops=int(weight * flops), bytes_accessed=int(weight * nbytes), transcendentals=int(trans))


def struct(shape, dtype):
    return jax.ShapeDtypeStruct(shape, dtype)


TILE = 256


def order_matrix():
    row = lax.broadcasted_iota(jnp.int32, (TILE, TILE), 0)
    token = lax.broadcasted_iota(jnp.int32, (TILE, TILE), 1)
    return jnp.where(token == (row % 8) * (TILE // 8) + row // 8, 1.0, 0.0).astype(BF16)


def to_rows(order, value):
    return jnp.dot(order, value, preferred_element_type=F32)


def to_tokens(order, value):
    return lax.dot_general(order, value, (((0,), (0,)), ((), ())), preferred_element_type=F32)


def norm_kernel(
    meta, x_ref, gain_ref, bias_ref, res_ref, pad_ref, out_ref, mu_ref, inv_ref, own_ref, keep_ref, live_ref, PM, XP, S1, S2
):
    @pl.when(pl.program_id(0) == 0)
    def _():
        PM[...] = order_matrix()

    order = PM[...]
    features = x_ref.shape[1]
    groups = features // LANES
    wide = 2 * LANES
    ones = jnp.ones((TILE, LANES), BF16)
    keep_ref[...] = jnp.dot(order * (1 - res_ref[0]).astype(F32).astype(BF16), ones, preferred_element_type=F32)
    live_ref[...] = jnp.dot(order * pad_ref[0].astype(F32).astype(BF16), ones, preferred_element_type=F32)
    shift = None
    first = second = None
    for g in range(0, features, wide):
        value = to_rows(order, x_ref[:, g : g + wide])
        XP[:, g : g + wide] = value
        if shift is None:
            shift = jnp.broadcast_to(value[:, 0:1], (TILE, LANES))
            S1[...] = shift
        one, two = value[:, :LANES] - shift, value[:, LANES:] - shift
        first = one + two if first is None else first + (one + two)
        squares = one * one + two * two
        second = squares if second is None else second + squares
    drift = jnp.sum(first, axis=1, keepdims=True) * (1.0 / features)
    spread = jnp.sum(second, axis=1, keepdims=True) * (1.0 / features) - drift * drift
    mu_ref[...] = shift + drift
    inv_ref[...] = jnp.broadcast_to(lax.rsqrt(jnp.maximum(spread, 0.0) + epsilon), inv_ref.shape)
    tall = 16

    def scaled(i, carry):
        rows = pl.ds(pl.multiple_of(i * tall, tall), tall)
        mean = mu_ref[rows, :]
        scale = inv_ref[rows, :]
        for g in range(groups):
            at = slice(g * LANES, (g + 1) * LANES)
            value = (XP[rows, at] - mean) * scale * gain_ref[0:1, at] + bias_ref[0:1, at]
            out_ref[rows, at] = value.astype(BF16)
        return carry

    lax.fori_loop(0, TILE // tall, scaled, 0, unroll=2)
    channels = own_ref.shape[1]
    own_ref[...] = XP[:, pl.ds(pl.multiple_of(meta[M_GATE] * channels, channels), channels)].astype(BF16)


def norm(meta, x, gain, bias, resets, padding, channels):
    tokens, features = x.shape
    tiles = tokens // TILE
    row = pl.BlockSpec((TILE, features), lambda t, m: (t, 0))
    whole = pl.BlockSpec((1, features), lambda t, m: (0, 0))
    flag = pl.BlockSpec((1, 1, TILE), lambda t, m: (t, 0, 0))
    stat = pl.BlockSpec((TILE, LANES), lambda t, m: (t, 0))
    stats = struct((tokens, LANES), F32)
    return call(
        norm_kernel,
        meta,
        (x, gain[None], bias[None], resets.reshape(tiles, 1, TILE), padding.reshape(tiles, 1, TILE)),
        (tiles,),
        [row, whole, whole, flag, flag],
        [row, stat, stat, pl.BlockSpec((TILE, channels), lambda t, m: (t, 0)), stat, stat],
        [struct(x.shape, BF16), stats, stats, struct((tokens, channels), BF16), stats, stats],
        scratch=[pltpu.VMEM((TILE, TILE), BF16), pltpu.VMEM((TILE, features), F32)] + [pltpu.VMEM((TILE, LANES), F32)] * 2,
        cost=cost(8 * tokens * features, 4 * tokens * features, weight=COVER),
    )


def column_of(meta, table, plane, block):
    blk = block ^ meta[M_CORE] if plane == 2 else block
    return pl.multiple_of((blk * 3 + meta[table + plane]) * LANES, LANES)


def cut_kernel(widths, meta, *refs):
    for n, width in enumerate(widths):
        out_ref = refs[sum(widths) + n]
        for b in range(width):
            out_ref[:, b * LANES : (b + 1) * LANES] = refs[sum(widths[:n]) + b][...]


def cut(meta, weight, pieces, tb=512):
    rows = weight.shape[0]
    widths = [width for _, width in pieces]
    specs = [
        pl.BlockSpec((tb, LANES), lambda t, m, at=at, b=b: (t, m[at] + b)) for at, width in pieces for b in range(width)
    ]
    return call(
        functools.partial(cut_kernel, widths),
        meta,
        [weight] * len(specs),
        (rows // tb,),
        specs,
        [pl.BlockSpec((tb, width * LANES), lambda t, m: (t, 0)) for width in widths],
        [struct((rows, width * LANES), BF16) for width in widths],
        cost=cost(0, 4 * rows * LANES * sum(widths)),
    )


def unit_specs(units, rows, row_of):
    return [pl.BlockSpec((rows, LANES), lambda *i, at=at, b=b: (row_of(*i), (i[-1][at] if at else 0) + b)) for _, at, b in units]


def gather_units(meta, table, refs, W, base):
    for n, ref in enumerate(refs):
        at = pl.multiple_of(base + column_of(meta, table, n // 2, n % 2), LANES)
        W[:, pl.ds(at, LANES)] = ref[...]


def project_kernel(table, meta, normed_ref, *refs):
    out_ref, W = refs[-2:]

    @pl.when(pl.program_id(0) == 0)
    def _():
        gather_units(meta, table, refs[:6], W, 0)

    out_ref[...] = jnp.dot(normed_ref[...], W[...], preferred_element_type=F32).astype(BF16)


def project(meta, table, normed, units, tb=512):
    tokens, features = normed.shape
    columns = 6 * LANES
    return call(
        functools.partial(project_kernel, table),
        meta,
        [normed] + [array for array, _, _ in units],
        (tokens // tb,),
        [pl.BlockSpec((tb, features), lambda t, m: (t, 0))] + unit_specs(units, features, lambda t, m: 0),
        pl.BlockSpec((tb, columns), lambda t, m: (t, 0)),
        struct((tokens, columns), BF16),
        scratch=[pltpu.VMEM((features, columns), BF16)],
        cost=cost(2 * tokens * features * columns, 2 * tokens * (features + 2 * columns), weight=COVER),
    )


def sigmoid(z):
    return 0.5 * jnp.tanh(0.5 * z) + 0.5


def scan_kernel(meta, u_ref, x_ref, g_ref, keep_ref, live_ref, prm_ref, *refs):
    (hid_ref, ds_ref, direct_ref, vec_ref, PM, A, B, FG, R, PV, GL, XF, UT, HP, CE, PE, CI, EI) = refs[-18:]
    length = x_ref.shape[0]
    tiles = length // TILE
    seg = TILE // 8
    rows_in = 64
    each = TILE // rows_in
    groups = rows_in // 8
    pf, pr, bf, br = (jnp.broadcast_to(prm_ref[i : i + 1, :], (rows_in, LANES)) for i in range(4))

    @pl.when(pl.program_id(0) == 0)
    def _():
        PM[...] = order_matrix()

    order = PM[...]
    for q in range(tiles):
        GL[q * TILE : (q + 1) * TILE, :] = to_rows(order, g_ref[q * TILE : (q + 1) * TILE, :])

    zeros = jnp.zeros((8, LANES), F32)
    ones = jnp.ones((8, LANES), F32)

    def rows_at(i):
        return pl.ds(pl.multiple_of(i * rows_in, rows_in), rows_in)

    def tile_at(i):
        return pl.ds(pl.multiple_of((i // each) * 8, 8), 8)

    def gates(i, carry):
        rows = rows_at(i)
        x = x_ref[rows, :].astype(F32)
        ut = u_ref[rows, 0:LANES].astype(F32)
        forget = sigmoid(u_ref[rows, LANES : 2 * LANES].astype(F32) + pf * x + bf)
        reset = sigmoid(u_ref[rows, 2 * LANES :].astype(F32) + pr * x + br)
        a = forget * keep_ref[rows, :]
        b = (1.0 - forget) * ut
        gl = GL[rows, :] * live_ref[rows, :]
        d = gl * reset
        XF[rows, :] = x
        UT[rows, :] = ut
        FG[rows, :] = forget
        R[rows, :] = reset
        A[rows, :] = a
        B[rows, :] = b
        GL[rows, :] = gl
        fresh = i % each == 0
        c, p, e = (jnp.where(fresh, start, old) for start, old in zip((zeros, ones, zeros), carry))
        for j in range(groups):
            at = slice(8 * j, 8 * j + 8)
            c = a[at] * c + b[at]
            p = a[at] * p
            e = e + p * d[at]
        CE[tile_at(i), :] = c
        PE[tile_at(i), :] = p
        EI[tile_at(i), :] = e
        return (c, p, e)

    lax.fori_loop(0, tiles * each, gates, (zeros, ones, zeros))

    count = 8 * tiles
    c = jnp.zeros((1, LANES), F32)
    e = jnp.zeros((1, LANES), F32)
    for j in range(count):
        CI[j : j + 1, :] = c
        c = CE[j : j + 1, :] + PE[j : j + 1, :] * c
        r = count - 1 - j
        own = EI[r : r + 1, :]
        EI[r : r + 1, :] = e
        e = own + PE[r : r + 1, :] * e

    def forward(i, carry):
        out = []
        for q in range(tiles):
            rows = pl.ds(pl.multiple_of(q * TILE + i * 8, 8), 8)
            PV[rows, :] = carry[q]
            out.append(A[rows, :] * carry[q] + B[rows, :])
        return tuple(out)

    lax.fori_loop(0, seg, forward, tuple(CI[8 * q : 8 * q + 8, :] for q in range(tiles)), unroll=4)

    def fold(v):
        return v.reshape(groups, 8, LANES).sum(axis=0)

    def grads(n, carry):
        i = tiles * each - 1 - n
        rows = rows_at(i)
        e, s0, s1, s2, s3 = carry
        e = jnp.where(n % each == 0, EI[tile_at(i), :], e)
        g = GL[rows, :]
        reset = R[rows, :]
        a = A[rows, :]
        d = g * reset
        dcs = [None] * groups
        for j in reversed(range(groups)):
            at = slice(8 * j, 8 * j + 8)
            dcs[j] = d[at] + e
            e = a[at] * dcs[j]
        dc = jnp.concatenate(dcs, axis=0)
        x = XF[rows, :]
        forget = FG[rows, :]
        prev = PV[rows, :]
        gap = a * prev + B[rows, :] - x
        HP[rows, :] = (live_ref[rows, :] * (x + reset * gap)).astype(BF16)
        rest = 1.0 - reset
        dreset = g * gap * (reset * rest)
        dtilde = dc * (1.0 - forget)
        dforget = dtilde * forget * (prev * keep_ref[rows, :] - UT[rows, :])
        ds_ref[rows, 0:LANES] = dtilde.astype(BF16)
        ds_ref[rows, LANES : 2 * LANES] = dforget.astype(BF16)
        ds_ref[rows, 2 * LANES :] = dreset.astype(BF16)
        direct_ref[rows, :] = (g * rest + dforget * pf + dreset * pr).astype(BF16)
        return (e, s0 + fold(dforget * x), s1 + fold(dreset * x), s2 + fold(dforget), s3 + fold(dreset))

    sums = lax.fori_loop(0, tiles * each, grads, (zeros,) * 5)[1:]
    for n, s in enumerate(sums):
        vec_ref[n : n + 1, :] = jnp.sum(s, axis=0, keepdims=True)
    vec_ref[4:8, :] = jnp.zeros((4, LANES), F32)
    for q in range(tiles):
        at = slice(q * TILE, (q + 1) * TILE)
        hid_ref[at, :] = to_tokens(order, HP[at, :]).astype(BF16)


def scan(meta, half, u, x, grad, keep, live, params, earlier):
    length, channels = x.shape
    blocks = u.shape[1] // (3 * LANES)
    col = lambda k, m: (0, m[half] * blocks + k)
    tall = (length, LANES)
    chunk = pl.BlockSpec((length, 3 * LANES), lambda k, m: (0, k))
    fixed = pl.BlockSpec(tall, lambda k, m: (0, 0))
    own = pl.BlockSpec(tall, col)
    small = pl.BlockSpec((8, LANES), col)
    in_specs = [chunk, own, own, fixed, fixed, small]
    args = [u, x, grad, keep, live, params]
    aliases = None
    if earlier is not None:
        aliases = {len(args) + 1: 0, len(args) + 2: 2, len(args) + 3: 3}
        args += list(earlier)
        in_specs += [pl.BlockSpec(memory_space=pl.ANY)] * 3
    ends = pltpu.VMEM((8 * length // TILE, LANES), F32)
    return call(
        scan_kernel,
        meta,
        args,
        (blocks,),
        in_specs,
        [own, chunk, own, small],
        [
            struct((length, channels), BF16),
            struct(u.shape, BF16),
            struct((length, channels), BF16),
            struct((8, channels), F32),
        ],
        scratch=[pltpu.VMEM((TILE, TILE), BF16)]
        + [pltpu.VMEM(tall, F32)] * 8
        + [pltpu.VMEM(tall, BF16)]
        + [ends] * 4,
        aliases=aliases,
        cost=cost(60 * length * channels // 2, 9 * length * channels, length * channels, weight=COVER),
    )


def wgrad_kernel(meta, normed_ref, ds_ref, a_ref, b_ref):
    first = pl.program_id(0) < pl.num_programs(0) // 2
    dims = (((0,), (0,)), ((), ()))

    @pl.when(first)
    def _():
        a_ref[...] = lax.dot_general(normed_ref[...], ds_ref[...], dims, preferred_element_type=F32).astype(BF16)

    @pl.when(jnp.logical_not(first))
    def _():
        b_ref[...] = lax.dot_general(normed_ref[...], ds_ref[...], dims, preferred_element_type=F32).astype(BF16)


def wgrad(meta, normed, ds, first, mb=512):
    tokens, features = normed.shape
    width = ds.shape[1]
    rows = features // 4
    steps = rows // mb

    def lhs(i, m):
        return (0, m[first + i // steps] * steps + i % steps)

    return call(
        wgrad_kernel,
        meta,
        (normed, ds),
        (2 * steps,),
        [
            pl.BlockSpec((tokens, mb), lhs),
            pl.BlockSpec((tokens, width), lambda i, m: (0, 0)),
        ],
        [
            pl.BlockSpec((mb, width), lambda i, m: (jnp.minimum(i, steps - 1), 0)),
            pl.BlockSpec((mb, width), lambda i, m: (jnp.maximum(i - steps, 0), 0)),
        ],
        [struct((rows, width), BF16)] * 2,
        cost=cost(4 * tokens * rows * width, 2 * tokens * (features // 2 + width), weight=COVER),
    )


def back_kernel(meta, ds1_ref, ds2_ref, *refs):
    out_ref, W = refs[-2:]
    chunk = ds1_ref.shape[1]

    @pl.when(pl.program_id(0) == 0)
    def _():
        gather_units(meta, M_S1, refs[:6], W, 0)
        gather_units(meta, M_S2, refs[6:12], W, chunk)

    dims = (((1,), (1,)), ((), ()))
    value = lax.dot_general(ds1_ref[...], W[:, :chunk], dims, preferred_element_type=F32)
    value += lax.dot_general(ds2_ref[...], W[:, chunk:], dims, preferred_element_type=F32)
    out_ref[...] = value.astype(BF16)


def back(meta, ds1, ds2, units, at, tb=1024):
    tokens, width = ds1.shape
    features = units[0][0].shape[0]
    block = features // 4
    dspec = pl.BlockSpec((tb, width), lambda t, m: (t, 0))
    return call(
        back_kernel,
        meta,
        [ds1, ds2] + [array for array, _, _ in units],
        (tokens // tb,),
        [dspec, dspec] + unit_specs(units, block, lambda t, m: m[at]),
        pl.BlockSpec((tb, block), lambda t, m: (t, 0)),
        struct((tokens, block), BF16),
        scratch=[pltpu.VMEM((block, 2 * width), BF16)],
        cost=cost(4 * tokens * block * width, 4 * tokens * width, weight=COVER),
    )


def unit_of(x_ref, mu_ref, inv_ref):
    repeat = x_ref.shape[1] // LANES
    mu = jnp.concatenate([mu_ref[...]] * repeat, axis=1)
    inv = jnp.concatenate([inv_ref[...]] * repeat, axis=1)
    return (x_ref[...].astype(F32) - mu) * inv, inv


def lane_sums(value):
    part = value[:, :LANES]
    for g in range(1, value.shape[1] // LANES):
        part = part + value[:, g * LANES : (g + 1) * LANES]
    return jnp.sum(part.T, axis=0, keepdims=True)


def tail_sums_kernel(meta, k_ref, rc_ref, r1_ref, r2_ref, x_ref, mu_ref, inv_ref, gain_ref, dn_ref, row_ref, col_ref):
    unit, _ = unit_of(x_ref, mu_ref, inv_ref)
    early = pl.program_id(0) < pl.num_programs(0) * FIRST // 8
    far = jnp.where(early, r1_ref[...].astype(F32), r2_ref[...].astype(F32))
    dn = k_ref[...].astype(F32) + rc_ref[...].astype(F32) + far
    dn_ref[...] = dn
    gu = dn * gain_ref[...]
    row_ref[0:1, :] = lane_sums(gu)
    row_ref[1:2, :] = lane_sums(gu * unit)
    row_ref[2:8, :] = jnp.zeros((6, row_ref.shape[1]), F32)

    @pl.when(pl.program_id(0) == 0)
    def _():
        col_ref[...] = jnp.zeros_like(col_ref)

    col_ref[0:1, :] += jnp.sum(dn * unit, axis=0, keepdims=True)
    col_ref[1:2, :] += jnp.sum(dn, axis=0, keepdims=True)


def tail_sums(meta, keep, got, far, x, mu, inv, gain, tb=256):
    tokens, channels = x.shape
    first = tokens // tb * FIRST // 8
    wide = pl.BlockSpec((tb, channels), lambda t, m: (t, 0))
    stat = pl.BlockSpec((tb, LANES), lambda t, m: (t, 0))
    return call(
        tail_sums_kernel,
        meta,
        (keep, got, *far, x, mu, inv, gain[None]),
        (tokens // tb,),
        [
            wide,
            wide,
            pl.BlockSpec((tb, channels), lambda t, m: (jnp.minimum(t, first - 1), 0)),
            pl.BlockSpec((tb, channels), lambda t, m: (jnp.maximum(t - first, 0), 0)),
            wide,
            stat,
            stat,
            pl.BlockSpec((1, channels), lambda t, m: (0, m[M_GATE])),
        ],
        [
            wide,
            pl.BlockSpec((8, tb), lambda t, m: (0, t)),
            pl.BlockSpec((8, channels), lambda t, m: (0, 0)),
        ],
        [struct((tokens, channels), F32), struct((8, tokens), F32), struct((8, channels), F32)],
        cost=cost(20 * tokens * channels, 12 * tokens * channels, weight=COVER),
    )


def tail_kernel(features, meta, dn_ref, row_ref, x_ref, mu_ref, inv_ref, gain_ref, direct_ref, out_ref, PM):
    @pl.when(pl.program_id(0) == 0)
    def _():
        PM[...] = order_matrix()

    unit, inv = unit_of(x_ref, mu_ref, inv_ref)
    repeat = x_ref.shape[1] // LANES
    tb = x_ref.shape[0]

    def mean(n):
        row = row_ref[n : n + 1, :] * (1.0 / features)
        return jnp.concatenate([jnp.broadcast_to(row, (LANES, tb)).T] * repeat, axis=1)

    gu = dn_ref[...] * gain_ref[...]
    value = (inv * (gu - mean(0) - unit * mean(1)) + direct_ref[...].astype(F32)).astype(BF16)
    for q in range(tb // TILE):
        at = slice(q * TILE, (q + 1) * TILE)
        out_ref[at, :] = to_tokens(PM[...], value[at]).astype(BF16)


def tail(meta, dn, rows, x, mu, inv, gain, direct, features, tb=512):
    tokens, channels = dn.shape
    wide = pl.BlockSpec((tb, channels), lambda t, m: (t, 0))
    stat = pl.BlockSpec((tb, LANES), lambda t, m: (t, 0))
    return call(
        functools.partial(tail_kernel, features),
        meta,
        (dn, rows, x, mu, inv, gain[None], direct),
        (tokens // tb,),
        [
            wide,
            pl.BlockSpec((rows.shape[0], tb), lambda t, m: (0, t)),
            wide,
            stat,
            stat,
            pl.BlockSpec((1, channels), lambda t, m: (0, m[M_GATE])),
            wide,
        ],
        wide,
        struct((tokens, channels), BF16),
        scratch=[pltpu.VMEM((TILE, TILE), BF16)],
        cost=cost(10 * tokens * channels, 12 * tokens * channels, weight=COVER),
    )


def halve_kernel(meta, *refs):
    ins, (away_ref, stay_ref) = refs[:-2], refs[-2:]
    for n, out_ref in ((0, away_ref), (1, stay_ref)):
        part = ins[n * len(ins) // 2 : (n + 1) * len(ins) // 2]
        if len(part) == 4:
            for o in range(2):
                out_ref[o] = (part[o][...].astype(F32) + part[2 + o][...].astype(F32)).astype(BF16)
        else:
            out_ref[...] = (part[0][...].astype(F32) + part[1][...].astype(F32)).astype(BF16)


def halve(meta, at, kept, got, parts=2):
    if len(kept) == 2:
        rows, width = kept[0].shape
        lead = ()
    else:
        lead, rows, width = kept[0].shape
        lead = (lead,)
    half = rows // 2
    tb = half // parts
    zeros = (0,) * len(lead)
    specs, args = [], []
    for side in range(2):
        for array in (*kept, *got):
            specs.append(
                pl.BlockSpec((*lead, tb, width), lambda i, m, side=side: (*zeros, (m[at] ^ (1 - side)) * parts + i, 0))
            )
            args.append(array)
    out = pl.BlockSpec((2, tb, width), lambda i, m: (0, i, 0))
    return call(
        halve_kernel,
        meta,
        args,
        (parts,),
        specs,
        [out, out],
        [struct((2, half, width), BF16)] * 2,
        cost=cost(4 * rows * width, 12 * rows * width),
    )


def split_kernel(late, half, meta, a_ref, b_ref, near_ref, far_ref):
    core = meta[M_CORE]
    h = meta[half]
    pair_ref, single_ref = (far_ref, near_ref) if late else (near_ref, far_ref)

    def take(owner, stream, block):
        col = pl.ds(pl.multiple_of((block * 3 + stream) * LANES, LANES), LANES)
        return (a_ref[owner, :, col].astype(F32) + b_ref[owner, :, col].astype(F32)).astype(BF16)

    for store in range(2):
        k = core ^ store
        for owner in range(2):
            for block in range(2):
                at = (2 * owner + block) * LANES
                pair_ref[store, :, at : at + LANES] = take(owner, k + h, block)
            single_ref[store, :, owner * LANES : (owner + 1) * LANES] = take(owner, 2 * (1 - h), k)


def split(meta, half, late, kept, got):
    _, rows, width = kept.shape
    pair, single = 4 * LANES, 2 * LANES
    widths = (single, pair) if late else (pair, single)
    whole = pl.BlockSpec((2, rows, width), lambda i, m: (0, 0, 0))
    return call(
        functools.partial(split_kernel, late, half),
        meta,
        (kept, got),
        (1,),
        [whole] * 2,
        [pl.BlockSpec((2, rows, w), lambda i, m: (0, 0, 0)) for w in widths],
        [struct((2, rows, w), BF16) for w in widths],
        cost=cost(2 * rows * width, 12 * rows * width),
    )


def join_kernel(meta, a_ref, b_ref, *outs):
    rows = a_ref.shape[1]
    for n, out_ref in enumerate(outs):
        out_ref[:rows, :] = a_ref[n]
        out_ref[rows:, :] = b_ref[n]


def join(meta, a, b):
    _, rows, width = a.shape
    whole = pl.BlockSpec((2, rows, width), lambda i, m: (0, 0, 0))
    out = pl.BlockSpec((2 * rows, width), lambda i, m: (0, 0))
    return call(
        join_kernel,
        meta,
        (a, b),
        (1,),
        [whole] * 2,
        [out] * 2,
        [struct((2 * rows, width), BF16)] * 2,
        cost=cost(0, 16 * rows * width),
    )


def place_kernel(blocks, meta, *refs):
    out_ref = refs[-1]
    step = pl.program_id(0)
    piece = out_ref.shape[1] // 4
    unit = piece // 3
    rows = out_ref.shape[0] // blocks
    core = meta[M_CORE]
    for stream in range(2):
        for part in range(2):

            @pl.when(step == stream * 2 + part)
            def _(stream=stream, part=part):
                one = refs[stream * 2 + part]
                two = refs[4 + stream * 2 + part]
                inner = meta[M_RHO + stream] % blocks

                def put(owner, single, src, col):
                    base = meta[M_OWN + (owner ^ stream)] * piece
                    wide = unit if single else 2 * unit
                    at = base + (jnp.where(core == 0, 2 * unit, 0) if single else core * unit)
                    at = pl.ds(pl.multiple_of(at, LANES), wide)
                    for j in range(blocks):
                        to = pl.ds(pl.multiple_of((inner ^ j) * rows, rows), rows)
                        out_ref[to, at] = src[j * rows : (j + 1) * rows, col : col + wide].astype(F32)

                put(0, False, one, 0)
                put(1, False, one, 2 * unit)
                put(2, True, one, 4 * unit)
                put(3, True, one, 5 * unit)
                put(0, True, two, 0)
                put(1, True, two, unit)
                put(2, False, two, 2 * unit)
                put(3, False, two, 4 * unit)


def place(meta, parts1, parts2, n_dp, features, columns):
    blocks = n_dp // 2
    whole = pl.BlockSpec((features // 4, columns // 2), lambda i, m: (0, 0))

    def where_to(i, m):
        stream = i // 2
        return ((m[M_CORE] ^ stream) * 2 + (i % 2 ^ m[M_RHO + stream] // blocks), 0)

    return call(
        functools.partial(place_kernel, blocks),
        meta,
        (*parts1, *parts2),
        (4,),
        [whole] * 8,
        pl.BlockSpec((features // 4, columns), where_to),
        struct((features, columns), F32),
        cost=cost(features * columns, 6 * features * columns),
    )


M_GATE, M_CORE, M_H1, M_H2 = 0, 1, 2, 3
M_S1, M_S2 = 4, 7
M_SEND, M_KEEP = 10, 12
M_FAR, M_HERE = 14, 16
M_OWN, M_RHO = 18, 22
M_TO2, M_TO3, M_NEAR, M_LATE2, M_LATE3 = 24, 25, 26, 27, 28
M_PAIR, M_SINGLE, M_GOT_PAIR, M_GOT_SINGLE = 29, 30, 31, 32
M_BIT = 33


def shards(
    n_dp,
    n_gate,
    inputs,
    weight,
    ln_gain,
    ln_bias,
    forget_peep,
    reset_peep,
    forget_bias,
    reset_bias,
    resets,
    padding,
    grad_out,
):
    rows, tokens, features = inputs.shape
    assert rows == 1 and n_gate == 4
    channels = forget_peep.shape[0]
    assert channels == 4 * LANES
    bits = n_dp.bit_length() - 1
    assert 1 << bits == n_dp
    gate = lax.axis_index("gate")
    dp = lax.axis_index("dp")
    hi, core = gate // 2, gate % 2
    other = 1 - core

    orders = [list(range(bits)), [1, 0, *range(2, bits)]]

    def bit(stream, step):
        return (dp >> jnp.where(stream == 0, orders[0][step], orders[1][step])) & 1

    def rho(stream):
        value = 0
        for step in range(bits):
            value = value * 2 + bit(stream, step)
        return value

    def streams(h):
        return [core + h, other + h, 2 * (1 - h)]

    h1, h2 = hi, 1 - hi
    far = (1 - hi) * 2
    single, pair = 2 * other, core
    meta = jnp.stack(
        [gate, core, h1, h2, *streams(h1), *streams(h2)]
        + [other * 2 + 1 - bit(other, 0), core * 2 + 1 - bit(core, 0)]
        + [other * 2 + bit(other, 0), core * 2 + bit(core, 0)]
        + [far + other, far + core, hi * 2 + other, hi * 2 + core]
        + [gate, hi * 2 + other, far + core, far + other]
        + [rho(core), rho(other)]
        + [(far + core) * 3 + single, (far + other) * 3 + single, (hi * 2 + other) * 3]
        + [(far + core) * 3 + pair, (far + other) * 3 + pair]
        + [gate * 3 + pair, gate * 3 + single, other, 2 * core]
        + [bit(core, step) for step in range(bits)]
    ).astype(jnp.int32)

    def over_gate(value, delta):
        return lax.ppermute(value, "gate", [(g, g ^ delta) for g in range(n_gate)])

    def over_dp(value, step):
        pairs = [
            (d * n_gate + g, (d ^ (1 << orders[g % 2][step])) * n_gate + g) for d in range(n_dp) for g in range(n_gate)
        ]
        return lax.ppermute(value, ("dp", "gate"), pairs)

    def after(value, *others):
        return lax.optimization_barrier((value, *others))[0]

    x = inputs.reshape(tokens, features)
    grad = grad_out.reshape(tokens, channels)
    params = jnp.concatenate(
        [jnp.stack([forget_peep, reset_peep, forget_bias, reset_bias]), jnp.zeros((4, channels), F32)]
    )

    to2, to3, near = cut(meta, weight, [(M_TO2, 1), (M_TO3, 1), (M_NEAR, 3)])
    sent2, sent3, near = over_gate(to2, 2), over_gate(to3, 3), over_gate(near, 1)
    normed, mu, inv, own_x, keep, live = norm(
        after(meta, to2, to3), x, ln_gain, ln_bias, resets, padding, channels
    )
    away2, away3 = cut(after(meta, normed), weight, [(M_LATE2, 2), (M_LATE3, 2)])
    late2, late3 = over_gate(away2, 2), over_gate(away3, 3)
    units1 = [(weight, M_PAIR, 0), (weight, M_PAIR, 1), (near, M_GOT_PAIR, 0), (near, M_GOT_PAIR, 1)]
    units1 += [(sent2, None, 0), (sent3, None, 0)]
    units2 = [(late2, None, 0), (late2, None, 1), (late3, None, 0), (late3, None, 1)]
    units2 += [(weight, M_SINGLE, 0), (near, M_GOT_SINGLE, 0)]
    units = units1 + units2

    def first_sends(meta, ds):
        theirs, mine = wgrad(meta, normed, ds, M_SEND)
        return mine, [over_dp(mine, 0), over_dp(over_gate(theirs, 1), 0)]

    def first_keeps(meta, ds):
        theirs, mine = wgrad(meta, normed, ds, M_KEEP)
        return [mine, over_gate(theirs, 1)]

    def gathered(meta, half, late, kept, got):
        near, far = split(meta, half, late, kept, got)
        return near, over_gate(far, 2)

    def last_steps(shard, *others):
        for step in reversed(range(2, bits)):
            shard = jnp.concatenate([after(shard, *others), over_dp(shard, step)], axis=1)
        return shard

    u1 = project(after(meta, away2, away3), M_S1, normed, units1)
    hidden, ds1, direct, vecs = scan(meta, M_H1, u1, own_x, grad, keep, live, params, None)
    mine1, got1 = first_sends(meta, ds1)
    kept1 = first_keeps(after(meta, mine1), ds1)
    u2 = project(after(meta, kept1[0]), M_S2, normed, units2)
    away1, stay1 = halve(after(meta, u2), M_BIT + 1, kept1, got1)
    step1 = over_dp(away1, 1)
    hidden, ds2, direct, vecs = scan(
        after(meta, away1), M_H2, u2, own_x, grad, keep, live, params, (hidden, direct, vecs)
    )
    for step in range(2, bits):
        away1, stay1 = halve(after(meta, ds2), M_BIT + step, [stay1], [step1])
        step1 = over_dp(away1, step)
    mine2, got2 = first_sends(after(meta, away1), ds2)
    kept2 = first_keeps(after(meta, mine2), ds2)
    far_theirs = back(after(meta, kept2[0]), ds1, ds2, units, M_FAR)
    far_got = over_gate(far_theirs, 1)
    away2, stay2 = halve(after(meta, far_theirs), M_BIT + 1, kept2, got2)
    step2 = over_dp(away2, 1)
    near1, far1 = gathered(after(meta, away2), M_H1, False, stay1, step1)
    far_mine = back(after(meta, near1), ds1, ds2, units, M_FAR + 1)
    for step in range(2, bits):
        away2, stay2 = halve(after(meta, far_mine), M_BIT + step, [stay2], [step2])
        step2 = over_dp(away2, step)
    far_mine = after(far_mine, away2)
    cut_at = tokens * FIRST // 8
    far_send = [
        (far_mine[at].astype(F32) + far_got[at].astype(F32)).astype(BF16) for at in (slice(cut_at), slice(cut_at, None))
    ]
    far_part = [over_gate(part, 2) for part in far_send]
    theirs = back(after(meta, away2, *far_send), ds1, ds2, units, M_HERE)
    got = over_gate(theirs, 1)
    shard1 = jnp.concatenate([after(near1, theirs), far1], axis=2)
    mine = back(after(meta, theirs, shard1), ds1, ds2, units, M_HERE + 1)

    def last_doubling(meta, shard):
        mine, theirs = join(meta, shard, over_dp(shard, 1))
        moved = over_dp(theirs, 0)
        return [mine, over_dp(mine, 0), over_gate(theirs, 1), over_gate(moved, 1)]

    near2, far2 = gathered(after(meta, mine, far_part[0]), M_H2, True, stay2, step2)
    shard1 = last_steps(shard1, near2)
    shard2 = last_steps(jnp.concatenate([after(near2, shard1), far2], axis=2))
    parts1 = last_doubling(after(meta, shard2), shard1)
    dn, row_sums, col_sums = tail_sums(after(meta, parts1[0]), mine, got, far_part, own_x, mu, inv, ln_gain)
    parts2 = last_doubling(after(meta, dn, parts1[1]), shard2)
    for delta in (1, 2):
        row_sums = row_sums + over_gate(row_sums, delta)
    dinputs = tail(after(meta, parts2[1]), dn, row_sums, own_x, mu, inv, ln_gain, direct, features)

    totals = jnp.concatenate([col_sums[:2], vecs[:4]], axis=0)
    for step in range(bits):
        if step == bits - 1:
            totals = after(totals, dinputs)
        totals = totals + lax.ppermute(totals, "dp", [(d, d ^ (1 << step)) for d in range(n_dp)])

    grad_weight = place(after(meta, dinputs), parts1, parts2, n_dp, features, weight.shape[1])
    return (
        hidden.reshape(rows, tokens, channels),
        dinputs.reshape(rows, tokens, channels),
        grad_weight,
        totals[0],
        totals[1],
        totals[2],
        totals[3],
        totals[4],
        totals[5],
    )


def solution(mesh):
    return jax.shard_map(
        functools.partial(shards, mesh.shape["dp"], mesh.shape["gate"]),
        mesh=mesh,
        in_specs=(
            P("dp", None, None),
            P(None, "gate"),
            P(),
            P(),
            P("gate"),
            P("gate"),
            P("gate"),
            P("gate"),
            P("dp", None),
            P("dp", None),
            P("dp", None, "gate"),
        ),
        out_specs=(
            P("dp", None, "gate"),
            P("dp", None, "gate"),
            P(None, "gate"),
            P("gate"),
            P("gate"),
            P("gate"),
            P("gate"),
            P("gate"),
            P("gate"),
        ),
        check_vma=False,
    )
```

```python
import functools

import jax
import jax.numpy as jnp
from jax import lax
from jax.experimental import pallas as pl
from jax.experimental.pallas import tpu as pltpu
from jax.sharding import PartitionSpec as P

epsilon = 1e-05
F32 = jnp.float32
BF16 = jnp.bfloat16
LANES = 128
VMEM_LIMIT = 60 * 1024 * 1024
COVER = 20
FIRST = 2


def call(kernel, meta, args, grid, in_specs, out_specs, out_shape, scratch=(), aliases=None, cost=None):
    return pl.pallas_call(
        kernel,
        grid_spec=pltpu.PrefetchScalarGridSpec(
            num_scalar_prefetch=1,
            grid=grid,
            in_specs=in_specs,
            out_specs=out_specs,
            scratch_shapes=list(scratch),
        ),
        out_shape=out_shape,
        input_output_aliases=aliases or {},
        compiler_params=pltpu.CompilerParams(
            dimension_semantics=("arbitrary",) * len(grid), vmem_limit_bytes=VMEM_LIMIT
        ),
        cost_estimate=cost,
    )(meta, *args)


def cost(flops, nbytes, trans=0, weight=1):
    return pl.CostEstimate(flops=int(weight * flops), bytes_accessed=int(weight * nbytes), transcendentals=int(trans))


def struct(shape, dtype):
    return jax.ShapeDtypeStruct(shape, dtype)


TILE = 256


def order_matrix():
    row = lax.broadcasted_iota(jnp.int32, (TILE, TILE), 0)
    token = lax.broadcasted_iota(jnp.int32, (TILE, TILE), 1)
    return jnp.where(token == (row % 8) * (TILE // 8) + row // 8, 1.0, 0.0).astype(BF16)


def to_rows(order, value):
    return jnp.dot(order, value, preferred_element_type=F32)


def to_tokens(order, value):
    return lax.dot_general(order, value, (((0,), (0,)), ((), ())), preferred_element_type=F32)


def norm_kernel(
    meta, x_ref, gain_ref, bias_ref, res_ref, pad_ref, out_ref, mu_ref, inv_ref, own_ref, keep_ref, live_ref, PM, XP, S1, S2
):
    @pl.when(pl.program_id(0) == 0)
    def _():
        PM[...] = order_matrix()

    order = PM[...]
    features = x_ref.shape[1]
    groups = features // LANES
    wide = 2 * LANES
    ones = jnp.ones((TILE, LANES), BF16)
    keep_ref[...] = jnp.dot(order * (1 - res_ref[0]).astype(F32).astype(BF16), ones, preferred_element_type=F32)
    live_ref[...] = jnp.dot(order * pad_ref[0].astype(F32).astype(BF16), ones, preferred_element_type=F32)
    shift = None
    first = second = None
    for g in range(0, features, wide):
        value = to_rows(order, x_ref[:, g : g + wide])
        XP[:, g : g + wide] = value
        if shift is None:
            shift = jnp.broadcast_to(value[:, 0:1], (TILE, LANES))
            S1[...] = shift
        one, two = value[:, :LANES] - shift, value[:, LANES:] - shift
        first = one + two if first is None else first + (one + two)
        squares = one * one + two * two
        second = squares if second is None else second + squares
    drift = jnp.sum(first, axis=1, keepdims=True) * (1.0 / features)
    spread = jnp.sum(second, axis=1, keepdims=True) * (1.0 / features) - drift * drift
    mu_ref[...] = shift + drift
    inv_ref[...] = jnp.broadcast_to(lax.rsqrt(jnp.maximum(spread, 0.0) + epsilon), inv_ref.shape)
    tall = 16

    def scaled(i, carry):
        rows = pl.ds(pl.multiple_of(i * tall, tall), tall)
        mean = mu_ref[rows, :]
        scale = inv_ref[rows, :]
        for g in range(groups):
            at = slice(g * LANES, (g + 1) * LANES)
            value = (XP[rows, at] - mean) * scale * gain_ref[0:1, at] + bias_ref[0:1, at]
            out_ref[rows, at] = value.astype(BF16)
        return carry

    lax.fori_loop(0, TILE // tall, scaled, 0, unroll=2)
    channels = own_ref.shape[1]
    own_ref[...] = XP[:, pl.ds(pl.multiple_of(meta[M_GATE] * channels, channels), channels)].astype(BF16)


def norm(meta, x, gain, bias, resets, padding, channels):
    tokens, features = x.shape
    tiles = tokens // TILE
    row = pl.BlockSpec((TILE, features), lambda t, m: (t, 0))
    whole = pl.BlockSpec((1, features), lambda t, m: (0, 0))
    flag = pl.BlockSpec((1, 1, TILE), lambda t, m: (t, 0, 0))
    stat = pl.BlockSpec((TILE, LANES), lambda t, m: (t, 0))
    stats = struct((tokens, LANES), F32)
    return call(
        norm_kernel,
        meta,
        (x, gain[None], bias[None], resets.reshape(tiles, 1, TILE), padding.reshape(tiles, 1, TILE)),
        (tiles,),
        [row, whole, whole, flag, flag],
        [row, stat, stat, pl.BlockSpec((TILE, channels), lambda t, m: (t, 0)), stat, stat],
        [struct(x.shape, BF16), stats, stats, struct((tokens, channels), BF16), stats, stats],
        scratch=[pltpu.VMEM((TILE, TILE), BF16), pltpu.VMEM((TILE, features), F32)] + [pltpu.VMEM((TILE, LANES), F32)] * 2,
        cost=cost(8 * tokens * features, 4 * tokens * features, weight=COVER),
    )


def column_of(meta, table, plane, block):
    blk = block ^ meta[M_CORE] if plane == 2 else block
    return pl.multiple_of((blk * 3 + meta[table + plane]) * LANES, LANES)


def cut_kernel(widths, meta, *refs):
    for n, width in enumerate(widths):
        out_ref = refs[sum(widths) + n]
        for b in range(width):
            out_ref[:, b * LANES : (b + 1) * LANES] = refs[sum(widths[:n]) + b][...]


def cut(meta, weight, pieces, tb=512):
    rows = weight.shape[0]
    widths = [width for _, width in pieces]
    specs = [
        pl.BlockSpec((tb, LANES), lambda t, m, at=at, b=b: (t, m[at] + b)) for at, width in pieces for b in range(width)
    ]
    return call(
        functools.partial(cut_kernel, widths),
        meta,
        [weight] * len(specs),
        (rows // tb,),
        specs,
        [pl.BlockSpec((tb, width * LANES), lambda t, m: (t, 0)) for width in widths],
        [struct((rows, width * LANES), BF16) for width in widths],
        cost=cost(0, 4 * rows * LANES * sum(widths)),
    )


def unit_specs(units, rows, row_of):
    return [pl.BlockSpec((rows, LANES), lambda *i, at=at, b=b: (row_of(*i), (i[-1][at] if at else 0) + b)) for _, at, b in units]


def gather_units(meta, table, refs, W, base):
    for n, ref in enumerate(refs):
        at = pl.multiple_of(base + column_of(meta, table, n // 2, n % 2), LANES)
        W[:, pl.ds(at, LANES)] = ref[...]


def project_kernel(table, meta, normed_ref, *refs):
    out_ref, W = refs[-2:]

    @pl.when(pl.program_id(0) == 0)
    def _():
        gather_units(meta, table, refs[:6], W, 0)

    out_ref[...] = jnp.dot(normed_ref[...], W[...], preferred_element_type=F32).astype(BF16)


def project(meta, table, normed, units, tb=512):
    tokens, features = normed.shape
    columns = 6 * LANES
    return call(
        functools.partial(project_kernel, table),
        meta,
        [normed] + [array for array, _, _ in units],
        (tokens // tb,),
        [pl.BlockSpec((tb, features), lambda t, m: (t, 0))] + unit_specs(units, features, lambda t, m: 0),
        pl.BlockSpec((tb, columns), lambda t, m: (t, 0)),
        struct((tokens, columns), BF16),
        scratch=[pltpu.VMEM((features, columns), BF16)],
        cost=cost(2 * tokens * features * columns, 2 * tokens * (features + 2 * columns), weight=COVER),
    )


def sigmoid(z):
    return 0.5 * jnp.tanh(0.5 * z) + 0.5


def scan_kernel(meta, u_ref, x_ref, g_ref, keep_ref, live_ref, prm_ref, *refs):
    (hid_ref, ds_ref, direct_ref, vec_ref, PM, A, B, FG, R, PV, GL, XF, UT, HP, CE, PE, CI, EI) = refs[-18:]
    length = x_ref.shape[0]
    tiles = length // TILE
    seg = TILE // 8
    rows_in = 64
    each = TILE // rows_in
    groups = rows_in // 8
    pf, pr, bf, br = (jnp.broadcast_to(prm_ref[i : i + 1, :], (rows_in, LANES)) for i in range(4))

    @pl.when(pl.program_id(0) == 0)
    def _():
        PM[...] = order_matrix()

    order = PM[...]
    for q in range(tiles):
        GL[q * TILE : (q + 1) * TILE, :] = to_rows(order, g_ref[q * TILE : (q + 1) * TILE, :])

    zeros = jnp.zeros((8, LANES), F32)
    ones = jnp.ones((8, LANES), F32)

    def rows_at(i):
        return pl.ds(pl.multiple_of(i * rows_in, rows_in), rows_in)

    def tile_at(i):
        return pl.ds(pl.multiple_of((i // each) * 8, 8), 8)

    def gates(i, carry):
        rows = rows_at(i)
        x = x_ref[rows, :].astype(F32)
        ut = u_ref[rows, 0:LANES].astype(F32)
        forget = sigmoid(u_ref[rows, LANES : 2 * LANES].astype(F32) + pf * x + bf)
        reset = sigmoid(u_ref[rows, 2 * LANES :].astype(F32) + pr * x + br)
        a = forget * keep_ref[rows, :]
        b = (1.0 - forget) * ut
        gl = GL[rows, :] * live_ref[rows, :]
        d = gl * reset
        XF[rows, :] = x
        UT[rows, :] = ut
        FG[rows, :] = forget
        R[rows, :] = reset
        A[rows, :] = a
        B[rows, :] = b
        GL[rows, :] = gl
        fresh = i % each == 0
        c, p, e = (jnp.where(fresh, start, old) for start, old in zip((zeros, ones, zeros), carry))
        for j in range(groups):
            at = slice(8 * j, 8 * j + 8)
            c = a[at] * c + b[at]
            p = a[at] * p
            e = e + p * d[at]
        CE[tile_at(i), :] = c
        PE[tile_at(i), :] = p
        EI[tile_at(i), :] = e
        return (c, p, e)

    lax.fori_loop(0, tiles * each, gates, (zeros, ones, zeros))

    count = 8 * tiles
    c = jnp.zeros((1, LANES), F32)
    e = jnp.zeros((1, LANES), F32)
    for j in range(count):
        CI[j : j + 1, :] = c
        c = CE[j : j + 1, :] + PE[j : j + 1, :] * c
        r = count - 1 - j
        own = EI[r : r + 1, :]
        EI[r : r + 1, :] = e
        e = own + PE[r : r + 1, :] * e

    def forward(i, carry):
        out = []
        for q in range(tiles):
            rows = pl.ds(pl.multiple_of(q * TILE + i * 8, 8), 8)
            PV[rows, :] = carry[q]
            out.append(A[rows, :] * carry[q] + B[rows, :])
        return tuple(out)

    lax.fori_loop(0, seg, forward, tuple(CI[8 * q : 8 * q + 8, :] for q in range(tiles)), unroll=4)

    def fold(v):
        return v.reshape(groups, 8, LANES).sum(axis=0)

    def grads(n, carry):
        i = tiles * each - 1 - n
        rows = rows_at(i)
        e, s0, s1, s2, s3 = carry
        e = jnp.where(n % each == 0, EI[tile_at(i), :], e)
        g = GL[rows, :]
        reset = R[rows, :]
        a = A[rows, :]
        d = g * reset
        dcs = [None] * groups
        for j in reversed(range(groups)):
            at = slice(8 * j, 8 * j + 8)
            dcs[j] = d[at] + e
            e = a[at] * dcs[j]
        dc = jnp.concatenate(dcs, axis=0)
        x = XF[rows, :]
        forget = FG[rows, :]
        prev = PV[rows, :]
        gap = a * prev + B[rows, :] - x
        HP[rows, :] = (live_ref[rows, :] * (x + reset * gap)).astype(BF16)
        rest = 1.0 - reset
        dreset = g * gap * (reset * rest)
        dtilde = dc * (1.0 - forget)
        dforget = dtilde * forget * (prev * keep_ref[rows, :] - UT[rows, :])
        ds_ref[rows, 0:LANES] = dtilde.astype(BF16)
        ds_ref[rows, LANES : 2 * LANES] = dforget.astype(BF16)
        ds_ref[rows, 2 * LANES :] = dreset.astype(BF16)
        direct_ref[rows, :] = (g * rest + dforget * pf + dreset * pr).astype(BF16)
        return (e, s0 + fold(dforget * x), s1 + fold(dreset * x), s2 + fold(dforget), s3 + fold(dreset))

    sums = lax.fori_loop(0, tiles * each, grads, (zeros,) * 5)[1:]
    for n, s in enumerate(sums):
        vec_ref[n : n + 1, :] = jnp.sum(s, axis=0, keepdims=True)
    vec_ref[4:8, :] = jnp.zeros((4, LANES), F32)
    for q in range(tiles):
        at = slice(q * TILE, (q + 1) * TILE)
        hid_ref[at, :] = to_tokens(order, HP[at, :]).astype(BF16)


def scan(meta, half, u, x, grad, keep, live, params, earlier):
    length, channels = x.shape
    blocks = u.shape[1] // (3 * LANES)
    col = lambda k, m: (0, m[half] * blocks + k)
    tall = (length, LANES)
    chunk = pl.BlockSpec((length, 3 * LANES), lambda k, m: (0, k))
    fixed = pl.BlockSpec(tall, lambda k, m: (0, 0))
    own = pl.BlockSpec(tall, col)
    small = pl.BlockSpec((8, LANES), col)
    in_specs = [chunk, own, own, fixed, fixed, small]
    args = [u, x, grad, keep, live, params]
    aliases = None
    if earlier is not None:
        aliases = {len(args) + 1: 0, len(args) + 2: 2, len(args) + 3: 3}
        args += list(earlier)
        in_specs += [pl.BlockSpec(memory_space=pl.ANY)] * 3
    ends = pltpu.VMEM((8 * length // TILE, LANES), F32)
    return call(
        scan_kernel,
        meta,
        args,
        (blocks,),
        in_specs,
        [own, chunk, own, small],
        [
            struct((length, channels), BF16),
            struct(u.shape, BF16),
            struct((length, channels), BF16),
            struct((8, channels), F32),
        ],
        scratch=[pltpu.VMEM((TILE, TILE), BF16)]
        + [pltpu.VMEM(tall, F32)] * 8
        + [pltpu.VMEM(tall, BF16)]
        + [ends] * 4,
        aliases=aliases,
        cost=cost(60 * length * channels // 2, 9 * length * channels, length * channels, weight=COVER),
    )


def wgrad_kernel(meta, normed_ref, ds_ref, a_ref, b_ref):
    first = pl.program_id(0) < pl.num_programs(0) // 2
    dims = (((0,), (0,)), ((), ()))

    @pl.when(first)
    def _():
        a_ref[...] = lax.dot_general(normed_ref[...], ds_ref[...], dims, preferred_element_type=F32).astype(BF16)

    @pl.when(jnp.logical_not(first))
    def _():
        b_ref[...] = lax.dot_general(normed_ref[...], ds_ref[...], dims, preferred_element_type=F32).astype(BF16)


def wgrad(meta, normed, ds, first, mb=512):
    tokens, features = normed.shape
    width = ds.shape[1]
    rows = features // 4
    steps = rows // mb

    def lhs(i, m):
        return (0, m[first + i // steps] * steps + i % steps)

    return call(
        wgrad_kernel,
        meta,
        (normed, ds),
        (2 * steps,),
        [
            pl.BlockSpec((tokens, mb), lhs),
            pl.BlockSpec((tokens, width), lambda i, m: (0, 0)),
        ],
        [
            pl.BlockSpec((mb, width), lambda i, m: (jnp.minimum(i, steps - 1), 0)),
            pl.BlockSpec((mb, width), lambda i, m: (jnp.maximum(i - steps, 0), 0)),
        ],
        [struct((rows, width), BF16)] * 2,
        cost=cost(4 * tokens * rows * width, 2 * tokens * (features // 2 + width), weight=COVER),
    )


def back_kernel(meta, ds1_ref, ds2_ref, *refs):
    out_ref, W = refs[-2:]
    chunk = ds1_ref.shape[1]

    @pl.when(pl.program_id(0) == 0)
    def _():
        gather_units(meta, M_S1, refs[:6], W, 0)
        gather_units(meta, M_S2, refs[6:12], W, chunk)

    dims = (((1,), (1,)), ((), ()))
    value = lax.dot_general(ds1_ref[...], W[:, :chunk], dims, preferred_element_type=F32)
    value += lax.dot_general(ds2_ref[...], W[:, chunk:], dims, preferred_element_type=F32)
    out_ref[...] = value.astype(BF16)


def back(meta, ds1, ds2, units, at, tb=1024):
    tokens, width = ds1.shape
    features = units[0][0].shape[0]
    block = features // 4
    dspec = pl.BlockSpec((tb, width), lambda t, m: (t, 0))
    return call(
        back_kernel,
        meta,
        [ds1, ds2] + [array for array, _, _ in units],
        (tokens // tb,),
        [dspec, dspec] + unit_specs(units, block, lambda t, m: m[at]),
        pl.BlockSpec((tb, block), lambda t, m: (t, 0)),
        struct((tokens, block), BF16),
        scratch=[pltpu.VMEM((block, 2 * width), BF16)],
        cost=cost(4 * tokens * block * width, 4 * tokens * width, weight=COVER),
    )


def unit_of(x_ref, mu_ref, inv_ref):
    repeat = x_ref.shape[1] // LANES
    mu = jnp.concatenate([mu_ref[...]] * repeat, axis=1)
    inv = jnp.concatenate([inv_ref[...]] * repeat, axis=1)
    return (x_ref[...].astype(F32) - mu) * inv, inv


def lane_sums(value):
    part = value[:, :LANES]
    for g in range(1, value.shape[1] // LANES):
        part = part + value[:, g * LANES : (g + 1) * LANES]
    return jnp.sum(part.T, axis=0, keepdims=True)


def tail_sums_kernel(meta, k_ref, rc_ref, r1_ref, r2_ref, x_ref, mu_ref, inv_ref, gain_ref, dn_ref, row_ref, col_ref):
    unit, _ = unit_of(x_ref, mu_ref, inv_ref)
    early = pl.program_id(0) < pl.num_programs(0) * FIRST // 8
    far = jnp.where(early, r1_ref[...].astype(F32), r2_ref[...].astype(F32))
    dn = k_ref[...].astype(F32) + rc_ref[...].astype(F32) + far
    dn_ref[...] = dn
    gu = dn * gain_ref[...]
    row_ref[0:1, :] = lane_sums(gu)
    row_ref[1:2, :] = lane_sums(gu * unit)
    row_ref[2:8, :] = jnp.zeros((6, row_ref.shape[1]), F32)

    @pl.when(pl.program_id(0) == 0)
    def _():
        col_ref[...] = jnp.zeros_like(col_ref)

    col_ref[0:1, :] += jnp.sum(dn * unit, axis=0, keepdims=True)
    col_ref[1:2, :] += jnp.sum(dn, axis=0, keepdims=True)


def tail_sums(meta, keep, got, far, x, mu, inv, gain, tb=256):
    tokens, channels = x.shape
    first = tokens // tb * FIRST // 8
    wide = pl.BlockSpec((tb, channels), lambda t, m: (t, 0))
    stat = pl.BlockSpec((tb, LANES), lambda t, m: (t, 0))
    return call(
        tail_sums_kernel,
        meta,
        (keep, got, *far, x, mu, inv, gain[None]),
        (tokens // tb,),
        [
            wide,
            wide,
            pl.BlockSpec((tb, channels), lambda t, m: (jnp.minimum(t, first - 1), 0)),
            pl.BlockSpec((tb, channels), lambda t, m: (jnp.maximum(t - first, 0), 0)),
            wide,
            stat,
            stat,
            pl.BlockSpec((1, channels), lambda t, m: (0, m[M_GATE])),
        ],
        [
            wide,
            pl.BlockSpec((8, tb), lambda t, m: (0, t)),
            pl.BlockSpec((8, channels), lambda t, m: (0, 0)),
        ],
        [struct((tokens, channels), F32), struct((8, tokens), F32), struct((8, channels), F32)],
        cost=cost(20 * tokens * channels, 12 * tokens * channels, weight=COVER),
    )


def tail_kernel(features, meta, dn_ref, row_ref, x_ref, mu_ref, inv_ref, gain_ref, direct_ref, out_ref, PM):
    @pl.when(pl.program_id(0) == 0)
    def _():
        PM[...] = order_matrix()

    unit, inv = unit_of(x_ref, mu_ref, inv_ref)
    repeat = x_ref.shape[1] // LANES
    tb = x_ref.shape[0]

    def mean(n):
        row = row_ref[n : n + 1, :] * (1.0 / features)
        return jnp.concatenate([jnp.broadcast_to(row, (LANES, tb)).T] * repeat, axis=1)

    gu = dn_ref[...] * gain_ref[...]
    value = (inv * (gu - mean(0) - unit * mean(1)) + direct_ref[...].astype(F32)).astype(BF16)
    for q in range(tb // TILE):
        at = slice(q * TILE, (q + 1) * TILE)
        out_ref[at, :] = to_tokens(PM[...], value[at]).astype(BF16)


def tail(meta, dn, rows, x, mu, inv, gain, direct, features, tb=512):
    tokens, channels = dn.shape
    wide = pl.BlockSpec((tb, channels), lambda t, m: (t, 0))
    stat = pl.BlockSpec((tb, LANES), lambda t, m: (t, 0))
    return call(
        functools.partial(tail_kernel, features),
        meta,
        (dn, rows, x, mu, inv, gain[None], direct),
        (tokens // tb,),
        [
            wide,
            pl.BlockSpec((rows.shape[0], tb), lambda t, m: (0, t)),
            wide,
            stat,
            stat,
            pl.BlockSpec((1, channels), lambda t, m: (0, m[M_GATE])),
            wide,
        ],
        wide,
        struct((tokens, channels), BF16),
        scratch=[pltpu.VMEM((TILE, TILE), BF16)],
        cost=cost(10 * tokens * channels, 12 * tokens * channels),
    )


def halve_kernel(meta, *refs):
    ins, (away_ref, stay_ref) = refs[:-2], refs[-2:]
    for n, out_ref in ((0, away_ref), (1, stay_ref)):
        part = ins[n * len(ins) // 2 : (n + 1) * len(ins) // 2]
        if len(part) == 4:
            for o in range(2):
                out_ref[o] = (part[o][...].astype(F32) + part[2 + o][...].astype(F32)).astype(BF16)
        else:
            out_ref[...] = (part[0][...].astype(F32) + part[1][...].astype(F32)).astype(BF16)


def halve(meta, at, kept, got, parts=2):
    if len(kept) == 2:
        rows, width = kept[0].shape
        lead = ()
    else:
        lead, rows, width = kept[0].shape
        lead = (lead,)
    half = rows // 2
    tb = half // parts
    zeros = (0,) * len(lead)
    specs, args = [], []
    for side in range(2):
        for array in (*kept, *got):
            specs.append(
                pl.BlockSpec((*lead, tb, width), lambda i, m, side=side: (*zeros, (m[at] ^ (1 - side)) * parts + i, 0))
            )
            args.append(array)
    out = pl.BlockSpec((2, tb, width), lambda i, m: (0, i, 0))
    return call(
        halve_kernel,
        meta,
        args,
        (parts,),
        specs,
        [out, out],
        [struct((2, half, width), BF16)] * 2,
        cost=cost(4 * rows * width, 12 * rows * width),
    )


def split_kernel(late, half, meta, a_ref, b_ref, near_ref, far_ref):
    core = meta[M_CORE]
    h = meta[half]
    pair_ref, single_ref = (far_ref, near_ref) if late else (near_ref, far_ref)

    def take(owner, stream, block):
        col = pl.ds(pl.multiple_of((block * 3 + stream) * LANES, LANES), LANES)
        return (a_ref[owner, :, col].astype(F32) + b_ref[owner, :, col].astype(F32)).astype(BF16)

    for store in range(2):
        k = core ^ store
        for owner in range(2):
            for block in range(2):
                at = (2 * owner + block) * LANES
                pair_ref[store, :, at : at + LANES] = take(owner, k + h, block)
            single_ref[store, :, owner * LANES : (owner + 1) * LANES] = take(owner, 2 * (1 - h), k)


def split(meta, half, late, kept, got):
    _, rows, width = kept.shape
    pair, single = 4 * LANES, 2 * LANES
    widths = (single, pair) if late else (pair, single)
    whole = pl.BlockSpec((2, rows, width), lambda i, m: (0, 0, 0))
    return call(
        functools.partial(split_kernel, late, half),
        meta,
        (kept, got),
        (1,),
        [whole] * 2,
        [pl.BlockSpec((2, rows, w), lambda i, m: (0, 0, 0)) for w in widths],
        [struct((2, rows, w), BF16) for w in widths],
        cost=cost(2 * rows * width, 12 * rows * width),
    )


def join_kernel(meta, a_ref, b_ref, *outs):
    rows = a_ref.shape[1]
    for n, out_ref in enumerate(outs):
        out_ref[:rows, :] = a_ref[n]
        out_ref[rows:, :] = b_ref[n]


def join(meta, a, b):
    _, rows, width = a.shape
    whole = pl.BlockSpec((2, rows, width), lambda i, m: (0, 0, 0))
    out = pl.BlockSpec((2 * rows, width), lambda i, m: (0, 0))
    return call(
        join_kernel,
        meta,
        (a, b),
        (1,),
        [whole] * 2,
        [out] * 2,
        [struct((2 * rows, width), BF16)] * 2,
        cost=cost(0, 16 * rows * width),
    )


def place_kernel(blocks, meta, *refs):
    out_ref = refs[-1]
    step = pl.program_id(0)
    piece = out_ref.shape[1] // 4
    unit = piece // 3
    rows = out_ref.shape[0] // blocks
    core = meta[M_CORE]
    for stream in range(2):
        for part in range(2):

            @pl.when(step == stream * 2 + part)
            def _(stream=stream, part=part):
                one = refs[stream * 2 + part]
                two = refs[4 + stream * 2 + part]
                inner = meta[M_RHO + stream] % blocks

                def put(owner, single, src, col):
                    base = meta[M_OWN + (owner ^ stream)] * piece
                    wide = unit if single else 2 * unit
                    at = base + (jnp.where(core == 0, 2 * unit, 0) if single else core * unit)
                    at = pl.ds(pl.multiple_of(at, LANES), wide)
                    for j in range(blocks):
                        to = pl.ds(pl.multiple_of((inner ^ j) * rows, rows), rows)
                        out_ref[to, at] = src[j * rows : (j + 1) * rows, col : col + wide].astype(F32)

                put(0, False, one, 0)
                put(1, False, one, 2 * unit)
                put(2, True, one, 4 * unit)
                put(3, True, one, 5 * unit)
                put(0, True, two, 0)
                put(1, True, two, unit)
                put(2, False, two, 2 * unit)
                put(3, False, two, 4 * unit)


def place(meta, parts1, parts2, n_dp, features, columns):
    blocks = n_dp // 2
    whole = pl.BlockSpec((features // 4, columns // 2), lambda i, m: (0, 0))

    def where_to(i, m):
        stream = i // 2
        return ((m[M_CORE] ^ stream) * 2 + (i % 2 ^ m[M_RHO + stream] // blocks), 0)

    return call(
        functools.partial(place_kernel, blocks),
        meta,
        (*parts1, *parts2),
        (4,),
        [whole] * 8,
        pl.BlockSpec((features // 4, columns), where_to),
        struct((features, columns), F32),
        cost=cost(features * columns, 6 * features * columns, weight=COVER),
    )


M_GATE, M_CORE, M_H1, M_H2 = 0, 1, 2, 3
M_S1, M_S2 = 4, 7
M_SEND, M_KEEP = 10, 12
M_FAR, M_HERE = 14, 16
M_OWN, M_RHO = 18, 22
M_TO2, M_TO3, M_NEAR, M_LATE2, M_LATE3 = 24, 25, 26, 27, 28
M_PAIR, M_SINGLE, M_GOT_PAIR, M_GOT_SINGLE = 29, 30, 31, 32
M_BIT = 33


def shards(
    n_dp,
    n_gate,
    inputs,
    weight,
    ln_gain,
    ln_bias,
    forget_peep,
    reset_peep,
    forget_bias,
    reset_bias,
    resets,
    padding,
    grad_out,
):
    rows, tokens, features = inputs.shape
    assert rows == 1 and n_gate == 4
    channels = forget_peep.shape[0]
    assert channels == 4 * LANES
    bits = n_dp.bit_length() - 1
    assert 1 << bits == n_dp
    gate = lax.axis_index("gate")
    dp = lax.axis_index("dp")
    hi, core = gate // 2, gate % 2
    other = 1 - core

    orders = [list(range(bits)), [1, 0, *range(2, bits)]]

    def bit(stream, step):
        return (dp >> jnp.where(stream == 0, orders[0][step], orders[1][step])) & 1

    def rho(stream):
        value = 0
        for step in range(bits):
            value = value * 2 + bit(stream, step)
        return value

    def streams(h):
        return [core + h, other + h, 2 * (1 - h)]

    h1, h2 = hi, 1 - hi
    far = (1 - hi) * 2
    single, pair = 2 * other, core
    meta = jnp.stack(
        [gate, core, h1, h2, *streams(h1), *streams(h2)]
        + [other * 2 + 1 - bit(other, 0), core * 2 + 1 - bit(core, 0)]
        + [other * 2 + bit(other, 0), core * 2 + bit(core, 0)]
        + [far + other, far + core, hi * 2 + other, hi * 2 + core]
        + [gate, hi * 2 + other, far + core, far + other]
        + [rho(core), rho(other)]
        + [(far + core) * 3 + single, (far + other) * 3 + single, (hi * 2 + other) * 3]
        + [(far + core) * 3 + pair, (far + other) * 3 + pair]
        + [gate * 3 + pair, gate * 3 + single, other, 2 * core]
        + [bit(core, step) for step in range(bits)]
    ).astype(jnp.int32)

    def over_gate(value, delta):
        return lax.ppermute(value, "gate", [(g, g ^ delta) for g in range(n_gate)])

    def over_dp(value, step):
        pairs = [
            (d * n_gate + g, (d ^ (1 << orders[g % 2][step])) * n_gate + g) for d in range(n_dp) for g in range(n_gate)
        ]
        return lax.ppermute(value, ("dp", "gate"), pairs)

    def after(value, *others):
        return lax.optimization_barrier((value, *others))[0]

    x = inputs.reshape(tokens, features)
    grad = grad_out.reshape(tokens, channels)
    params = jnp.concatenate(
        [jnp.stack([forget_peep, reset_peep, forget_bias, reset_bias]), jnp.zeros((4, channels), F32)]
    )

    to2, to3, near = cut(meta, weight, [(M_TO2, 1), (M_TO3, 1), (M_NEAR, 3)])
    sent2, sent3, near = over_gate(to2, 2), over_gate(to3, 3), over_gate(near, 1)
    normed, mu, inv, own_x, keep, live = norm(
        after(meta, to2, to3), x, ln_gain, ln_bias, resets, padding, channels
    )
    away2, away3 = cut(after(meta, normed), weight, [(M_LATE2, 2), (M_LATE3, 2)])
    late2, late3 = over_gate(away2, 2), over_gate(away3, 3)
    units1 = [(weight, M_PAIR, 0), (weight, M_PAIR, 1), (near, M_GOT_PAIR, 0), (near, M_GOT_PAIR, 1)]
    units1 += [(sent2, None, 0), (sent3, None, 0)]
    units2 = [(late2, None, 0), (late2, None, 1), (late3, None, 0), (late3, None, 1)]
    units2 += [(weight, M_SINGLE, 0), (near, M_GOT_SINGLE, 0)]
    units = units1 + units2

    def first_sends(meta, ds):
        theirs, mine = wgrad(meta, normed, ds, M_SEND)
        return mine, [over_dp(mine, 0), over_dp(over_gate(theirs, 1), 0)]

    def first_keeps(meta, ds):
        theirs, mine = wgrad(meta, normed, ds, M_KEEP)
        return [mine, over_gate(theirs, 1)]

    def gathered(meta, half, late, kept, got):
        near, far = split(meta, half, late, kept, got)
        return near, over_gate(far, 2)

    def last_steps(shard, *others):
        for step in reversed(range(2, bits)):
            shard = jnp.concatenate([after(shard, *others), over_dp(shard, step)], axis=1)
        return shard

    u1 = project(after(meta, away2, away3), M_S1, normed, units1)
    hidden, ds1, direct, vecs = scan(meta, M_H1, u1, own_x, grad, keep, live, params, None)
    mine1, got1 = first_sends(meta, ds1)
    kept1 = first_keeps(after(meta, mine1), ds1)
    u2 = project(after(meta, kept1[0]), M_S2, normed, units2)
    away1, stay1 = halve(after(meta, u2), M_BIT + 1, kept1, got1)
    step1 = over_dp(away1, 1)
    hidden, ds2, direct, vecs = scan(
        after(meta, away1), M_H2, u2, own_x, grad, keep, live, params, (hidden, direct, vecs)
    )
    for step in range(2, bits):
        away1, stay1 = halve(after(meta, ds2), M_BIT + step, [stay1], [step1])
        step1 = over_dp(away1, step)
    mine2, got2 = first_sends(after(meta, away1), ds2)
    kept2 = first_keeps(after(meta, mine2), ds2)
    far_theirs = back(after(meta, kept2[0]), ds1, ds2, units, M_FAR)
    far_got = over_gate(far_theirs, 1)
    away2, stay2 = halve(after(meta, far_theirs), M_BIT + 1, kept2, got2)
    step2 = over_dp(away2, 1)
    near1, far1 = gathered(after(meta, away2), M_H1, False, stay1, step1)
    far_mine = back(after(meta, near1), ds1, ds2, units, M_FAR + 1)
    for step in range(2, bits):
        away2, stay2 = halve(after(meta, far_mine), M_BIT + step, [stay2], [step2])
        step2 = over_dp(away2, step)
    far_mine = after(far_mine, away2)
    cut_at = tokens * FIRST // 8
    far_send = [
        (far_mine[at].astype(F32) + far_got[at].astype(F32)).astype(BF16) for at in (slice(cut_at), slice(cut_at, None))
    ]
    far_part = [over_gate(part, 2) for part in far_send]
    theirs = back(after(meta, away2, *far_send), ds1, ds2, units, M_HERE)
    got = over_gate(theirs, 1)
    shard1 = jnp.concatenate([after(near1, theirs), far1], axis=2)
    mine = back(after(meta, theirs, shard1), ds1, ds2, units, M_HERE + 1)

    def last_doubling(meta, shard):
        mine, theirs = join(meta, shard, over_dp(shard, 1))
        moved = over_dp(theirs, 0)
        return [mine, over_dp(mine, 0), over_gate(theirs, 1), over_gate(moved, 1)]

    near2, far2 = gathered(after(meta, mine, far_part[0]), M_H2, True, stay2, step2)
    shard1 = last_steps(shard1, near2)
    shard2 = last_steps(jnp.concatenate([after(near2, shard1), far2], axis=2))
    parts1 = last_doubling(after(meta, shard2), shard1)
    parts2 = last_doubling(after(meta, parts1[0]), shard2)
    dn, row_sums, col_sums = tail_sums(after(meta, parts2[0], parts1[1]), mine, got, far_part, own_x, mu, inv, ln_gain)
    for delta in (1, 2):
        row_sums = row_sums + over_gate(row_sums, delta)
    dinputs = tail(after(meta, parts2[1]), dn, row_sums, own_x, mu, inv, ln_gain, direct, features)

    totals = jnp.concatenate([col_sums[:2], vecs[:4]], axis=0)
    grad_weight = place(after(meta, dinputs), parts1, parts2, n_dp, features, weight.shape[1])
    for step in range(bits):
        last = step == bits - 1
        got = lax.ppermute(
            after(totals, dinputs) if last else totals, "dp", [(d, d ^ (1 << step)) for d in range(n_dp)]
        )
        totals = (after(totals, grad_weight) if last else totals) + got
    return (
        hidden.reshape(rows, tokens, channels),
        dinputs.reshape(rows, tokens, channels),
        grad_weight,
        totals[0],
        totals[1],
        totals[2],
        totals[3],
        totals[4],
        totals[5],
    )


def solution(mesh):
    return jax.shard_map(
        functools.partial(shards, mesh.shape["dp"], mesh.shape["gate"]),
        mesh=mesh,
        in_specs=(
            P("dp", None, None),
            P(None, "gate"),
            P(),
            P(),
            P("gate"),
            P("gate"),
            P("gate"),
            P("gate"),
            P("dp", None),
            P("dp", None),
            P("dp", None, "gate"),
        ),
        out_specs=(
            P("dp", None, "gate"),
            P("dp", None, "gate"),
            P(None, "gate"),
            P("gate"),
            P("gate"),
            P("gate"),
            P("gate"),
            P("gate"),
            P("gate"),
        ),
        check_vma=False,
    )
```

```python
import functools

import jax
import jax.numpy as jnp
from jax import lax
from jax.experimental import pallas as pl
from jax.experimental.pallas import tpu as pltpu
from jax.sharding import PartitionSpec as P

epsilon = 1e-05
F32 = jnp.float32
BF16 = jnp.bfloat16
LANES = 128
VMEM_LIMIT = 60 * 1024 * 1024
COVER = 20
FIRST = 2


def call(kernel, meta, args, grid, in_specs, out_specs, out_shape, scratch=(), aliases=None, cost=None):
    return pl.pallas_call(
        kernel,
        grid_spec=pltpu.PrefetchScalarGridSpec(
            num_scalar_prefetch=1,
            grid=grid,
            in_specs=in_specs,
            out_specs=out_specs,
            scratch_shapes=list(scratch),
        ),
        out_shape=out_shape,
        input_output_aliases=aliases or {},
        compiler_params=pltpu.CompilerParams(
            dimension_semantics=("arbitrary",) * len(grid), vmem_limit_bytes=VMEM_LIMIT
        ),
        cost_estimate=cost,
    )(meta, *args)


def cost(flops, nbytes, trans=0, weight=1):
    return pl.CostEstimate(flops=int(weight * flops), bytes_accessed=int(weight * nbytes), transcendentals=int(trans))


def struct(shape, dtype):
    return jax.ShapeDtypeStruct(shape, dtype)


TILE = 256


def order_matrix():
    row = lax.broadcasted_iota(jnp.int32, (TILE, TILE), 0)
    token = lax.broadcasted_iota(jnp.int32, (TILE, TILE), 1)
    return jnp.where(token == (row % 8) * (TILE // 8) + row // 8, 1.0, 0.0).astype(BF16)


def to_rows(order, value):
    return jnp.dot(order, value, preferred_element_type=F32)


def to_tokens(order, value):
    return lax.dot_general(order, value, (((0,), (0,)), ((), ())), preferred_element_type=F32)


def norm_kernel(
    meta, x_ref, gain_ref, bias_ref, res_ref, pad_ref, out_ref, mu_ref, inv_ref, own_ref, keep_ref, live_ref, PM, XP, S1, S2
):
    @pl.when(pl.program_id(0) == 0)
    def _():
        PM[...] = order_matrix()

    order = PM[...]
    features = x_ref.shape[1]
    groups = features // LANES
    wide = 2 * LANES
    ones = jnp.ones((TILE, LANES), BF16)
    keep_ref[...] = jnp.dot(order * (1 - res_ref[0]).astype(F32).astype(BF16), ones, preferred_element_type=F32)
    live_ref[...] = jnp.dot(order * pad_ref[0].astype(F32).astype(BF16), ones, preferred_element_type=F32)
    shift = None
    first = second = None
    for g in range(0, features, wide):
        value = to_rows(order, x_ref[:, g : g + wide])
        XP[:, g : g + wide] = value
        if shift is None:
            shift = jnp.broadcast_to(value[:, 0:1], (TILE, LANES))
            S1[...] = shift
        one, two = value[:, :LANES] - shift, value[:, LANES:] - shift
        first = one + two if first is None else first + (one + two)
        squares = one * one + two * two
        second = squares if second is None else second + squares
    drift = jnp.sum(first, axis=1, keepdims=True) * (1.0 / features)
    spread = jnp.sum(second, axis=1, keepdims=True) * (1.0 / features) - drift * drift
    mu_ref[...] = shift + drift
    inv_ref[...] = jnp.broadcast_to(lax.rsqrt(jnp.maximum(spread, 0.0) + epsilon), inv_ref.shape)
    tall = 16

    def scaled(i, carry):
        rows = pl.ds(pl.multiple_of(i * tall, tall), tall)
        mean = mu_ref[rows, :]
        scale = inv_ref[rows, :]
        for g in range(groups):
            at = slice(g * LANES, (g + 1) * LANES)
            value = (XP[rows, at] - mean) * scale * gain_ref[0:1, at] + bias_ref[0:1, at]
            out_ref[rows, at] = value.astype(BF16)
        return carry

    lax.fori_loop(0, TILE // tall, scaled, 0, unroll=2)
    channels = own_ref.shape[1]
    own_ref[...] = XP[:, pl.ds(pl.multiple_of(meta[M_GATE] * channels, channels), channels)].astype(BF16)


def norm(meta, x, gain, bias, resets, padding, channels):
    tokens, features = x.shape
    tiles = tokens // TILE
    row = pl.BlockSpec((TILE, features), lambda t, m: (t, 0))
    whole = pl.BlockSpec((1, features), lambda t, m: (0, 0))
    flag = pl.BlockSpec((1, 1, TILE), lambda t, m: (t, 0, 0))
    stat = pl.BlockSpec((TILE, LANES), lambda t, m: (t, 0))
    stats = struct((tokens, LANES), F32)
    return call(
        norm_kernel,
        meta,
        (x, gain[None], bias[None], resets.reshape(tiles, 1, TILE), padding.reshape(tiles, 1, TILE)),
        (tiles,),
        [row, whole, whole, flag, flag],
        [row, stat, stat, pl.BlockSpec((TILE, channels), lambda t, m: (t, 0)), stat, stat],
        [struct(x.shape, BF16), stats, stats, struct((tokens, channels), BF16), stats, stats],
        scratch=[pltpu.VMEM((TILE, TILE), BF16), pltpu.VMEM((TILE, features), F32)] + [pltpu.VMEM((TILE, LANES), F32)] * 2,
        cost=cost(8 * tokens * features, 4 * tokens * features, weight=COVER),
    )


def column_of(meta, table, plane, block):
    blk = block ^ meta[M_CORE] if plane == 2 else block
    return pl.multiple_of((blk * 3 + meta[table + plane]) * LANES, LANES)


def cut_kernel(widths, meta, *refs):
    for n, width in enumerate(widths):
        out_ref = refs[sum(widths) + n]
        for b in range(width):
            out_ref[:, b * LANES : (b + 1) * LANES] = refs[sum(widths[:n]) + b][...]


def cut(meta, weight, pieces, tb=512):
    rows = weight.shape[0]
    widths = [width for _, width in pieces]
    specs = [
        pl.BlockSpec((tb, LANES), lambda t, m, at=at, b=b: (t, m[at] + b)) for at, width in pieces for b in range(width)
    ]
    return call(
        functools.partial(cut_kernel, widths),
        meta,
        [weight] * len(specs),
        (rows // tb,),
        specs,
        [pl.BlockSpec((tb, width * LANES), lambda t, m: (t, 0)) for width in widths],
        [struct((rows, width * LANES), BF16) for width in widths],
        cost=cost(0, 4 * rows * LANES * sum(widths)),
    )


def unit_specs(units, rows, row_of):
    return [pl.BlockSpec((rows, LANES), lambda *i, at=at, b=b: (row_of(*i), (i[-1][at] if at else 0) + b)) for _, at, b in units]


def gather_units(meta, table, refs, W, base):
    for n, ref in enumerate(refs):
        at = pl.multiple_of(base + column_of(meta, table, n // 2, n % 2), LANES)
        W[:, pl.ds(at, LANES)] = ref[...]


def project_kernel(table, meta, normed_ref, *refs):
    out_ref, W = refs[-2:]

    @pl.when(pl.program_id(0) == 0)
    def _():
        gather_units(meta, table, refs[:6], W, 0)

    out_ref[...] = jnp.dot(normed_ref[...], W[...], preferred_element_type=F32).astype(BF16)


def project(meta, table, normed, units, tb=512):
    tokens, features = normed.shape
    columns = 6 * LANES
    return call(
        functools.partial(project_kernel, table),
        meta,
        [normed] + [array for array, _, _ in units],
        (tokens // tb,),
        [pl.BlockSpec((tb, features), lambda t, m: (t, 0))] + unit_specs(units, features, lambda t, m: 0),
        pl.BlockSpec((tb, columns), lambda t, m: (t, 0)),
        struct((tokens, columns), BF16),
        scratch=[pltpu.VMEM((features, columns), BF16)],
        cost=cost(2 * tokens * features * columns, 2 * tokens * (features + 2 * columns), weight=COVER),
    )


def sigmoid(z):
    return 0.5 * jnp.tanh(0.5 * z) + 0.5


def scan_kernel(meta, u_ref, x_ref, g_ref, keep_ref, live_ref, prm_ref, *refs):
    (hid_ref, ds_ref, direct_ref, vec_ref, PM, A, B, FG, R, PV, GL, XF, UT, HP, CE, PE, CI, EI) = refs[-18:]
    length = x_ref.shape[0]
    tiles = length // TILE
    seg = TILE // 8
    rows_in = 64
    each = TILE // rows_in
    groups = rows_in // 8
    pf, pr, bf, br = (jnp.broadcast_to(prm_ref[i : i + 1, :], (rows_in, LANES)) for i in range(4))

    @pl.when(pl.program_id(0) == 0)
    def _():
        PM[...] = order_matrix()

    order = PM[...]
    for q in range(tiles):
        GL[q * TILE : (q + 1) * TILE, :] = to_rows(order, g_ref[q * TILE : (q + 1) * TILE, :])

    zeros = jnp.zeros((8, LANES), F32)
    ones = jnp.ones((8, LANES), F32)

    def rows_at(i):
        return pl.ds(pl.multiple_of(i * rows_in, rows_in), rows_in)

    def tile_at(i):
        return pl.ds(pl.multiple_of((i // each) * 8, 8), 8)

    def gates(i, carry):
        rows = rows_at(i)
        x = x_ref[rows, :].astype(F32)
        ut = u_ref[rows, 0:LANES].astype(F32)
        forget = sigmoid(u_ref[rows, LANES : 2 * LANES].astype(F32) + pf * x + bf)
        reset = sigmoid(u_ref[rows, 2 * LANES :].astype(F32) + pr * x + br)
        a = forget * keep_ref[rows, :]
        b = (1.0 - forget) * ut
        gl = GL[rows, :] * live_ref[rows, :]
        d = gl * reset
        XF[rows, :] = x
        UT[rows, :] = ut
        FG[rows, :] = forget
        R[rows, :] = reset
        A[rows, :] = a
        B[rows, :] = b
        GL[rows, :] = gl
        fresh = i % each == 0
        c, p, e = (jnp.where(fresh, start, old) for start, old in zip((zeros, ones, zeros), carry))
        for j in range(groups):
            at = slice(8 * j, 8 * j + 8)
            c = a[at] * c + b[at]
            p = a[at] * p
            e = e + p * d[at]
        CE[tile_at(i), :] = c
        PE[tile_at(i), :] = p
        EI[tile_at(i), :] = e
        return (c, p, e)

    lax.fori_loop(0, tiles * each, gates, (zeros, ones, zeros))

    count = 8 * tiles
    c = jnp.zeros((1, LANES), F32)
    e = jnp.zeros((1, LANES), F32)
    for j in range(count):
        CI[j : j + 1, :] = c
        c = CE[j : j + 1, :] + PE[j : j + 1, :] * c
        r = count - 1 - j
        own = EI[r : r + 1, :]
        EI[r : r + 1, :] = e
        e = own + PE[r : r + 1, :] * e

    def forward(i, carry):
        out = []
        for q in range(tiles):
            rows = pl.ds(pl.multiple_of(q * TILE + i * 8, 8), 8)
            PV[rows, :] = carry[q]
            out.append(A[rows, :] * carry[q] + B[rows, :])
        return tuple(out)

    lax.fori_loop(0, seg, forward, tuple(CI[8 * q : 8 * q + 8, :] for q in range(tiles)), unroll=4)

    def fold(v):
        return v.reshape(groups, 8, LANES).sum(axis=0)

    def grads(n, carry):
        i = tiles * each - 1 - n
        rows = rows_at(i)
        e, s0, s1, s2, s3 = carry
        e = jnp.where(n % each == 0, EI[tile_at(i), :], e)
        g = GL[rows, :]
        reset = R[rows, :]
        a = A[rows, :]
        d = g * reset
        dcs = [None] * groups
        for j in reversed(range(groups)):
            at = slice(8 * j, 8 * j + 8)
            dcs[j] = d[at] + e
            e = a[at] * dcs[j]
        dc = jnp.concatenate(dcs, axis=0)
        x = XF[rows, :]
        forget = FG[rows, :]
        prev = PV[rows, :]
        gap = a * prev + B[rows, :] - x
        HP[rows, :] = (live_ref[rows, :] * (x + reset * gap)).astype(BF16)
        rest = 1.0 - reset
        dreset = g * gap * (reset * rest)
        dtilde = dc * (1.0 - forget)
        dforget = dtilde * forget * (prev * keep_ref[rows, :] - UT[rows, :])
        ds_ref[rows, 0:LANES] = dtilde.astype(BF16)
        ds_ref[rows, LANES : 2 * LANES] = dforget.astype(BF16)
        ds_ref[rows, 2 * LANES :] = dreset.astype(BF16)
        direct_ref[rows, :] = (g * rest + dforget * pf + dreset * pr).astype(BF16)
        return (e, s0 + fold(dforget * x), s1 + fold(dreset * x), s2 + fold(dforget), s3 + fold(dreset))

    sums = lax.fori_loop(0, tiles * each, grads, (zeros,) * 5)[1:]
    for n, s in enumerate(sums):
        vec_ref[n : n + 1, :] = jnp.sum(s, axis=0, keepdims=True)
    vec_ref[4:8, :] = jnp.zeros((4, LANES), F32)
    for q in range(tiles):
        at = slice(q * TILE, (q + 1) * TILE)
        hid_ref[at, :] = to_tokens(order, HP[at, :]).astype(BF16)


def scan(meta, half, u, x, grad, keep, live, params, earlier):
    length, channels = x.shape
    blocks = u.shape[1] // (3 * LANES)
    col = lambda k, m: (0, m[half] * blocks + k)
    tall = (length, LANES)
    chunk = pl.BlockSpec((length, 3 * LANES), lambda k, m: (0, k))
    fixed = pl.BlockSpec(tall, lambda k, m: (0, 0))
    own = pl.BlockSpec(tall, col)
    small = pl.BlockSpec((8, LANES), col)
    in_specs = [chunk, own, own, fixed, fixed, small]
    args = [u, x, grad, keep, live, params]
    aliases = None
    if earlier is not None:
        aliases = {len(args) + 1: 0, len(args) + 2: 2, len(args) + 3: 3}
        args += list(earlier)
        in_specs += [pl.BlockSpec(memory_space=pl.ANY)] * 3
    ends = pltpu.VMEM((8 * length // TILE, LANES), F32)
    return call(
        scan_kernel,
        meta,
        args,
        (blocks,),
        in_specs,
        [own, chunk, own, small],
        [
            struct((length, channels), BF16),
            struct(u.shape, BF16),
            struct((length, channels), BF16),
            struct((8, channels), F32),
        ],
        scratch=[pltpu.VMEM((TILE, TILE), BF16)]
        + [pltpu.VMEM(tall, F32)] * 8
        + [pltpu.VMEM(tall, BF16)]
        + [ends] * 4,
        aliases=aliases,
        cost=cost(60 * length * channels // 2, 9 * length * channels, length * channels, weight=COVER),
    )


def wgrad_kernel(meta, normed_ref, ds_ref, a_ref, b_ref):
    first = pl.program_id(0) < pl.num_programs(0) // 2
    dims = (((0,), (0,)), ((), ()))

    @pl.when(first)
    def _():
        a_ref[...] = lax.dot_general(normed_ref[...], ds_ref[...], dims, preferred_element_type=F32).astype(BF16)

    @pl.when(jnp.logical_not(first))
    def _():
        b_ref[...] = lax.dot_general(normed_ref[...], ds_ref[...], dims, preferred_element_type=F32).astype(BF16)


def wgrad(meta, normed, ds, first, mb=512):
    tokens, features = normed.shape
    width = ds.shape[1]
    rows = features // 4
    steps = rows // mb

    def lhs(i, m):
        return (0, m[first + i // steps] * steps + i % steps)

    return call(
        wgrad_kernel,
        meta,
        (normed, ds),
        (2 * steps,),
        [
            pl.BlockSpec((tokens, mb), lhs),
            pl.BlockSpec((tokens, width), lambda i, m: (0, 0)),
        ],
        [
            pl.BlockSpec((mb, width), lambda i, m: (jnp.minimum(i, steps - 1), 0)),
            pl.BlockSpec((mb, width), lambda i, m: (jnp.maximum(i - steps, 0), 0)),
        ],
        [struct((rows, width), BF16)] * 2,
        cost=cost(4 * tokens * rows * width, 2 * tokens * (features // 2 + width), weight=COVER),
    )


def back_kernel(meta, ds1_ref, ds2_ref, *refs):
    out_ref, W = refs[-2:]
    chunk = ds1_ref.shape[1]

    @pl.when(pl.program_id(0) == 0)
    def _():
        gather_units(meta, M_S1, refs[:6], W, 0)
        gather_units(meta, M_S2, refs[6:12], W, chunk)

    dims = (((1,), (1,)), ((), ()))
    value = lax.dot_general(ds1_ref[...], W[:, :chunk], dims, preferred_element_type=F32)
    value += lax.dot_general(ds2_ref[...], W[:, chunk:], dims, preferred_element_type=F32)
    out_ref[...] = value.astype(BF16)


def back(meta, ds1, ds2, units, at, tb=1024):
    tokens, width = ds1.shape
    features = units[0][0].shape[0]
    block = features // 4
    dspec = pl.BlockSpec((tb, width), lambda t, m: (t, 0))
    return call(
        back_kernel,
        meta,
        [ds1, ds2] + [array for array, _, _ in units],
        (tokens // tb,),
        [dspec, dspec] + unit_specs(units, block, lambda t, m: m[at]),
        pl.BlockSpec((tb, block), lambda t, m: (t, 0)),
        struct((tokens, block), BF16),
        scratch=[pltpu.VMEM((block, 2 * width), BF16)],
        cost=cost(4 * tokens * block * width, 4 * tokens * width, weight=COVER),
    )


def unit_of(x_ref, mu_ref, inv_ref):
    repeat = x_ref.shape[1] // LANES
    mu = jnp.concatenate([mu_ref[...]] * repeat, axis=1)
    inv = jnp.concatenate([inv_ref[...]] * repeat, axis=1)
    return (x_ref[...].astype(F32) - mu) * inv, inv


def lane_sums(value):
    part = value[:, :LANES]
    for g in range(1, value.shape[1] // LANES):
        part = part + value[:, g * LANES : (g + 1) * LANES]
    return jnp.sum(part.T, axis=0, keepdims=True)


def tail_sums_kernel(meta, k_ref, rc_ref, r1_ref, r2_ref, x_ref, mu_ref, inv_ref, gain_ref, dn_ref, row_ref, col_ref):
    unit, _ = unit_of(x_ref, mu_ref, inv_ref)
    early = pl.program_id(0) < pl.num_programs(0) * FIRST // 8
    far = jnp.where(early, r1_ref[...].astype(F32), r2_ref[...].astype(F32))
    dn = k_ref[...].astype(F32) + rc_ref[...].astype(F32) + far
    dn_ref[...] = dn
    gu = dn * gain_ref[...]
    row_ref[0:1, :] = lane_sums(gu)
    row_ref[1:2, :] = lane_sums(gu * unit)
    row_ref[2:8, :] = jnp.zeros((6, row_ref.shape[1]), F32)

    @pl.when(pl.program_id(0) == 0)
    def _():
        col_ref[...] = jnp.zeros_like(col_ref)

    col_ref[0:1, :] += jnp.sum(dn * unit, axis=0, keepdims=True)
    col_ref[1:2, :] += jnp.sum(dn, axis=0, keepdims=True)


def tail_sums(meta, keep, got, far, x, mu, inv, gain, tb=256):
    tokens, channels = x.shape
    first = tokens // tb * FIRST // 8
    wide = pl.BlockSpec((tb, channels), lambda t, m: (t, 0))
    stat = pl.BlockSpec((tb, LANES), lambda t, m: (t, 0))
    return call(
        tail_sums_kernel,
        meta,
        (keep, got, *far, x, mu, inv, gain[None]),
        (tokens // tb,),
        [
            wide,
            wide,
            pl.BlockSpec((tb, channels), lambda t, m: (jnp.minimum(t, first - 1), 0)),
            pl.BlockSpec((tb, channels), lambda t, m: (jnp.maximum(t - first, 0), 0)),
            wide,
            stat,
            stat,
            pl.BlockSpec((1, channels), lambda t, m: (0, m[M_GATE])),
        ],
        [
            wide,
            pl.BlockSpec((8, tb), lambda t, m: (0, t)),
            pl.BlockSpec((8, channels), lambda t, m: (0, 0)),
        ],
        [struct((tokens, channels), F32), struct((8, tokens), F32), struct((8, channels), F32)],
        cost=cost(20 * tokens * channels, 12 * tokens * channels, weight=COVER),
    )


def tail_kernel(features, meta, dn_ref, row_ref, x_ref, mu_ref, inv_ref, gain_ref, direct_ref, out_ref, PM):
    @pl.when(pl.program_id(0) == 0)
    def _():
        PM[...] = order_matrix()

    unit, inv = unit_of(x_ref, mu_ref, inv_ref)
    repeat = x_ref.shape[1] // LANES
    tb = x_ref.shape[0]

    def mean(n):
        row = row_ref[n : n + 1, :] * (1.0 / features)
        return jnp.concatenate([jnp.broadcast_to(row, (LANES, tb)).T] * repeat, axis=1)

    gu = dn_ref[...] * gain_ref[...]
    value = (inv * (gu - mean(0) - unit * mean(1)) + direct_ref[...].astype(F32)).astype(BF16)
    for q in range(tb // TILE):
        at = slice(q * TILE, (q + 1) * TILE)
        out_ref[at, :] = to_tokens(PM[...], value[at]).astype(BF16)


def tail(meta, dn, rows, x, mu, inv, gain, direct, features, tb=512):
    tokens, channels = dn.shape
    wide = pl.BlockSpec((tb, channels), lambda t, m: (t, 0))
    stat = pl.BlockSpec((tb, LANES), lambda t, m: (t, 0))
    return call(
        functools.partial(tail_kernel, features),
        meta,
        (dn, rows, x, mu, inv, gain[None], direct),
        (tokens // tb,),
        [
            wide,
            pl.BlockSpec((rows.shape[0], tb), lambda t, m: (0, t)),
            wide,
            stat,
            stat,
            pl.BlockSpec((1, channels), lambda t, m: (0, m[M_GATE])),
            wide,
        ],
        wide,
        struct((tokens, channels), BF16),
        scratch=[pltpu.VMEM((TILE, TILE), BF16)],
        cost=cost(10 * tokens * channels, 12 * tokens * channels),
    )


def halve_kernel(meta, *refs):
    ins, (away_ref, stay_ref) = refs[:-2], refs[-2:]
    for n, out_ref in ((0, away_ref), (1, stay_ref)):
        part = ins[n * len(ins) // 2 : (n + 1) * len(ins) // 2]
        if len(part) == 4:
            for o in range(2):
                out_ref[o] = (part[o][...].astype(F32) + part[2 + o][...].astype(F32)).astype(BF16)
        else:
            out_ref[...] = (part[0][...].astype(F32) + part[1][...].astype(F32)).astype(BF16)


def halve(meta, at, kept, got, parts=2):
    if len(kept) == 2:
        rows, width = kept[0].shape
        lead = ()
    else:
        lead, rows, width = kept[0].shape
        lead = (lead,)
    half = rows // 2
    tb = half // parts
    zeros = (0,) * len(lead)
    specs, args = [], []
    for side in range(2):
        for array in (*kept, *got):
            specs.append(
                pl.BlockSpec((*lead, tb, width), lambda i, m, side=side: (*zeros, (m[at] ^ (1 - side)) * parts + i, 0))
            )
            args.append(array)
    out = pl.BlockSpec((2, tb, width), lambda i, m: (0, i, 0))
    return call(
        halve_kernel,
        meta,
        args,
        (parts,),
        specs,
        [out, out],
        [struct((2, half, width), BF16)] * 2,
        cost=cost(4 * rows * width, 12 * rows * width),
    )


def split_kernel(late, half, meta, a_ref, b_ref, near_ref, far_ref):
    core = meta[M_CORE]
    h = meta[half]
    pair_ref, single_ref = (far_ref, near_ref) if late else (near_ref, far_ref)

    def take(owner, stream, block):
        col = pl.ds(pl.multiple_of((block * 3 + stream) * LANES, LANES), LANES)
        return (a_ref[owner, :, col].astype(F32) + b_ref[owner, :, col].astype(F32)).astype(BF16)

    for store in range(2):
        k = core ^ store
        for owner in range(2):
            for block in range(2):
                at = (2 * owner + block) * LANES
                pair_ref[store, :, at : at + LANES] = take(owner, k + h, block)
            single_ref[store, :, owner * LANES : (owner + 1) * LANES] = take(owner, 2 * (1 - h), k)


def split(meta, half, late, kept, got):
    _, rows, width = kept.shape
    pair, single = 4 * LANES, 2 * LANES
    widths = (single, pair) if late else (pair, single)
    whole = pl.BlockSpec((2, rows, width), lambda i, m: (0, 0, 0))
    return call(
        functools.partial(split_kernel, late, half),
        meta,
        (kept, got),
        (1,),
        [whole] * 2,
        [pl.BlockSpec((2, rows, w), lambda i, m: (0, 0, 0)) for w in widths],
        [struct((2, rows, w), BF16) for w in widths],
        cost=cost(2 * rows * width, 12 * rows * width),
    )


def join_kernel(meta, a_ref, b_ref, *outs):
    rows = a_ref.shape[1]
    for n, out_ref in enumerate(outs):
        out_ref[:rows, :] = a_ref[n]
        out_ref[rows:, :] = b_ref[n]


def join(meta, a, b):
    _, rows, width = a.shape
    whole = pl.BlockSpec((2, rows, width), lambda i, m: (0, 0, 0))
    out = pl.BlockSpec((2 * rows, width), lambda i, m: (0, 0))
    return call(
        join_kernel,
        meta,
        (a, b),
        (1,),
        [whole] * 2,
        [out] * 2,
        [struct((2 * rows, width), BF16)] * 2,
        cost=cost(0, 16 * rows * width),
    )


def place_kernel(blocks, meta, *refs):
    out_ref = refs[-1]
    step = pl.program_id(0)
    piece = out_ref.shape[1] // 4
    unit = piece // 3
    rows = out_ref.shape[0] // blocks
    core = meta[M_CORE]
    for stream in range(2):
        for part in range(2):

            @pl.when(step == stream * 2 + part)
            def _(stream=stream, part=part):
                one = refs[stream * 2 + part]
                two = refs[4 + stream * 2 + part]
                inner = meta[M_RHO + stream] % blocks

                def put(owner, single, src, col):
                    base = meta[M_OWN + (owner ^ stream)] * piece
                    wide = unit if single else 2 * unit
                    at = base + (jnp.where(core == 0, 2 * unit, 0) if single else core * unit)
                    at = pl.ds(pl.multiple_of(at, LANES), wide)
                    for j in range(blocks):
                        to = pl.ds(pl.multiple_of((inner ^ j) * rows, rows), rows)
                        out_ref[to, at] = src[j * rows : (j + 1) * rows, col : col + wide].astype(F32)

                put(0, False, one, 0)
                put(1, False, one, 2 * unit)
                put(2, True, one, 4 * unit)
                put(3, True, one, 5 * unit)
                put(0, True, two, 0)
                put(1, True, two, unit)
                put(2, False, two, 2 * unit)
                put(3, False, two, 4 * unit)


def place(meta, parts1, parts2, n_dp, features, columns):
    blocks = n_dp // 2
    whole = pl.BlockSpec((features // 4, columns // 2), lambda i, m: (0, 0))

    def where_to(i, m):
        stream = i // 2
        return ((m[M_CORE] ^ stream) * 2 + (i % 2 ^ m[M_RHO + stream] // blocks), 0)

    return call(
        functools.partial(place_kernel, blocks),
        meta,
        (*parts1, *parts2),
        (4,),
        [whole] * 8,
        pl.BlockSpec((features // 4, columns), where_to),
        struct((features, columns), F32),
        cost=cost(features * columns, 6 * features * columns, weight=COVER),
    )


M_GATE, M_CORE, M_H1, M_H2 = 0, 1, 2, 3
M_S1, M_S2 = 4, 7
M_SEND, M_KEEP = 10, 12
M_FAR, M_HERE = 14, 16
M_OWN, M_RHO = 18, 22
M_TO2, M_TO3, M_NEAR, M_LATE2, M_LATE3 = 24, 25, 26, 27, 28
M_PAIR, M_SINGLE, M_GOT_PAIR, M_GOT_SINGLE = 29, 30, 31, 32
M_BIT = 33


def shards(
    n_dp,
    n_gate,
    inputs,
    weight,
    ln_gain,
    ln_bias,
    forget_peep,
    reset_peep,
    forget_bias,
    reset_bias,
    resets,
    padding,
    grad_out,
):
    rows, tokens, features = inputs.shape
    assert rows == 1 and n_gate == 4
    channels = forget_peep.shape[0]
    assert channels == 4 * LANES
    bits = n_dp.bit_length() - 1
    assert 1 << bits == n_dp
    gate = lax.axis_index("gate")
    dp = lax.axis_index("dp")
    hi, core = gate // 2, gate % 2
    other = 1 - core

    orders = [list(range(bits)), [1, 0, *range(2, bits)]]

    def bit(stream, step):
        return (dp >> jnp.where(stream == 0, orders[0][step], orders[1][step])) & 1

    def rho(stream):
        value = 0
        for step in range(bits):
            value = value * 2 + bit(stream, step)
        return value

    def streams(h):
        return [core + h, other + h, 2 * (1 - h)]

    h1, h2 = hi, 1 - hi
    far = (1 - hi) * 2
    single, pair = 2 * other, core
    meta = jnp.stack(
        [gate, core, h1, h2, *streams(h1), *streams(h2)]
        + [other * 2 + 1 - bit(other, 0), core * 2 + 1 - bit(core, 0)]
        + [other * 2 + bit(other, 0), core * 2 + bit(core, 0)]
        + [far + other, far + core, hi * 2 + other, hi * 2 + core]
        + [gate, hi * 2 + other, far + core, far + other]
        + [rho(core), rho(other)]
        + [(far + core) * 3 + single, (far + other) * 3 + single, (hi * 2 + other) * 3]
        + [(far + core) * 3 + pair, (far + other) * 3 + pair]
        + [gate * 3 + pair, gate * 3 + single, other, 2 * core]
        + [bit(core, step) for step in range(bits)]
    ).astype(jnp.int32)

    def over_gate(value, delta):
        return lax.ppermute(value, "gate", [(g, g ^ delta) for g in range(n_gate)])

    def over_dp(value, step):
        pairs = [
            (d * n_gate + g, (d ^ (1 << orders[g % 2][step])) * n_gate + g) for d in range(n_dp) for g in range(n_gate)
        ]
        return lax.ppermute(value, ("dp", "gate"), pairs)

    def after(value, *others):
        return lax.optimization_barrier((value, *others))[0]

    x = inputs.reshape(tokens, features)
    grad = grad_out.reshape(tokens, channels)
    params = jnp.concatenate(
        [jnp.stack([forget_peep, reset_peep, forget_bias, reset_bias]), jnp.zeros((4, channels), F32)]
    )

    to2, to3, near = cut(meta, weight, [(M_TO2, 1), (M_TO3, 1), (M_NEAR, 3)])
    sent2, sent3, near = over_gate(to2, 2), over_gate(to3, 3), over_gate(near, 1)
    normed, mu, inv, own_x, keep, live = norm(
        after(meta, to2, to3), x, ln_gain, ln_bias, resets, padding, channels
    )
    away2, away3 = cut(after(meta, normed), weight, [(M_LATE2, 2), (M_LATE3, 2)])
    late2, late3 = over_gate(away2, 2), over_gate(away3, 3)
    units1 = [(weight, M_PAIR, 0), (weight, M_PAIR, 1), (near, M_GOT_PAIR, 0), (near, M_GOT_PAIR, 1)]
    units1 += [(sent2, None, 0), (sent3, None, 0)]
    units2 = [(late2, None, 0), (late2, None, 1), (late3, None, 0), (late3, None, 1)]
    units2 += [(weight, M_SINGLE, 0), (near, M_GOT_SINGLE, 0)]
    units = units1 + units2

    def first_sends(meta, ds):
        theirs, mine = wgrad(meta, normed, ds, M_SEND)
        return mine, [over_dp(mine, 0), over_dp(over_gate(theirs, 1), 0)]

    def first_keeps(meta, ds):
        theirs, mine = wgrad(meta, normed, ds, M_KEEP)
        return [mine, over_gate(theirs, 1)]

    def gathered(meta, half, late, kept, got):
        near, far = split(meta, half, late, kept, got)
        return near, over_gate(far, 2)

    def last_steps(shard, *others):
        for step in reversed(range(2, bits)):
            shard = jnp.concatenate([after(shard, *others), over_dp(shard, step)], axis=1)
        return shard

    u1 = project(after(meta, away2, away3), M_S1, normed, units1)
    hidden, ds1, direct, vecs = scan(meta, M_H1, u1, own_x, grad, keep, live, params, None)
    mine1, got1 = first_sends(meta, ds1)
    kept1 = first_keeps(after(meta, mine1), ds1)
    u2 = project(after(meta, kept1[0]), M_S2, normed, units2)
    away1, stay1 = halve(after(meta, u2), M_BIT + 1, kept1, got1)
    step1 = over_dp(away1, 1)
    hidden, ds2, direct, vecs = scan(
        after(meta, away1), M_H2, u2, own_x, grad, keep, live, params, (hidden, direct, vecs)
    )
    for step in range(2, bits):
        away1, stay1 = halve(after(meta, ds2), M_BIT + step, [stay1], [step1])
        step1 = over_dp(away1, step)
    mine2, got2 = first_sends(after(meta, away1), ds2)
    kept2 = first_keeps(after(meta, mine2), ds2)
    far_theirs = back(after(meta, kept2[0]), ds1, ds2, units, M_FAR)
    far_got = over_gate(far_theirs, 1)
    away2, stay2 = halve(after(meta, far_theirs), M_BIT + 1, kept2, got2)
    step2 = over_dp(away2, 1)
    near1, far1 = gathered(after(meta, away2), M_H1, False, stay1, step1)
    far_mine = back(after(meta, near1), ds1, ds2, units, M_FAR + 1)
    for step in range(2, bits):
        away2, stay2 = halve(after(meta, far_mine), M_BIT + step, [stay2], [step2])
        step2 = over_dp(away2, step)
    far_mine = after(far_mine, away2)
    cut_at = tokens * FIRST // 8
    far_send = [
        (far_mine[at].astype(F32) + far_got[at].astype(F32)).astype(BF16) for at in (slice(cut_at), slice(cut_at, None))
    ]
    far_part = [over_gate(part, 2) for part in far_send]
    theirs = back(after(meta, away2, *far_send), ds1, ds2, units, M_HERE)
    got = over_gate(theirs, 1)
    shard1 = jnp.concatenate([after(near1, theirs), far1], axis=2)
    mine = back(after(meta, theirs, shard1), ds1, ds2, units, M_HERE + 1)

    def last_doubling(meta, shard):
        mine, theirs = join(meta, shard, over_dp(shard, 1))
        moved = over_dp(theirs, 0)
        return [mine, over_dp(mine, 0), over_gate(theirs, 1), over_gate(moved, 1)]

    near2, far2 = gathered(after(meta, mine, far_part[0]), M_H2, True, stay2, step2)
    shard1 = last_steps(shard1, near2)
    shard2 = last_steps(jnp.concatenate([after(near2, shard1), far2], axis=2))
    parts1 = last_doubling(after(meta, shard2), shard1)
    parts2 = last_doubling(after(meta, parts1[0]), shard2)
    dn, row_sums, col_sums = tail_sums(after(meta, parts2[0], parts1[1]), mine, got, far_part, own_x, mu, inv, ln_gain)
    for delta in (1, 2):
        row_sums = row_sums + over_gate(row_sums, delta)
    dinputs = tail(after(meta, parts2[1]), dn, row_sums, own_x, mu, inv, ln_gain, direct, features)

    totals = jnp.concatenate([col_sums[:2], vecs[:4]], axis=0)
    totals = after(totals, parts2[1])
    grad_weight = place(after(meta, dinputs), parts1, parts2, n_dp, features, weight.shape[1])
    for step in range(bits):
        last = step == bits - 1
        got = lax.ppermute(
            after(totals, dinputs) if last else totals, "dp", [(d, d ^ (1 << step)) for d in range(n_dp)]
        )
        totals = (after(totals, grad_weight) if last else totals) + got
    return (
        hidden.reshape(rows, tokens, channels),
        dinputs.reshape(rows, tokens, channels),
        grad_weight,
        totals[0],
        totals[1],
        totals[2],
        totals[3],
        totals[4],
        totals[5],
    )


def solution(mesh):
    return jax.shard_map(
        functools.partial(shards, mesh.shape["dp"], mesh.shape["gate"]),
        mesh=mesh,
        in_specs=(
            P("dp", None, None),
            P(None, "gate"),
            P(),
            P(),
            P("gate"),
            P("gate"),
            P("gate"),
            P("gate"),
            P("dp", None),
            P("dp", None),
            P("dp", None, "gate"),
        ),
        out_specs=(
            P("dp", None, "gate"),
            P("dp", None, "gate"),
            P(None, "gate"),
            P("gate"),
            P("gate"),
            P("gate"),
            P("gate"),
            P("gate"),
            P("gate"),
        ),
        check_vma=False,
    )
```
